128 devices in a mesh: row: 8 (over z, core), col: 16 (over y, x).
Axes of the slice: x: 4, y: 4, z: 4, core: 2. Of those that a mesh axis runs over, the one named last changes fastest.
Arguments:
- a_blocks: bfloat16 [1024, 16, 4, 4096], P('row', 'col'), may hold values from -0.125 to 0.125
- a_index: int32 [1024, 16, 4], P('row', 'col'), may hold values from 0 to 63, as said below
- p_blocks: bfloat16 [64, 16, 4, 4096], P('row', 'col'), may hold values from -2 to 2
- p_index: int32 [64, 16, 4], P('row', 'col'), may hold values from 0 to 127, as said below
- ap_index: int32 [1024, 8], P('row'), may hold values from 0 to 127, as said below
- coarse_index: int32 [128, 8], replicated, may hold values from 0 to 127, as said below
Outputs:
- ap_out: bfloat16 [64, 16, 8, 4096], P('row', 'col')
- coarse_out: float32 [128, 8, 4096], P(('row', 'col'))
The draws below stay inside these ranges and needn't reach their ends.
Inputs may be any that keep to these rules, and one draw needn't show every extreme that they name: `a_index`: within one (i, c) the 4 entries are distinct. `p_index`: within one row the 4 entries are distinct. `ap_index`: within one row the 8 entries are distinct. `coarse_index`: within one row the 8 entries are distinct.
All inputs are finite; a program needn't handle non-finite values.
Results may differ from the reference program's by a relative error of at most 0.0029.
Values may be sent and summed in bfloat16 or wider, within the bound.
No kernel may reach another device: no remote copies, remote signals or barrier semaphores. Data moves between devices by JAX's collectives and lax.ppermute only.
A program may use at most 320 MiB of HBM per device.

```python
import jax
import jax.numpy as jnp
from jax import lax

B = 64
KA = 4
KP = 4
KAP = 8
KC = 8
NB = 1024
NQ = 64
NCB = 128
SPAN = 18
OFFLO = 8
N_COL = 16


def hub_table(key):
    return jax.random.randint(jax.random.fold_in(key, 11), (NCB,), 0, NQ)


def aggregate_order(key):
    return jax.random.permutation(jax.random.fold_in(key, 13), NCB).astype(jnp.int32)


def distinct_pick(key, lead, width, keep):
    scores = jax.random.randint(key, lead + (width,), 0, 2 ** 20)
    scores = scores * width + jnp.arange(width, dtype=jnp.int32)
    order = jnp.argsort(scores, axis=-1, stable=True).astype(jnp.int32)
    return order[..., :keep]


def draw_a_index(key, part):
    hubs = hub_table(key)
    fine = jnp.arange(NB, dtype=jnp.int32)
    base = hubs[fine // 8]
    delta = distinct_pick(jax.random.fold_in(key, 21), (NB, N_COL), 7, KA) - 3
    return ((base[:, None, None] + delta) % NQ).astype(jnp.int32)


def draw_p_index(key, part):
    relabel = aggregate_order(key)
    fine = jnp.arange(NQ, dtype=jnp.int32)[:, None] * N_COL + jnp.arange(N_COL, dtype=jnp.int32)[None, :]
    delta = distinct_pick(jax.random.fold_in(key, 31), (NQ, N_COL), 5, KP) - 2
    geometric = ((fine[:, :, None] // 8 + delta) % NCB).astype(jnp.int32)
    return relabel[geometric].astype(jnp.int32)


def draw_ap_index(key, part):
    hubs = hub_table(key)
    relabel = aggregate_order(key)
    fine = jnp.arange(NB, dtype=jnp.int32)
    base = hubs[fine // 8] * N_COL // 8 - OFFLO
    offset = distinct_pick(jax.random.fold_in(key, 41), (NB,), SPAN, KAP)
    geometric = ((base[:, None] + offset) % NCB).astype(jnp.int32)
    return relabel[geometric].astype(jnp.int32)


def draw_coarse_index(key, part):
    hubs = hub_table(key)
    relabel = aggregate_order(key)
    base = hubs * N_COL // 8 - OFFLO
    offset = distinct_pick(jax.random.fold_in(key, 51), (NCB,), SPAN, KC)
    geometric = ((base[:, None] + offset) % NCB).astype(jnp.int32)
    values = relabel[geometric].astype(jnp.int32)
    result = jnp.zeros((NCB, KC), jnp.int32).at[relabel].set(values)
    return result.astype(jnp.int32)


def steps_of(own_key, dims, shards, smallest, largest):
    def one(position, parts):
        steps = jax.random.uniform(jax.random.fold_in(jax.random.fold_in(own_key, 6), position), (parts,), jnp.float32, smallest / len(shards), largest / len(shards))
        return jnp.repeat(jnp.exp(steps), dims[position] // parts).reshape((-1,) + (1,) * (len(dims) - position - 1))

    level = one(*shards[0])
    for cut in shards[1:]:
        level = level * one(*cut)
    return level


def normal_values(stream_key, extent, spread, most, cuts=(), kind=jnp.bfloat16):
    level = steps_of(stream_key, extent, cuts, -0.22, 0.18) if cuts else 1.0
    array = jax.random.normal(stream_key, extent, jnp.float32) * spread * level
    return jnp.minimum(jnp.maximum(array, -most), most).astype(kind)


def setup_inputs(seed: int = 0) -> dict:
    keys = jax.random.split(jax.random.key(seed), 7)
    a_blocks = normal_values(keys[0], (NB, N_COL, KA, B * B), (B * KA * N_COL // 2) ** -0.5, 0.125, ((0, 8), (1, 16)))
    a_index = draw_a_index(jax.random.fold_in(keys[6], 71), 0)
    p_blocks = normal_values(keys[2], (NQ, N_COL, KP, B * B), 0.35, 2.0, ((0, 8), (1, 16)))
    p_index = draw_p_index(jax.random.fold_in(keys[6], 71), 0)
    ap_index = draw_ap_index(jax.random.fold_in(keys[6], 71), 0)
    coarse_index = draw_coarse_index(jax.random.fold_in(keys[6], 71), 0)
    return dict(a_blocks=a_blocks, a_index=a_index, p_blocks=p_blocks, p_index=p_index, ap_index=ap_index, coarse_index=coarse_index)


def reference(a_blocks, a_index, p_blocks, p_index, ap_index, coarse_index):
    hp = lax.Precision.HIGHEST
    prolong = p_blocks.reshape(NB, KP, B, B)
    prolong_cols = p_index.reshape(NB, KP)
    group_pos = jnp.arange(N_COL, dtype=jnp.int32)[None, :, None]
    fine_cols = (a_index * N_COL + group_pos).astype(jnp.int32).reshape(NB, N_COL * KA)
    jac_rows = a_blocks.reshape(NB, N_COL * KA, B, B)

    def one_row(packed):
        blocks, fine_k, slots = packed
        picked = jnp.take(prolong, fine_k, axis=0).astype(jnp.float32)
        picked_cols = jnp.take(prolong_cols, fine_k, axis=0)
        product = jnp.einsum('nax,nmxb->nmab', blocks.astype(jnp.float32), picked, precision=hp)
        match = (picked_cols[:, :, None] == slots[None, None, :]).astype(jnp.float32)
        return jnp.einsum('nms,nmab->sab', match, product, precision=hp)

    ap_full = lax.map(one_row, (jac_rows, fine_cols, ap_index))
    ap_low = ap_full.astype(jnp.bfloat16)

    step_rows = 8
    prolong_steps = prolong.reshape(NB // step_rows, step_rows, KP, B, B)
    pcol_steps = prolong_cols.reshape(NB // step_rows, step_rows, KP)
    ap_steps = ap_low.reshape(NB // step_rows, step_rows, KAP, B, B)
    slot_steps = ap_index.reshape(NB // step_rows, step_rows, KAP)

    def add_block(total, packed):
        pro_blk, pcol_blk, ap_blk, slot_blk = packed
        terms = jnp.einsum('umxa,usxb->umsab', pro_blk.astype(jnp.float32), ap_blk.astype(jnp.float32), precision=hp)
        targets = jnp.take(coarse_index, pcol_blk, axis=0)
        equal = targets[:, :, None, :] == slot_blk[:, None, :, None]
        where_slot = jnp.sum(jnp.where(equal, lax.broadcasted_iota(jnp.int32, equal.shape, 3), 0), axis=3).astype(jnp.int32)
        found = jnp.any(equal, axis=3)
        flat = jnp.where(found, pcol_blk[:, :, None] * KC + where_slot, NCB * KC).astype(jnp.int32).reshape(-1)
        total = total.at[flat].add(terms.reshape(-1, B * B), mode="drop")
        return total, None

    start = jnp.zeros((NCB * KC, B * B), jnp.float32)
    coarse_total, unused = lax.scan(add_block, start, (prolong_steps, pcol_steps, ap_steps, slot_steps))
    return ap_low.reshape(NQ, N_COL, KAP, B * B), coarse_total.reshape(NCB, KC, B * B)
```

```python
import jax
import jax.numpy as jnp
from jax import lax
from jax.experimental import pallas as pl
from jax.experimental.pallas import tpu as pltpu
from jax.sharding import PartitionSpec as P

B = 64
KA = 4
KP = 4
KAP = 8
KC = 8
NROW = 8
NCOL = 16
NK = 64
NCB = 128
CB = 4


def nt_dot(a, b):
    return lax.dot_general(a, b, (((1,), (1,)), ((), ())), preferred_element_type=jnp.float32)


def product_kernel(idx_ref, a_ref, pt_ref, out_ref, dup_ref, w_ref):
    ih = pl.program_id(0)
    qh = pl.program_id(1)
    cblk = pl.program_id(2)
    low = lax.broadcasted_iota(jnp.int32, (B, 128), 1) < B

    @pl.when((ih == 0) & (qh == 0) & (cblk == 0))
    def _():
        def fill(k, carry):
            for mh in range(2):
                v = pt_ref[k, :, mh * 128:(mh + 1) * 128]
                turned = jnp.concatenate([v[:, B:], v[:, :B]], axis=1)
                dup_ref[k * 4 + 2 * mh] = jnp.where(low, v, turned)
                dup_ref[k * 4 + 2 * mh + 1] = jnp.where(low, turned, v)
            return carry

        lax.fori_loop(0, NK, fill, 0)
        dup_ref[NK * KP] = jnp.zeros((B, 128), jnp.bfloat16)

    def pair(cc, carry):
        for lo in range(2):
            base = (((ih * 4 + qh * 2 + lo) * NCOL) + cblk * CB + cc) * (KA * KAP)
            for ep in range(2):
                for s in range(KAP):
                    first = dup_ref[idx_ref[base + (2 * ep) * KAP + s]]
                    second = dup_ref[idx_ref[base + (2 * ep + 1) * KAP + s]]
                    column = (lo * 2 + ep) * 128
                    w_ref[s * B:(s + 1) * B, column:column + 128] = jnp.where(low, first, second)
        zero = jnp.zeros((B, KA * B), jnp.bfloat16)
        stacked = jnp.concatenate(
            [
                jnp.concatenate([a_ref[0, 0, 0, cc], zero], axis=1),
                jnp.concatenate([zero, a_ref[0, 0, 1, cc]], axis=1),
            ],
            axis=0,
        )
        res = nt_dot(w_ref[...], stacked)
        for s in range(KAP):
            out_ref[:, 0, cc, 0, s] = res[s * B:(s + 1) * B].reshape(8, 8, 128)
        return carry

    lax.fori_loop(0, CB, pair, 0)


def products(idx, a, pt):
    return pl.pallas_call(
        product_kernel,
        grid_spec=pltpu.PrefetchScalarGridSpec(
            num_scalar_prefetch=1,
            grid=(2, 2, NCOL // CB),
            in_specs=[
                pl.BlockSpec((1, 1, 2, CB, B, KA * B), lambda ih, qh, c, idx: (ih, qh, 0, c, 0, 0)),
                pl.BlockSpec((NK, B, KP * B), lambda ih, qh, c, idx: (0, 0, 0)),
            ],
            out_specs=pl.BlockSpec(
                (8, 1, CB, 1, KAP, 8, 128), lambda ih, qh, c, idx: (0, ih, c, qh, 0, 0, 0)
            ),
            scratch_shapes=[
                pltpu.VMEM((NK * KP + 1, B, 128), jnp.bfloat16),
                pltpu.VMEM((KAP * B, 2 * KA * B), jnp.bfloat16),
            ],
        ),
        out_shape=jax.ShapeDtypeStruct((8, 2, NCOL, 2, KAP, 8, 128), jnp.float32),
        name="products",
    )(idx, a, pt)


def coarse_kernel(tgt_ref, half_ref, x_ref, p_ref, out_ref, acc_ref):
    c = pl.program_id(0)
    low = lax.broadcasted_iota(jnp.int32, (8, 128), 1) < B
    low_x = lax.broadcasted_iota(jnp.int32, (B, 128), 1) < B

    @pl.when(c == 0)
    def _():
        acc_ref[...] = jnp.zeros_like(acc_ref)

    for qh in range(2):
        x = x_ref[0, qh]
        none = jnp.zeros_like(x)
        lhs = jnp.concatenate([jnp.where(low_x, x, none), jnp.where(low_x, none, x)], axis=0)
        rhs = p_ref[0, 2 * qh:2 * qh + 2].reshape(2 * B, KP * B)
        res = lax.dot_general(
            lhs, rhs, (((1,), (0,)), ((), ())), preferred_element_type=jnp.float32
        )
        for lo in range(2):
            for m in range(KP):
                for s in range(KAP):
                    at = tgt_ref[(((c * 2 + qh) * 2 + lo) * KP + m) * KAP + s]
                    rows = (lo * KAP + s) * 8
                    tile = res[rows:rows + 8, (m // 2) * 128:(m // 2) * 128 + 128]
                    keep = low if m % 2 == 0 else jnp.logical_not(low)
                    acc_ref[at] = acc_ref[at] + jnp.where(keep, tile, 0.0)

    @pl.when(c == NCOL - 1)
    def _():
        def fold(j, carry):
            for tp in range(KC // 2):
                t0 = acc_ref[j * KC + 2 * tp]
                t1 = acc_ref[j * KC + 2 * tp + 1]
                t0 = t0 + pltpu.roll(t0, B, 1)
                t1 = t1 + pltpu.roll(t1, B, 1)
                out_ref[j, tp] = jnp.where(low, t0, t1)
            return carry

        lax.fori_loop(0, NCB, fold, 0)


def coarse_terms(tgt, half, x, p):
    return pl.pallas_call(
        coarse_kernel,
        grid_spec=pltpu.PrefetchScalarGridSpec(
            num_scalar_prefetch=2,
            grid=(NCOL,),
            in_specs=[
                pl.BlockSpec((1, 2, B, 128), lambda c, tgt, half: (c, 0, 0, 0)),
                pl.BlockSpec((1, 4, B, KP * B), lambda c, tgt, half: (c, half[0], 0, 0)),
            ],
            out_specs=pl.BlockSpec((NCB, KC // 2, 8, 128), lambda c, tgt, half: (0, 0, 0, 0)),
            scratch_shapes=[pltpu.VMEM((NCB * KC + 1, 8, 128), jnp.float32)],
        ),
        out_shape=jax.ShapeDtypeStruct((NCB, KC // 2, 8, 128), jnp.float32),
        name="coarse_terms",
    )(tgt, half, x, p)


def pick_rows(table, index):
    hot = (index[..., None] == jnp.arange(table.shape[0], dtype=jnp.int32)).astype(jnp.bfloat16)
    rows = jnp.einsum(
        "...k,km->...m", hot, table.astype(jnp.bfloat16), preferred_element_type=jnp.float32
    )
    return rows.astype(jnp.int32)


def shards(a_blocks, a_index, p_blocks, p_index, ap_index, coarse_index):
    own = p_blocks[:, 0].reshape(8, KP, B, B)
    pt = own.transpose(0, 3, 1, 2).reshape(8, B, KP * B)
    pn = own.transpose(0, 2, 1, 3).reshape(8, B, KP * B)
    ptg = lax.all_gather(pt, "row", axis=0, tiled=True)
    png = lax.all_gather(pn, "col", axis=0)
    cols_k = lax.all_gather(p_index[:, 0], "row", axis=0, tiled=True)
    cols_i = lax.all_gather(p_index[:, 0], "col", axis=1).reshape(128, KP)

    a_idx = a_index[:, 0]
    picked = pick_rows(cols_k, a_idx)
    equal = picked[:, :, None, :] == ap_index[:, None, :, None]
    ids = a_idx[:, :, None, None] * KP + jnp.arange(KP, dtype=jnp.int32)
    idx = jnp.min(jnp.where(equal, ids, NK * KP), axis=3).reshape(-1)

    a = a_blocks[:, 0].reshape(128, KA, B, B).transpose(0, 2, 1, 3).reshape(2, 2, 2, NCOL, B, KA * B)
    partial = products(idx, a, ptg)
    summed = lax.psum_scatter(
        partial.reshape(NCOL, NCOL, 2, KAP, 8, 128), "col", scatter_dimension=0, tiled=True
    )[0]
    apt = summed.astype(jnp.bfloat16)

    back = lax.all_to_all(apt, "col", 0, 0, tiled=True)
    ap_out = (
        back.reshape(8, 2, 2, KAP, 8, 2, B)
        .transpose(1, 2, 5, 3, 6, 0, 4)
        .reshape(8, 1, KAP, B * B)
    )

    half = lax.axis_index("col") % 2
    targets = pick_rows(coarse_index, cols_i)
    hit = targets[:, :, None, :] == ap_index[:, None, :, None]
    slot = cols_i[:, :, None, None] * KC + jnp.arange(KC, dtype=jnp.int32)
    tgt = jnp.min(jnp.where(hit, slot, NCB * KC), axis=3)
    tgt = tgt.reshape(2, 2, 2, NCOL, KP, KAP)
    tgt = lax.dynamic_index_in_dim(tgt, half, 0, keepdims=False)
    tgt = tgt.transpose(2, 0, 1, 3, 4).reshape(-1)
    coarse = coarse_terms(
        tgt, half.reshape(1).astype(jnp.int32), apt.reshape(NCOL, 2, KAP * 8, 128), png
    )
    coarse = lax.psum_scatter(
        coarse.reshape(NROW, NCOL, KC // 2, 8, 128), "row", scatter_dimension=0, tiled=True
    )[0]
    coarse = lax.all_to_all(coarse, "col", 0, 0, tiled=True)
    coarse = coarse.reshape(8, 2, KC // 2, 8, 2, B).sum(axis=1)
    coarse_out = coarse.transpose(1, 3, 4, 0, 2).reshape(1, KC, B * B)
    return ap_out, coarse_out


def solution(mesh):
    placed = (
        P("row", "col", None, None),
        P("row", "col", None),
        P("row", "col", None, None),
        P("row", "col", None),
        P("row", None),
        P(),
    )
    return jax.shard_map(
        shards,
        mesh=mesh,
        in_specs=placed,
        out_specs=(P("row", "col", None, None), P(("row", "col"), None, None)),
        check_vma=False,
    )
```

```python
import jax
import jax.numpy as jnp
from jax import lax
from jax.experimental import pallas as pl
from jax.experimental.pallas import tpu as pltpu
from jax.sharding import PartitionSpec as P

B = 64
KA = 4
KP = 4
KAP = 8
KC = 8
NCOL = 16
NK = 64
NCB = 128
FULL = 14.0
TINY = 1e-30


def along_row(v, dz, flip):
    pairs = [(r, ((r // 2 + dz) % 4) * 2 + (r % 2 + flip) % 2) for r in range(8)]
    return lax.ppermute(v, "row", pairs)


def along_col(v, dx, dy):
    pairs = [(c, ((c // 4 + dy) % 4) * 4 + (c % 4 + dx) % 4) for c in range(16)]
    return lax.ppermute(v, "col", pairs)


def low_lanes(rows):
    return lax.broadcasted_iota(jnp.int32, (rows, 128), 1) < B


def spread_kernel(a_ref, out_ref, buf_ref):
    low = low_lanes(32)

    def some(g, carry):
        for u in range(4):
            i = g * 4 + u
            v = a_ref[i].astype(jnp.float32)
            for h in range(32):
                buf_ref[u, h * 4:(h + 1) * 4, :] = v[:, h * 128:(h + 1) * 128]
        for u in range(4):
            i = g * 4 + u
            for ep in range(2):
                v0 = buf_ref[u, pl.ds(2 * ep, 32, stride=4), :]
                v1 = buf_ref[u, pl.ds(2 * ep + 1, 32, stride=4), :]
                top = jnp.where(low, v0, pltpu.roll(v1, B, 1))
                bottom = jnp.where(low, pltpu.roll(v0, B, 1), v1)
                out_ref[i, 0:32, ep * 128:(ep + 1) * 128] = top.astype(jnp.bfloat16)
                out_ref[i, 32:64, ep * 128:(ep + 1) * 128] = bottom.astype(jnp.bfloat16)
        return carry

    lax.fori_loop(0, 4, some, 0)


def spread(a):
    return pl.pallas_call(
        spread_kernel,
        grid=(8,),
        in_specs=[pl.BlockSpec((16, KA, B * B), lambda g: (g, 0, 0))],
        out_specs=pl.BlockSpec((16, B, KA * B), lambda g: (g, 0, 0)),
        scratch_shapes=[pltpu.VMEM((4, 128, 128), jnp.float32)],
        out_shape=jax.ShapeDtypeStruct((128, B, KA * B), jnp.bfloat16),
        name="spread",
    )(a)


def table_kernel(*refs):
    parts, out_ref = refs[:8], refs[8]
    low = low_lanes(B)
    for n, part in enumerate(parts):
        def fill(q, carry):
            for mh in range(2):
                v = part[q, :, mh * 128:(mh + 1) * 128]
                turned = jnp.concatenate([v[:, B:], v[:, :B]], axis=1)
                at = (n * 8 + q) * 4 + 2 * mh
                out_ref[at] = jnp.where(low, v, turned)
                out_ref[at + 1] = jnp.where(low, turned, v)
            return carry

        lax.fori_loop(0, 8, fill, 0)
    out_ref[NK * KP] = jnp.zeros((B, 128), jnp.bfloat16)


def table(parts):
    whole = pl.BlockSpec(memory_space=pltpu.VMEM)
    return pl.pallas_call(
        table_kernel,
        in_specs=[whole] * 8,
        out_specs=whole,
        out_shape=jax.ShapeDtypeStruct((NK * KP + 1, B, 128), jnp.bfloat16),
        name="table",
    )(*parts)


def nt_dot(a, b):
    return lax.dot_general(a, b, (((1,), (1,)), ((), ())), preferred_element_type=jnp.float32)


def exponent(most):
    return jnp.ceil(jnp.log2(jnp.maximum(most, TINY)))


def coded(v, mul):
    return jnp.round(v * mul).astype(jnp.int32).astype(jnp.int16)


def product_kernel(color, idx_ref, at_ref, a_ref, dup_ref, out_ref, w0_ref, w1_ref, exp_ref):
    ih = pl.program_id(0)
    cblk = pl.program_id(1)
    low = low_lanes(B)
    mine = at_ref[color]
    count = a_ref.shape[2]
    zero = jnp.zeros((B, KA * B), jnp.bfloat16)

    def build(cc, w_ref):
        for lo in range(2):
            base = (((ih * 4 + color * 2 + lo) * NCOL) + cblk * count + cc) * (KA * KAP)
            for ep in range(2):
                for s in range(KAP):
                    first = dup_ref[idx_ref[base + (2 * ep) * KAP + s]]
                    second = dup_ref[idx_ref[base + (2 * ep + 1) * KAP + s]]
                    column = (lo * 2 + ep) * 128
                    w_ref[s * B:(s + 1) * B, column:column + 128] = jnp.where(low, first, second)

    def multiply(cc, w_ref):
        stacked = jnp.concatenate(
            [
                jnp.concatenate([a_ref[0, 0, cc], zero], axis=1),
                jnp.concatenate([zero, a_ref[0, 1, cc]], axis=1),
            ],
            axis=0,
        )
        res = nt_dot(w_ref[...], stacked)
        most = jnp.max(jnp.abs(res), axis=0, keepdims=True)
        e = exponent(most)
        q = jnp.round(res * jnp.exp2(FULL - e)).astype(jnp.int32)
        c = cblk * count + cc
        exp_ref[ih, pl.ds(c, 1), :] = e
        for bg in range(8):
            g = bg % 2
            if color == 0:
                d = lax.rem(2 * g + ih - mine + 4, 4)
                u = bg // 2
            else:
                d = lax.rem(bg // 2 - mine + 4, 4)
                u = 2 * g + ih
            for sp in range(4):
                r0 = 2 * sp * B + bg * 8
                pair = jnp.concatenate([q[r0:r0 + 8], q[r0 + B:r0 + B + 8]], axis=0)
                out_ref[d, (u * NCOL + c) * 4 + sp] = pair.astype(jnp.int16)

    def pairs(k, carry):
        build(2 * k + 1, w1_ref)
        multiply(2 * k, w0_ref)

        @pl.when(k + 1 < count // 2)
        def _():
            build(2 * k + 2, w0_ref)

        multiply(2 * k + 1, w1_ref)
        return carry

    build(0, w0_ref)
    lax.fori_loop(0, count // 2, pairs, 0)

    @pl.when((ih == 1) & (cblk == pl.num_programs(1) - 1))
    def _():
        for d in range(4):
            for t in range(2):
                source = lax.rem(mine + d, 2) if color == 0 else t
                out_ref[d, 256 + t] = exp_ref[source].astype(jnp.int32).astype(jnp.int16)


def products(color, idx, at, a, dup):
    block = 8
    return pl.pallas_call(
        lambda *refs: product_kernel(color, *refs),
        grid_spec=pltpu.PrefetchScalarGridSpec(
            num_scalar_prefetch=2,
            grid=(2, NCOL // block),
            in_specs=[
                pl.BlockSpec(
                    (1, 2, block, B, KA * B), lambda ih, c, idx, at: (ih * 2 + color, 0, c, 0, 0)
                ),
                pl.BlockSpec((NK * KP + 1, B, 128), lambda ih, c, idx, at: (0, 0, 0)),
            ],
            out_specs=pl.BlockSpec((4, 258, 16, 128), lambda ih, c, idx, at: (0, 0, 0, 0)),
            scratch_shapes=[
                pltpu.VMEM((KAP * B, 2 * KA * B), jnp.bfloat16),
                pltpu.VMEM((KAP * B, 2 * KA * B), jnp.bfloat16),
                pltpu.VMEM((2, NCOL, 128), jnp.float32),
            ],
        ),
        out_shape=jax.ShapeDtypeStruct((4, 258, 16, 128), jnp.int16),
        name=f"products_{color}",
    )(idx, at, a, dup)


def middle_kernel(color, at_ref, own_ref, m1_ref, m2_ref, m3_ref, out_ref, scale_ref, exp_ref):
    other = at_ref[1 - color]
    for d, m in enumerate((own_ref, m1_ref, m2_ref, m3_ref)):
        for t in range(2):
            scale_ref[d, t] = jnp.exp2(m[256 + t].astype(jnp.float32) - FULL)

    for u in range(4):
        d2 = lax.rem(u - other + 4, 4)

        def one(c, carry):
            t = 0 if color == 0 else u % 2
            scales = [scale_ref[d, t, pl.ds(c, 1), :] for d in range(4)]
            sums = []
            for sp in range(4):
                total = None
                for d, m in enumerate((own_ref, m1_ref, m2_ref, m3_ref)):
                    term = m[(u * NCOL + c) * 4 + sp].astype(jnp.float32) * scales[d]
                    total = term if total is None else total + term
                sums.append(total)
            most = sums[0]
            most = jnp.maximum(
                jnp.maximum(jnp.abs(sums[0]), jnp.abs(sums[1])),
                jnp.maximum(jnp.abs(sums[2]), jnp.abs(sums[3])),
            )
            e = exponent(jnp.max(most, axis=0, keepdims=True))
            mul = jnp.exp2(FULL - e)
            exp_ref[u, pl.ds(c, 1), :] = e
            for sp in range(4):
                out_ref[d2, c * 4 + sp] = coded(sums[sp], mul)
            return carry

        lax.fori_loop(0, NCOL, one, 0)
        out_ref[d2, 64] = exp_ref[u].astype(jnp.int32).astype(jnp.int16)


def middle(color, at, own, m1, m2, m3):
    vmem = pl.BlockSpec(memory_space=pltpu.VMEM)
    return pl.pallas_call(
        lambda *refs: middle_kernel(color, *refs),
        in_specs=[
            pl.BlockSpec(memory_space=pltpu.SMEM),
            vmem, vmem, vmem, vmem,
        ],
        out_specs=vmem,
        scratch_shapes=[
            pltpu.VMEM((4, 2, NCOL, 128), jnp.float32),
            pltpu.VMEM((4, NCOL, 128), jnp.float32),
        ],
        out_shape=jax.ShapeDtypeStruct((4, 65, 16, 128), jnp.int16),
        name=f"middle_{color}",
    )(at, own, m1, m2, m3)


def final_kernel(*refs):
    parts, out_ref, scale_ref = refs[:8], refs[8], refs[9]
    for n, m in enumerate(parts):
        scale_ref[n] = jnp.exp2(m[64].astype(jnp.float32) - FULL)

    def one(c, carry):
        for qh in range(2):
            scales = [scale_ref[qh * 4 + d, pl.ds(c, 1), :] for d in range(4)]
            for sp in range(4):
                total = None
                for d in range(4):
                    m = parts[qh * 4 + d]
                    term = m[c * 4 + sp].astype(jnp.float32) * scales[d]
                    total = term if total is None else total + term
                out_ref[c, qh, sp * 16:(sp + 1) * 16, :] = total.astype(jnp.bfloat16)
        return carry

    lax.fori_loop(0, NCOL, one, 0)


def final(parts):
    vmem = pl.BlockSpec(memory_space=pltpu.VMEM)
    return pl.pallas_call(
        final_kernel,
        in_specs=[vmem] * 8,
        out_specs=vmem,
        scratch_shapes=[pltpu.VMEM((8, NCOL, 128), jnp.float32)],
        out_shape=jax.ShapeDtypeStruct((NCOL, 2, B, 128), jnp.bfloat16),
        name="final",
    )(*parts)


def coarse_kernel(tgt_ref, at_ref, x_ref, p0_ref, p1_ref, p2_ref, p3_ref, keep_ref, send_ref, acc_ref):
    dx = pl.program_id(0)
    low = low_lanes(8)
    low_x = low_lanes(B)
    my_x, my_y, my_z, my_core = at_ref[0], at_ref[1], at_ref[2], at_ref[3]

    @pl.when(dx == 0)
    def _():
        acc_ref[...] = jnp.zeros_like(acc_ref)

    for dy, p_ref in enumerate((p0_ref, p1_ref, p2_ref, p3_ref)):
        c = lax.rem(my_y - dy + 4, 4) * 4 + lax.rem(my_x - dx + 4, 4)
        for qh in range(2):
            x = x_ref[c, qh]
            none = jnp.zeros_like(x)
            lhs = jnp.concatenate([jnp.where(low_x, x, none), jnp.where(low_x, none, x)], axis=0)
            rhs = p_ref[0, 2 * qh:2 * qh + 2].reshape(2 * B, KP * B)
            res = lax.dot_general(
                lhs, rhs, (((1,), (0,)), ((), ())), preferred_element_type=jnp.float32
            )
            for lo in range(2):
                ats, sums = [], []
                for m in range(KP):
                    for s in range(KAP):
                        at = tgt_ref[(((c * 2 + qh) * 2 + lo) * KP + m) * KAP + s]
                        rows = (lo * KAP + s) * 8
                        tile = res[rows:rows + 8, (m // 2) * 128:(m // 2) * 128 + 128]
                        keep = low if m % 2 == 0 else jnp.logical_not(low)
                        ats.append(at)
                        sums.append(acc_ref[at] + jnp.where(keep, tile, 0.0))
                for at, total in zip(ats, sums):
                    acc_ref[at] = total

    @pl.when(dx == 3)
    def _():
        for flip, out_ref in ((1, send_ref), (0, keep_ref)):
            core = lax.rem(my_core + flip, 2)
            for d in range(4):
                first = (lax.rem(my_z + d, 4) * 2 + core) * NCOL

                def fold(col, carry):
                    for tp in range(KC // 2):
                        t0 = acc_ref[(first + col) * KC + 2 * tp]
                        t1 = acc_ref[(first + col) * KC + 2 * tp + 1]
                        t0 = t0 + pltpu.roll(t0, B, 1)
                        t1 = t1 + pltpu.roll(t1, B, 1)
                        out_ref[d, col, tp] = jnp.where(low, t0, t1)
                    return carry

                lax.fori_loop(0, NCOL, fold, 0)


def coarse_terms(tgt, at, x, ps):
    shape = (4, NCOL, KC // 2, 8, 128)
    out = pl.BlockSpec(shape, lambda dx, tgt, at: (0, 0, 0, 0, 0))
    return pl.pallas_call(
        coarse_kernel,
        grid_spec=pltpu.PrefetchScalarGridSpec(
            num_scalar_prefetch=2,
            grid=(4,),
            in_specs=[pl.BlockSpec((NCOL, 2, B, 128), lambda dx, tgt, at: (0, 0, 0, 0))]
            + [pl.BlockSpec((1, 5, B, KP * B), lambda dx, tgt, at: (dx, 0, 0, 0))] * 4,
            out_specs=[out, out],
            scratch_shapes=[pltpu.VMEM((NCB * KC + 1, 8, 128), jnp.float32)],
        ),
        out_shape=[jax.ShapeDtypeStruct(shape, jnp.float32)] * 2,
        name="coarse_terms",
    )(tgt, at, x, *ps)


def pick_rows(table, index):
    hot = (index[..., None] == jnp.arange(table.shape[0], dtype=jnp.int32)).astype(jnp.bfloat16)
    rows = jnp.einsum(
        "...k,km->...m", hot, table.astype(jnp.bfloat16), preferred_element_type=jnp.float32
    )
    return rows.astype(jnp.int32)


def index_slab(index):
    wide = jnp.pad(index.astype(jnp.bfloat16), ((0, B - index.shape[0]), (0, KP * B - KP)))
    return wide[None]


def shards(a_blocks, a_index, p_blocks, p_index, ap_index, coarse_index):
    row = lax.axis_index("row")
    col = lax.axis_index("col")
    z, core = row // 2, row % 2
    y, x = col // 4, col % 4
    at = jnp.stack([x, y, z, core]).astype(jnp.int32)
    half = x % 2

    own = p_blocks[:, 0].reshape(8, KP, B, B)
    pt = own.transpose(0, 3, 1, 2).reshape(8, B, KP * B)
    pt = jnp.concatenate([pt, index_slab(p_index[:, 0])], axis=0)
    by_z = [pt] + [along_row(pt, d, 0) for d in (1, 2, 3)]
    parts = []
    for part in by_z:
        parts += [part, along_row(part, 0, 1)]

    pn = own.reshape(8, KP, 32, 2, B).transpose(0, 3, 2, 1, 4).reshape(2, 4, B, KP * B)
    halves = jnp.stack(
        [
            jnp.concatenate([pn[h], index_slab(p_index[4 * h:4 * h + 4, 0])], axis=0)
            for h in range(2)
        ]
    )
    same = lax.dynamic_index_in_dim(halves, half, 0, keepdims=False)
    diff = lax.dynamic_index_in_dim(halves, 1 - half, 0, keepdims=False)
    by_x = jnp.stack(
        [same, along_col(diff, 1, 0), along_col(same, 2, 0), along_col(diff, 3, 0)]
    )
    ps = [by_x] + [along_col(by_x, 0, d) for d in (1, 2, 3)]

    a = spread(a_blocks[:, 0]).reshape(4, 2, NCOL, B, KA * B)

    a_idx = a_index[:, 0]
    from_row = a_idx // 8
    place = ((z - from_row // 2) % 4) * 2 + (core + from_row) % 2
    place = place * 8 + a_idx % 8
    cols_k = jnp.concatenate([part[8, :8, :KP] for part in parts], axis=0)
    picked = pick_rows(cols_k, place)
    equal = picked[:, :, None, :] == ap_index[:, None, :, None]
    ids = place[:, :, None, None] * KP + jnp.arange(KP, dtype=jnp.int32)
    idx = jnp.min(jnp.where(equal, ids, NK * KP), axis=3).reshape(-1)

    dup = table(parts)
    q0 = products(0, idx, at, a, dup)
    x_sent = [along_col(q0[d], d, 0) for d in (1, 2, 3)]
    q1 = products(1, idx, at, a, dup)
    y_sent = [along_col(q1[d], 0, d) for d in (1, 2, 3)]
    s0 = middle(0, at, q0[0], *x_sent)
    y_last = [along_col(s0[d], 0, d) for d in (1, 2, 3)]
    s1 = middle(1, at, q1[0], *y_sent)
    x_last = [along_col(s1[d], d, 0) for d in (1, 2, 3)]
    apt = final([s0[0], *y_last, s1[0], *x_last])

    back = lax.all_to_all(apt, "col", 0, 0, tiled=True)
    ap_out = (
        back.reshape(8, 2, 2, KAP, 8, 2, 2, 32)
        .transpose(1, 2, 5, 3, 7, 6, 0, 4)
        .reshape(8, 1, KAP, B * B)
    )

    cols_p = jnp.stack([p[:, 4, :4, :KP] for p in ps]).reshape(NCOL, 16)
    cc = jnp.arange(NCOL, dtype=jnp.int32)
    where = ((y - cc // 4) % 4) * 4 + (x - cc % 4) % 4
    cols_i = pick_rows(cols_p, where).reshape(NCOL, 4, KP)
    slots = lax.dynamic_index_in_dim(
        ap_index.reshape(2, 4, NCOL, KAP), half, 0, keepdims=False
    ).transpose(1, 0, 2)
    targets = pick_rows(coarse_index, cols_i)
    hit = targets[:, :, :, None, :] == slots[:, :, None, :, None]
    slot = cols_i[:, :, :, None, None] * KC + jnp.arange(KC, dtype=jnp.int32)
    tgt = jnp.min(jnp.where(hit, slot, NCB * KC), axis=4).reshape(-1)

    keep, send = coarse_terms(tgt, at, apt, ps)
    got = along_row(send, 0, 1)
    sums = [keep[d] + got[d] for d in range(4)]
    coarse = sums[0]
    for d in (1, 2, 3):
        coarse = coarse + along_row(sums[d], d, 0)
    coarse = lax.all_to_all(coarse, "col", 0, 0, tiled=True)
    coarse = coarse.reshape(8, 2, KC // 2, 8, 2, B).sum(axis=1)
    coarse_out = coarse.transpose(1, 3, 4, 0, 2).reshape(1, KC, B * B)
    return ap_out, coarse_out


def solution(mesh):
    placed = (
        P("row", "col", None, None),
        P("row", "col", None),
        P("row", "col", None, None),
        P("row", "col", None),
        P("row", None),
        P(),
    )
    return jax.shard_map(
        shards,
        mesh=mesh,
        in_specs=placed,
        out_specs=(P("row", "col", None, None), P(("row", "col"), None, None)),
        check_vma=False,
    )
```

```python
import jax
import jax.numpy as jnp
from jax import lax
from jax.experimental import pallas as pl
from jax.experimental.pallas import tpu as pltpu
from jax.sharding import PartitionSpec as P


B = 64
KA = 4
KP = 4
KAP = 8
KC = 8
NCOL = 16
NK = 64
NCB = 128
FULL = 14.0
TINY = 1e-30


def along_row(v, dz, flip):
    pairs = [(r, ((r // 2 + dz) % 4) * 2 + (r % 2 + flip) % 2) for r in range(8)]
    return lax.ppermute(v, "row", pairs)


def along_col(v, dx, dy):
    pairs = [(c, ((c // 4 + dy) % 4) * 4 + (c % 4 + dx) % 4) for c in range(16)]
    return lax.ppermute(v, "col", pairs)


def low_lanes(rows):
    return lax.broadcasted_iota(jnp.int32, (rows, 128), 1) < B


def spread_kernel(a_ref, out_ref, buf_ref):
    low = low_lanes(32)

    def some(g, carry):
        for u in range(4):
            i = g * 4 + u
            v = a_ref[i].astype(jnp.float32)
            for h in range(32):
                buf_ref[u, h * 4:(h + 1) * 4, :] = v[:, h * 128:(h + 1) * 128]
        for u in range(4):
            i = g * 4 + u
            for ep in range(2):
                v0 = buf_ref[u, pl.ds(2 * ep, 32, stride=4), :]
                v1 = buf_ref[u, pl.ds(2 * ep + 1, 32, stride=4), :]
                top = jnp.where(low, v0, pltpu.roll(v1, B, 1))
                bottom = jnp.where(low, pltpu.roll(v0, B, 1), v1)
                out_ref[i, 0:32, ep * 128:(ep + 1) * 128] = top.astype(jnp.bfloat16)
                out_ref[i, 32:64, ep * 128:(ep + 1) * 128] = bottom.astype(jnp.bfloat16)
        return carry

    lax.fori_loop(0, 4, some, 0)


def spread(a):
    return pl.pallas_call(
        spread_kernel,
        grid=(8,),
        in_specs=[pl.BlockSpec((16, KA, B * B), lambda g: (g, 0, 0))],
        out_specs=pl.BlockSpec((16, B, KA * B), lambda g: (g, 0, 0)),
        scratch_shapes=[pltpu.VMEM((4, 128, 128), jnp.float32)],
        out_shape=jax.ShapeDtypeStruct((128, B, KA * B), jnp.bfloat16),
        name="spread",
    )(a)


def table_kernel(*refs):
    parts, out_ref = refs[:8], refs[8]
    low = low_lanes(B)
    for n, part in enumerate(parts):
        def fill(q, carry):
            for mh in range(2):
                v = part[q, :, mh * 128:(mh + 1) * 128]
                turned = jnp.concatenate([v[:, B:], v[:, :B]], axis=1)
                at = (n * 8 + q) * 4 + 2 * mh
                out_ref[at] = jnp.where(low, v, turned)
                out_ref[at + 1] = jnp.where(low, turned, v)
            return carry

        lax.fori_loop(0, 8, fill, 0)
    out_ref[NK * KP] = jnp.zeros((B, 128), jnp.bfloat16)


def table(parts):
    whole = pl.BlockSpec(memory_space=pltpu.VMEM)
    return pl.pallas_call(
        table_kernel,
        in_specs=[whole] * 8,
        out_specs=whole,
        out_shape=jax.ShapeDtypeStruct((NK * KP + 1, B, 128), jnp.bfloat16),
        name="table",
    )(*parts)


def nt_dot(a, b):
    return lax.dot_general(a, b, (((1,), (1,)), ((), ())), preferred_element_type=jnp.float32)


def exponent(most):
    return jnp.ceil(jnp.log2(jnp.maximum(most, TINY)))


def coded(v, mul):
    return jnp.round(v * mul).astype(jnp.int32).astype(jnp.int16)


def product_kernel(color, idx_ref, at_ref, a_ref, dup_ref, out_ref, exp_ref):
    ih = pl.program_id(0)
    cblk = pl.program_id(1)
    low = low_lanes(B)
    mine = at_ref[color]
    count = a_ref.shape[2]
    zero = jnp.zeros((B, KA * B), jnp.bfloat16)

    def one(cc, carry):
        rows = []
        for s in range(KAP):
            pieces = []
            for lo in range(2):
                base = (((ih * 4 + color * 2 + lo) * NCOL) + cblk * count + cc) * (KA * KAP)
                for ep in range(2):
                    first = dup_ref[idx_ref[base + (2 * ep) * KAP + s]]
                    second = dup_ref[idx_ref[base + (2 * ep + 1) * KAP + s]]
                    pieces.append(jnp.where(low, first, second))
            rows.append(jnp.concatenate(pieces, axis=1))
        stacked = jnp.concatenate(
            [
                jnp.concatenate([a_ref[0, 0, cc], zero], axis=1),
                jnp.concatenate([zero, a_ref[0, 1, cc]], axis=1),
            ],
            axis=0,
        )
        res = nt_dot(jnp.concatenate(rows, axis=0), stacked)
        most = jnp.max(jnp.abs(res), axis=0, keepdims=True)
        e = exponent(most)
        q = jnp.round(res * jnp.exp2(FULL - e)).astype(jnp.int32)
        c = cblk * count + cc
        exp_ref[ih, pl.ds(c, 1), :] = e
        for bg in range(8):
            g = bg % 2
            if color == 0:
                d = lax.rem(2 * g + ih - mine + 4, 4)
                u = bg // 2
            else:
                d = lax.rem(bg // 2 - mine + 4, 4)
                u = 2 * g + ih
            for sp in range(4):
                r0 = 2 * sp * B + bg * 8
                pair = jnp.concatenate([q[r0:r0 + 8], q[r0 + B:r0 + B + 8]], axis=0)
                out_ref[d, (u * NCOL + c) * 4 + sp] = pair.astype(jnp.int16)

        return carry

    lax.fori_loop(0, count, one, 0)

    @pl.when((ih == 1) & (cblk == pl.num_programs(1) - 1))
    def _():
        for d in range(4):
            for t in range(2):
                source = lax.rem(mine + d, 2) if color == 0 else t
                out_ref[d, 256 + t] = exp_ref[source].astype(jnp.int32).astype(jnp.int16)


def products(color, idx, at, a, dup):
    block = 8
    return pl.pallas_call(
        lambda *refs: product_kernel(color, *refs),
        grid_spec=pltpu.PrefetchScalarGridSpec(
            num_scalar_prefetch=2,
            grid=(2, NCOL // block),
            in_specs=[
                pl.BlockSpec(
                    (1, 2, block, B, KA * B), lambda ih, c, idx, at: (ih * 2 + color, 0, c, 0, 0)
                ),
                pl.BlockSpec((NK * KP + 1, B, 128), lambda ih, c, idx, at: (0, 0, 0)),
            ],
            out_specs=pl.BlockSpec((4, 258, 16, 128), lambda ih, c, idx, at: (0, 0, 0, 0)),
            scratch_shapes=[
                pltpu.VMEM((2, NCOL, 128), jnp.float32),
            ],
        ),
        out_shape=jax.ShapeDtypeStruct((4, 258, 16, 128), jnp.int16),
    )(idx, at, a, dup)


def middle_kernel(color, at_ref, own_ref, m1_ref, m2_ref, m3_ref, out_ref, scale_ref, exp_ref):
    other = at_ref[1 - color]
    for d, m in enumerate((own_ref, m1_ref, m2_ref, m3_ref)):
        for t in range(2):
            scale_ref[d, t] = jnp.exp2(m[256 + t].astype(jnp.float32) - FULL)

    for u in range(4):
        d2 = lax.rem(u - other + 4, 4)

        def one(c, carry):
            t = 0 if color == 0 else u % 2
            scales = [scale_ref[d, t, pl.ds(c, 1), :] for d in range(4)]
            sums = []
            for sp in range(4):
                total = None
                for d, m in enumerate((own_ref, m1_ref, m2_ref, m3_ref)):
                    term = m[(u * NCOL + c) * 4 + sp].astype(jnp.float32) * scales[d]
                    total = term if total is None else total + term
                sums.append(total)
            most = sums[0]
            most = jnp.maximum(
                jnp.maximum(jnp.abs(sums[0]), jnp.abs(sums[1])),
                jnp.maximum(jnp.abs(sums[2]), jnp.abs(sums[3])),
            )
            e = exponent(jnp.max(most, axis=0, keepdims=True))
            mul = jnp.exp2(FULL - e)
            exp_ref[u, pl.ds(c, 1), :] = e
            for sp in range(4):
                out_ref[d2, c * 4 + sp] = coded(sums[sp], mul)
            return carry

        lax.fori_loop(0, NCOL, one, 0)
        out_ref[d2, 64] = exp_ref[u].astype(jnp.int32).astype(jnp.int16)


def middle(color, at, own, m1, m2, m3):
    vmem = pl.BlockSpec(memory_space=pltpu.VMEM)
    return pl.pallas_call(
        lambda *refs: middle_kernel(color, *refs),
        in_specs=[
            pl.BlockSpec(memory_space=pltpu.SMEM),
            vmem, vmem, vmem, vmem,
        ],
        out_specs=vmem,
        scratch_shapes=[
            pltpu.VMEM((4, 2, NCOL, 128), jnp.float32),
            pltpu.VMEM((4, NCOL, 128), jnp.float32),
        ],
        out_shape=jax.ShapeDtypeStruct((4, 65, 16, 128), jnp.int16),
    )(at, own, m1, m2, m3)


def final_kernel(*refs):
    parts, out_ref, scale_ref = refs[:8], refs[8], refs[9]
    for n, m in enumerate(parts):
        scale_ref[n] = jnp.exp2(m[64].astype(jnp.float32) - FULL)

    def one(c, carry):
        for qh in range(2):
            scales = [scale_ref[qh * 4 + d, pl.ds(c, 1), :] for d in range(4)]
            for sp in range(4):
                total = None
                for d in range(4):
                    m = parts[qh * 4 + d]
                    term = m[c * 4 + sp].astype(jnp.float32) * scales[d]
                    total = term if total is None else total + term
                out_ref[c, qh, sp * 16:(sp + 1) * 16, :] = total.astype(jnp.bfloat16)
        return carry

    lax.fori_loop(0, NCOL, one, 0)


def final(parts):
    vmem = pl.BlockSpec(memory_space=pltpu.VMEM)
    return pl.pallas_call(
        final_kernel,
        in_specs=[vmem] * 8,
        out_specs=vmem,
        scratch_shapes=[pltpu.VMEM((8, NCOL, 128), jnp.float32)],
        out_shape=jax.ShapeDtypeStruct((NCOL, 2, B, 128), jnp.bfloat16),
        name="final",
    )(*parts)


def coarse_kernel(tgt_ref, at_ref, x_ref, p0_ref, p1_ref, p2_ref, p3_ref, keep_ref, send_ref, acc_ref):
    dx = pl.program_id(0)
    low = low_lanes(8)
    low_x = low_lanes(B)
    my_x, my_y, my_z, my_core = at_ref[0], at_ref[1], at_ref[2], at_ref[3]

    @pl.when(dx == 0)
    def _():
        acc_ref[...] = jnp.zeros_like(acc_ref)

    for dy, p_ref in enumerate((p0_ref, p1_ref, p2_ref, p3_ref)):
        c = lax.rem(my_y - dy + 4, 4) * 4 + lax.rem(my_x - dx + 4, 4)
        for qh in range(2):
            x = x_ref[c, qh]
            none = jnp.zeros_like(x)
            lhs = jnp.concatenate([jnp.where(low_x, x, none), jnp.where(low_x, none, x)], axis=0)
            rhs = p_ref[0, 2 * qh:2 * qh + 2].reshape(2 * B, KP * B)
            res = lax.dot_general(
                lhs, rhs, (((1,), (0,)), ((), ())), preferred_element_type=jnp.float32
            )
            for lo in range(2):
                ats, sums = [], []
                for m in range(KP):
                    for s in range(KAP):
                        at = tgt_ref[(((c * 2 + qh) * 2 + lo) * KP + m) * KAP + s]
                        rows = (lo * KAP + s) * 8
                        tile = res[rows:rows + 8, (m // 2) * 128:(m // 2) * 128 + 128]
                        keep = low if m % 2 == 0 else jnp.logical_not(low)
                        ats.append(at)
                        sums.append(acc_ref[at] + jnp.where(keep, tile, 0.0))
                for at, total in zip(ats, sums):
                    acc_ref[at] = total

    @pl.when(dx == 3)
    def _():
        for flip, out_ref in ((1, send_ref), (0, keep_ref)):
            core = lax.rem(my_core + flip, 2)
            for d in range(4):
                first = (lax.rem(my_z + d, 4) * 2 + core) * NCOL

                def fold(col, carry):
                    for tp in range(KC // 2):
                        t0 = acc_ref[(first + col) * KC + 2 * tp]
                        t1 = acc_ref[(first + col) * KC + 2 * tp + 1]
                        t0 = t0 + pltpu.roll(t0, B, 1)
                        t1 = t1 + pltpu.roll(t1, B, 1)
                        out_ref[d, col, tp] = jnp.where(low, t0, t1)
                    return carry

                lax.fori_loop(0, NCOL, fold, 0, unroll=4)


def coarse_terms(tgt, at, x, ps):
    shape = (4, NCOL, KC // 2, 8, 128)
    out = pl.BlockSpec(shape, lambda dx, tgt, at: (0, 0, 0, 0, 0))
    return pl.pallas_call(
        coarse_kernel,
        grid_spec=pltpu.PrefetchScalarGridSpec(
            num_scalar_prefetch=2,
            grid=(4,),
            in_specs=[pl.BlockSpec((NCOL, 2, B, 128), lambda dx, tgt, at: (0, 0, 0, 0))]
            + [pl.BlockSpec((1, 5, B, KP * B), lambda dx, tgt, at: (dx, 0, 0, 0))] * 4,
            out_specs=[out, out],
            scratch_shapes=[pltpu.VMEM((NCB * KC + 1, 8, 128), jnp.float32)],
        ),
        out_shape=[jax.ShapeDtypeStruct(shape, jnp.float32)] * 2,
        name="coarse_terms",
    )(tgt, at, x, *ps)


def ap_out_kernel(x_ref, out_ref, turn_ref):
    for ih in range(2):
        for qh in range(2):
            for s in range(KAP):
                m = jnp.concatenate(
                    [x_ref[bg * 2 + ih, qh, s * 8:(s + 1) * 8, :] for bg in range(8)], axis=0
                )
                t = m.astype(jnp.float32).T
                for lo in range(2):
                    top, bottom = t[lo * B:lo * B + 32], t[lo * B + 32:lo * B + B]
                    turn_ref[lo, pl.ds(s, 32, stride=8), :] = jnp.concatenate([top, bottom], axis=1)
            for lo in range(2):
                for h in range(32):
                    tile = turn_ref[lo, h * 8:(h + 1) * 8, :]
                    out_ref[ih * 4 + qh * 2 + lo, :, h * 128:(h + 1) * 128] = tile.astype(jnp.bfloat16)


def ap_layout(x):
    vmem = pl.BlockSpec(memory_space=pltpu.VMEM)
    return pl.pallas_call(
        ap_out_kernel,
        in_specs=[vmem],
        out_specs=vmem,
        scratch_shapes=[pltpu.VMEM((2, 256, 128), jnp.float32)],
        out_shape=jax.ShapeDtypeStruct((8, KAP, B * B), jnp.bfloat16),
        name="ap_layout",
    )(x)


def coarse_out_kernel(x_ref, out_ref, turn_ref, flat_ref):
    for tp in range(KC // 2):
        m = jnp.concatenate([x_ref[bg * 2, tp] + x_ref[bg * 2 + 1, tp] for bg in range(8)], axis=0)
        turn_ref[...] = m.T
        for lo in range(2):
            even = turn_ref[pl.ds(lo * B, 32, stride=2), :]
            odd = turn_ref[pl.ds(lo * B + 1, 32, stride=2), :]
            flat_ref[pl.ds(tp * 2 + lo, 32, stride=8), :] = jnp.concatenate([even, odd], axis=1)
    for h in range(32):
        out_ref[:, h * 128:(h + 1) * 128] = flat_ref[h * 8:(h + 1) * 8, :]


def coarse_layout(x):
    vmem = pl.BlockSpec(memory_space=pltpu.VMEM)
    return pl.pallas_call(
        coarse_out_kernel,
        in_specs=[vmem],
        out_specs=vmem,
        scratch_shapes=[pltpu.VMEM((128, B), jnp.float32), pltpu.VMEM((256, 128), jnp.float32)],
        out_shape=jax.ShapeDtypeStruct((KC, B * B), jnp.float32),
        name="coarse_layout",
    )(x)


def pick_rows(table, index):
    hot = (index[..., None] == jnp.arange(table.shape[0], dtype=jnp.int32)).astype(jnp.bfloat16)
    rows = jnp.einsum(
        "...k,km->...m", hot, table.astype(jnp.bfloat16), preferred_element_type=jnp.float32
    )
    return rows.astype(jnp.int32)


def index_slab(index):
    wide = jnp.pad(index.astype(jnp.bfloat16), ((0, B - index.shape[0]), (0, KP * B - KP)))
    return wide[None]


def step(a_blocks, a_index, p_blocks, p_index, ap_index, coarse_index):
    row = lax.axis_index("row")
    col = lax.axis_index("col")
    z, core = row // 2, row % 2
    y, x = col // 4, col % 4
    at = jnp.stack([x, y, z, core]).astype(jnp.int32)
    half = x % 2

    own = p_blocks[:, 0].reshape(8, KP, B, B)
    pt = own.transpose(0, 3, 1, 2).reshape(8, B, KP * B)
    pt = jnp.concatenate([pt, index_slab(p_index[:, 0])], axis=0)
    by_z = [pt] + [along_row(pt, d, 0) for d in (1, 2, 3)]
    parts = []
    for part in by_z:
        parts += [part, along_row(part, 0, 1)]

    pn = own.reshape(8, KP, 32, 2, B).transpose(0, 3, 2, 1, 4).reshape(2, 4, B, KP * B)
    halves = jnp.stack(
        [
            jnp.concatenate([pn[h], index_slab(p_index[4 * h:4 * h + 4, 0])], axis=0)
            for h in range(2)
        ]
    )
    same = lax.dynamic_index_in_dim(halves, half, 0, keepdims=False)
    diff = lax.dynamic_index_in_dim(halves, 1 - half, 0, keepdims=False)
    by_x = jnp.stack(
        [same, along_col(diff, 1, 0), along_col(same, 2, 0), along_col(diff, 3, 0)]
    )
    ps = [by_x] + [along_col(by_x, 0, d) for d in (1, 2, 3)]

    a = spread(a_blocks[:, 0]).reshape(4, 2, NCOL, B, KA * B)

    a_idx = a_index[:, 0]
    from_row = a_idx // 8
    place = ((z - from_row // 2) % 4) * 2 + (core + from_row) % 2
    place = place * 8 + a_idx % 8
    cols_k = jnp.concatenate([part[8, :8, :KP] for part in parts], axis=0)
    picked = pick_rows(cols_k, place)
    equal = picked[:, :, None, :] == ap_index[:, None, :, None]
    ids = place[:, :, None, None] * KP + jnp.arange(KP, dtype=jnp.int32)
    idx = jnp.min(jnp.where(equal, ids, NK * KP), axis=3).reshape(-1)

    dup = table(parts)
    q0 = products(0, idx, at, a, dup)
    x_sent = [along_col(q0[d], d, 0) for d in (1, 2, 3)]
    q1 = products(1, idx, at, a, dup)
    y_sent = [along_col(q1[d], 0, d) for d in (1, 2, 3)]
    s0 = middle(0, at, q0[0], *x_sent)
    y_last = [along_col(s0[d], 0, d) for d in (1, 2, 3)]
    s1 = middle(1, at, q1[0], *y_sent)
    x_last = [along_col(s1[d], d, 0) for d in (1, 2, 3)]
    apt = final([s0[0], *y_last, s1[0], *x_last])

    back = lax.all_to_all(apt, "col", 0, 0, tiled=True)
    ap_out = ap_layout(back).reshape(8, 1, KAP, B * B)

    cols_p = jnp.stack([p[:, 4, :4, :KP] for p in ps]).reshape(NCOL, 16)
    cc = jnp.arange(NCOL, dtype=jnp.int32)
    where = ((y - cc // 4) % 4) * 4 + (x - cc % 4) % 4
    cols_i = pick_rows(cols_p, where).reshape(NCOL, 4, KP)
    slots = lax.dynamic_index_in_dim(
        ap_index.reshape(2, 4, NCOL, KAP), half, 0, keepdims=False
    ).transpose(1, 0, 2)
    targets = pick_rows(coarse_index, cols_i)
    hit = targets[:, :, :, None, :] == slots[:, :, None, :, None]
    slot = cols_i[:, :, :, None, None] * KC + jnp.arange(KC, dtype=jnp.int32)
    tgt = jnp.min(jnp.where(hit, slot, NCB * KC), axis=4).reshape(-1)

    keep, send = coarse_terms(tgt, at, apt, ps)
    got = along_row(send, 0, 1)
    sums = [keep[d] + got[d] for d in range(4)]
    coarse = sums[0]
    moved = [along_row(sums[d], d, 0) for d in (1, 2, 3)]
    for part in moved:
        coarse = coarse + part
    coarse = lax.all_to_all(coarse, "col", 0, 0, tiled=True)
    coarse_out = coarse_layout(coarse).reshape(1, KC, B * B)
    return ap_out, coarse_out


def solution(mesh):
    placed = (
        P("row", "col", None, None),
        P("row", "col", None),
        P("row", "col", None, None),
        P("row", "col", None),
        P("row", None),
        P(),
    )
    return jax.shard_map(
        step,
        mesh=mesh,
        in_specs=placed,
        out_specs=(P("row", "col", None, None), P(("row", "col"), None, None)),
        check_vma=False,
    )
```

```python
import jax
import jax.numpy as jnp
from jax import lax
from jax.experimental import pallas as pl
from jax.experimental.pallas import tpu as pltpu
from jax.sharding import PartitionSpec as P


B = 64
KA = 4
KP = 4
KAP = 8
KC = 8
NCOL = 16
NK = 64
NCB = 128
FULL = 14.0
TINY = 1e-30


def along_row(v, dz, flip):
    pairs = [(r, ((r // 2 + dz) % 4) * 2 + (r % 2 + flip) % 2) for r in range(8)]
    return lax.ppermute(v, "row", pairs)


def along_col(v, dx, dy):
    pairs = [(c, ((c // 4 + dy) % 4) * 4 + (c % 4 + dx) % 4) for c in range(16)]
    return lax.ppermute(v, "col", pairs)


def low_lanes(rows):
    return lax.broadcasted_iota(jnp.int32, (rows, 128), 1) < B


def spread_kernel(a_ref, out_ref, buf_ref):
    low = low_lanes(32)

    def some(g, carry):
        for u in range(4):
            i = g * 4 + u
            v = a_ref[i].astype(jnp.float32)
            for h in range(32):
                buf_ref[u, h * 4:(h + 1) * 4, :] = v[:, h * 128:(h + 1) * 128]
        for u in range(4):
            i = g * 4 + u
            for ep in range(2):
                v0 = buf_ref[u, pl.ds(2 * ep, 32, stride=4), :]
                v1 = buf_ref[u, pl.ds(2 * ep + 1, 32, stride=4), :]
                top = jnp.where(low, v0, pltpu.roll(v1, B, 1))
                bottom = jnp.where(low, pltpu.roll(v0, B, 1), v1)
                out_ref[i, 0:32, ep * 128:(ep + 1) * 128] = top.astype(jnp.bfloat16)
                out_ref[i, 32:64, ep * 128:(ep + 1) * 128] = bottom.astype(jnp.bfloat16)
        return carry

    lax.fori_loop(0, 4, some, 0)


def spread(a):
    return pl.pallas_call(
        spread_kernel,
        grid=(8,),
        in_specs=[pl.BlockSpec((16, KA, B * B), lambda g: (g, 0, 0))],
        out_specs=pl.BlockSpec((16, B, KA * B), lambda g: (g, 0, 0)),
        scratch_shapes=[pltpu.VMEM((4, 128, 128), jnp.float32)],
        out_shape=jax.ShapeDtypeStruct((128, B, KA * B), jnp.bfloat16),
        name="spread",
    )(a)


def table_kernel(*refs):
    parts, out_ref, cols_ref = refs[:8], refs[8], refs[9]
    low = low_lanes(B)
    for n, part in enumerate(parts):
        cols_ref[n * 8:(n + 1) * 8, :] = part[8, 0:8, 0:128].astype(jnp.float32)

        def fill(q, carry):
            for mh in range(2):
                v = part[q, :, mh * 128:(mh + 1) * 128]
                turned = jnp.concatenate([v[:, B:], v[:, :B]], axis=1)
                at = (n * 8 + q) * 4 + 2 * mh
                out_ref[at] = jnp.where(low, v, turned)
                out_ref[at + 1] = jnp.where(low, turned, v)
            return carry

        lax.fori_loop(0, 8, fill, 0, unroll=2)
    out_ref[NK * KP] = jnp.zeros((B, 128), jnp.bfloat16)


def table(parts):
    whole = pl.BlockSpec(memory_space=pltpu.VMEM)
    return pl.pallas_call(
        table_kernel,
        in_specs=[whole] * 8,
        out_specs=[whole, whole],
        out_shape=[
            jax.ShapeDtypeStruct((NK * KP + 1, B, 128), jnp.bfloat16),
            jax.ShapeDtypeStruct((NK, 128), jnp.float32),
        ],
        name="table",
    )(*parts)


def nt_dot(a, b):
    return lax.dot_general(a, b, (((1,), (1,)), ((), ())), preferred_element_type=jnp.float32)


def exponent(most):
    return jnp.ceil(jnp.log2(jnp.maximum(most, TINY)))


def coded(v, mul):
    return jnp.round(v * mul).astype(jnp.int32).astype(jnp.int16)


def row_pair(lhs, rhs_top, rhs_bottom):
    zero = jnp.zeros((B, KA * B), jnp.bfloat16)
    stacked = jnp.concatenate(
        [
            jnp.concatenate([rhs_top, zero], axis=1),
            jnp.concatenate([zero, rhs_bottom], axis=1),
        ],
        axis=0,
    )
    return nt_dot(lhs, stacked)


def chosen_blocks(idx_ref, dup_ref, low, first_row):
    rows = []
    for s in range(KAP):
        pieces = []
        for lo in range(2):
            base = (first_row + lo * NCOL) * (KA * KAP)
            for ep in range(2):
                first = dup_ref[idx_ref[base + (2 * ep) * KAP + s]]
                second = dup_ref[idx_ref[base + (2 * ep + 1) * KAP + s]]
                pieces.append(jnp.where(low, first, second))
        rows.append(jnp.concatenate(pieces, axis=1))
    return jnp.concatenate(rows, axis=0)


def coded_products(res):
    e = exponent(jnp.max(jnp.abs(res), axis=0, keepdims=True))
    q = jnp.round(res * jnp.exp2(FULL - e)).astype(jnp.int32)

    def tile(bg, sp):
        r0 = 2 * sp * B + bg * 8
        return jnp.concatenate([q[r0:r0 + 8], q[r0 + B:r0 + B + 8]], axis=0)

    return e, tile


def x_product_kernel(j, idx_ref, at_ref, a_ref, dup_ref, near_ref, far_ref, exp_ref):
    cblk = pl.program_id(0)
    low = low_lanes(B)
    goal = lax.rem(at_ref[0] + j, 4)
    ih = lax.rem(goal, 2)
    count = a_ref.shape[2]
    is_low = goal < 2

    def one(cc, carry):
        c = cblk * count + cc
        lhs = chosen_blocks(idx_ref, dup_ref, low, ih * 4 * NCOL + c)
        res = row_pair(lhs, a_ref[0, 0, cc], a_ref[0, 1, cc])
        e, tile = coded_products(res)
        exp_ref[pl.ds(c, 1), :] = e
        for u in range(4):
            for sp in range(4):
                t0, t1 = tile(2 * u, sp), tile(2 * u + 1, sp)
                at = (u * NCOL + c) * 4 + sp
                near_ref[at] = jnp.where(is_low, t0, t1).astype(jnp.int16)
                far_ref[at] = jnp.where(is_low, t1, t0).astype(jnp.int16)
        return carry

    lax.fori_loop(0, count, one, 0)

    @pl.when(cblk == pl.num_programs(0) - 1)
    def _():
        e = exp_ref[...].astype(jnp.int32).astype(jnp.int16)
        near_ref[256] = e
        far_ref[256] = e


def x_products(j, idx, at, a, dup):
    block = 8
    out = pl.BlockSpec((257, 16, 128), lambda c, idx, at: (0, 0, 0))
    return pl.pallas_call(
        lambda *refs: x_product_kernel(j, *refs),
        grid_spec=pltpu.PrefetchScalarGridSpec(
            num_scalar_prefetch=2,
            grid=(NCOL // block,),
            in_specs=[
                pl.BlockSpec(
                    (1, 2, block, B, KA * B),
                    lambda c, idx, at: (lax.rem(at[0] + j, 2) * 2, 0, c, 0, 0),
                ),
                pl.BlockSpec((NK * KP + 1, B, 128), lambda c, idx, at: (0, 0, 0)),
            ],
            out_specs=[out, out],
            scratch_shapes=[pltpu.VMEM((NCOL, 128), jnp.float32)],
        ),
        out_shape=[jax.ShapeDtypeStruct((257, 16, 128), jnp.int16)] * 2,
    )(idx, at, a, dup)


def y_product_kernel(part, idx_ref, at_ref, a_ref, dup_ref, o0_ref, o1_ref, o2_ref, o3_ref, exp_ref):
    ih = pl.program_id(0)
    low = low_lanes(B)
    y = at_ref[1]
    count = a_ref.shape[2]
    outs = (o0_ref, o1_ref, o2_ref, o3_ref)
    turn1 = lax.rem(y, 2) == 1
    turn2 = y >= 2

    def one(cc, carry):
        lhs = chosen_blocks(idx_ref, dup_ref, low, (ih * 4 + 2) * NCOL + part * count + cc)
        res = row_pair(lhs, a_ref[0, 0, cc], a_ref[0, 1, cc])
        e, tile = coded_products(res)
        exp_ref[pl.ds(ih * 8 + cc, 1), :] = e
        for g in range(2):
            for sp in range(4):
                t = [tile(2 * k + g, sp) for k in range(4)]
                t = [jnp.where(turn1, t[(k + 1) % 4], t[k]) for k in range(4)]
                t = [jnp.where(turn2, t[(k + 2) % 4], t[k]) for k in range(4)]
                for d in range(4):
                    outs[d][((2 * g + ih) * 8 + cc) * 4 + sp] = t[d].astype(jnp.int16)
        return carry

    lax.fori_loop(0, count, one, 0)

    @pl.when(ih == 1)
    def _():
        e = exp_ref[...].astype(jnp.int32).astype(jnp.int16)
        for o_ref in outs:
            o_ref[128] = e


def y_products(part, idx, at, a, dup):
    block = 8
    out = pl.BlockSpec((129, 16, 128), lambda ih, idx, at: (0, 0, 0))
    return pl.pallas_call(
        lambda *refs: y_product_kernel(part, *refs),
        grid_spec=pltpu.PrefetchScalarGridSpec(
            num_scalar_prefetch=2,
            grid=(2,),
            in_specs=[
                pl.BlockSpec(
                    (1, 2, block, B, KA * B), lambda ih, idx, at: (ih * 2 + 1, 0, part, 0, 0)
                ),
                pl.BlockSpec((NK * KP + 1, B, 128), lambda ih, idx, at: (0, 0, 0)),
            ],
            out_specs=[out] * 4,
            scratch_shapes=[pltpu.VMEM((NCOL, 128), jnp.float32)],
        ),
        out_shape=[jax.ShapeDtypeStruct((129, 16, 128), jnp.int16)] * 4,
    )(idx, at, a, dup)


def sum_and_code(tiles, out_ref, c):
    most = jnp.maximum(
        jnp.maximum(jnp.abs(tiles[0]), jnp.abs(tiles[1])),
        jnp.maximum(jnp.abs(tiles[2]), jnp.abs(tiles[3])),
    )
    e = exponent(jnp.max(most, axis=0, keepdims=True))
    mul = jnp.exp2(FULL - e)
    for sp in range(4):
        out_ref[c * 4 + sp] = coded(tiles[sp], mul)
    return e


def x_middle_kernel(at_ref, m0, m1, m2, m3, o0, o1, o2, o3, scale_ref, exp_ref):
    parts = (m0, m1, m2, m3)
    for d, m in enumerate(parts):
        scale_ref[d] = jnp.exp2(m[256].astype(jnp.float32) - FULL)
    for d2, out_ref in enumerate((o0, o1, o2, o3)):
        u = lax.rem(at_ref[1] + d2, 4)

        def one(c, carry):
            scales = [scale_ref[d, pl.ds(c, 1), :] for d in range(4)]
            tiles = []
            for sp in range(4):
                terms = [
                    m[(u * NCOL + c) * 4 + sp].astype(jnp.float32) * scale
                    for m, scale in zip(parts, scales)
                ]
                tiles.append((terms[0] + terms[1]) + (terms[2] + terms[3]))
            exp_ref[pl.ds(c, 1), :] = sum_and_code(tiles, out_ref, c)
            return carry

        lax.fori_loop(0, NCOL, one, 0, unroll=2)
        out_ref[64] = exp_ref[...].astype(jnp.int32).astype(jnp.int16)


def y_middle_kernel(at_ref, *refs):
    parts, outs, scale_ref, exp_ref = refs[:8], refs[8:12], refs[12], refs[13]
    for n, m in enumerate(parts):
        scale_ref[n] = jnp.exp2(m[128].astype(jnp.float32) - FULL)
    for d2, out_ref in enumerate(outs):
        u = lax.rem(at_ref[0] + d2, 4)
        ih = lax.rem(u, 2)
        for half in range(2):
            own = parts[half * 4:half * 4 + 4]

            def one(cc, carry):
                scales = [scale_ref[half * 4 + d, pl.ds(ih * 8 + cc, 1), :] for d in range(4)]
                tiles = []
                for sp in range(4):
                    terms = [
                        m[(u * 8 + cc) * 4 + sp].astype(jnp.float32) * scale
                        for m, scale in zip(own, scales)
                    ]
                    tiles.append((terms[0] + terms[1]) + (terms[2] + terms[3]))
                c = half * 8 + cc
                exp_ref[pl.ds(c, 1), :] = sum_and_code(tiles, out_ref, c)
                return carry

            lax.fori_loop(0, 8, one, 0, unroll=2)
        out_ref[64] = exp_ref[...].astype(jnp.int32).astype(jnp.int16)


def middle(kernel, at, parts):
    vmem = pl.BlockSpec(memory_space=pltpu.VMEM)
    return pl.pallas_call(
        kernel,
        in_specs=[pl.BlockSpec(memory_space=pltpu.SMEM)] + [vmem] * len(parts),
        out_specs=[vmem] * 4,
        scratch_shapes=[
            pltpu.VMEM((len(parts), NCOL, 128), jnp.float32),
            pltpu.VMEM((NCOL, 128), jnp.float32),
        ],
        out_shape=[jax.ShapeDtypeStruct((65, 16, 128), jnp.int16)] * 4,
    )(at, *parts)


def decode(parts, out_ref, scale_ref):
    for n, m in enumerate(parts):
        scale_ref[n] = jnp.exp2(m[64].astype(jnp.float32) - FULL)

    def one(c, carry):
        for qh in range(2):
            scales = [scale_ref[qh * 4 + d, pl.ds(c, 1), :] for d in range(4)]
            for sp in range(4):
                terms = [
                    parts[qh * 4 + d][c * 4 + sp].astype(jnp.float32) * scales[d] for d in range(4)
                ]
                total = (terms[0] + terms[1]) + (terms[2] + terms[3])
                out_ref[c, qh, sp * 16:(sp + 1) * 16, :] = total.astype(jnp.bfloat16)
        return carry

    lax.fori_loop(0, NCOL, one, 0)


def coarse_kernel(tgt_ref, at_ref, *refs):
    parts, (p0_ref, p1_ref, p2_ref, p3_ref) = refs[:8], refs[8:12]
    x_ref, keep_ref, send_ref, acc_ref, scale_ref = refs[12:]
    dx = pl.program_id(0)
    low = low_lanes(8)
    low_x = low_lanes(B)
    my_x, my_y, my_z, my_core = at_ref[0], at_ref[1], at_ref[2], at_ref[3]

    @pl.when(dx == 0)
    def _():
        acc_ref[...] = jnp.zeros_like(acc_ref)
        decode(parts, x_ref, scale_ref)

    for dy, p_ref in enumerate((p0_ref, p1_ref, p2_ref, p3_ref)):
        c = lax.rem(my_y - dy + 4, 4) * 4 + lax.rem(my_x - dx + 4, 4)
        for qh in range(2):
            x = x_ref[c, qh]
            none = jnp.zeros_like(x)
            lhs = jnp.concatenate([jnp.where(low_x, x, none), jnp.where(low_x, none, x)], axis=0)
            rhs = p_ref[0, 2 * qh:2 * qh + 2].reshape(2 * B, KP * B)
            res = lax.dot_general(
                lhs, rhs, (((1,), (0,)), ((), ())), preferred_element_type=jnp.float32
            )
            for lo in range(2):
                ats, sums = [], []
                for m in range(KP):
                    for s in range(KAP):
                        at = tgt_ref[(((c * 2 + qh) * 2 + lo) * KP + m) * KAP + s]
                        rows = (lo * KAP + s) * 8
                        tile = res[rows:rows + 8, (m // 2) * 128:(m // 2) * 128 + 128]
                        keep = low if m % 2 == 0 else jnp.logical_not(low)
                        ats.append(at)
                        sums.append(acc_ref[at] + jnp.where(keep, tile, 0.0))
                for at, total in zip(ats, sums):
                    acc_ref[at] = total

    @pl.when(dx == 3)
    def _():
        for flip, out_ref in ((1, send_ref), (0, keep_ref)):
            core = lax.rem(my_core + flip, 2)
            for d in range(4):
                first = (lax.rem(my_z + d, 4) * 2 + core) * NCOL

                def fold(col, carry):
                    for tp in range(KC // 2):
                        t0 = acc_ref[(first + col) * KC + 2 * tp]
                        t1 = acc_ref[(first + col) * KC + 2 * tp + 1]
                        t0 = t0 + pltpu.roll(t0, B, 1)
                        t1 = t1 + pltpu.roll(t1, B, 1)
                        out_ref[d, col, tp] = jnp.where(low, t0, t1)
                    return carry

                lax.fori_loop(0, NCOL, fold, 0, unroll=4)


def coarse_terms(tgt, at, parts, ps):
    shape = (4, NCOL, KC // 2, 8, 128)
    out = pl.BlockSpec(shape, lambda dx, tgt, at: (0, 0, 0, 0, 0))
    return pl.pallas_call(
        coarse_kernel,
        grid_spec=pltpu.PrefetchScalarGridSpec(
            num_scalar_prefetch=2,
            grid=(4,),
            in_specs=[pl.BlockSpec((65, 16, 128), lambda dx, tgt, at: (0, 0, 0))] * 8
            + [pl.BlockSpec((1, 5, B, KP * B), lambda dx, tgt, at: (dx, 0, 0, 0))] * 4,
            out_specs=[
                pl.BlockSpec((NCOL, 2, B, 128), lambda dx, tgt, at: (0, 0, 0, 0)), out, out
            ],
            scratch_shapes=[
                pltpu.VMEM((NCB * KC + 1, 8, 128), jnp.float32),
                pltpu.VMEM((8, NCOL, 128), jnp.float32),
            ],
        ),
        out_shape=[
            jax.ShapeDtypeStruct((NCOL, 2, B, 128), jnp.bfloat16),
            jax.ShapeDtypeStruct(shape, jnp.float32),
            jax.ShapeDtypeStruct(shape, jnp.float32),
        ],
        name="coarse_terms",
    )(tgt, at, *parts, *ps)


def ap_out_kernel(x_ref, out_ref, turn_ref):
    for ih in range(2):
        for qh in range(2):
            for s in range(KAP):
                m = jnp.concatenate(
                    [x_ref[bg * 2 + ih, qh, s * 8:(s + 1) * 8, :] for bg in range(8)], axis=0
                )
                t = m.astype(jnp.float32).T
                for lo in range(2):
                    top, bottom = t[lo * B:lo * B + 32], t[lo * B + 32:lo * B + B]
                    turn_ref[lo, pl.ds(s, 32, stride=8), :] = jnp.concatenate([top, bottom], axis=1)
            for lo in range(2):
                for h in range(32):
                    tile = turn_ref[lo, h * 8:(h + 1) * 8, :]
                    out_ref[ih * 4 + qh * 2 + lo, :, h * 128:(h + 1) * 128] = tile.astype(jnp.bfloat16)


def ap_layout(x):
    vmem = pl.BlockSpec(memory_space=pltpu.VMEM)
    return pl.pallas_call(
        ap_out_kernel,
        in_specs=[vmem],
        out_specs=vmem,
        scratch_shapes=[pltpu.VMEM((2, 256, 128), jnp.float32)],
        out_shape=jax.ShapeDtypeStruct((8, KAP, B * B), jnp.bfloat16),
        name="ap_layout",
    )(x)


def coarse_out_kernel(x_ref, out_ref, turn_ref, flat_ref):
    for tp in range(KC // 2):
        m = jnp.concatenate([x_ref[bg * 2, tp] + x_ref[bg * 2 + 1, tp] for bg in range(8)], axis=0)
        turn_ref[...] = m.T
        for lo in range(2):
            even = turn_ref[pl.ds(lo * B, 32, stride=2), :]
            odd = turn_ref[pl.ds(lo * B + 1, 32, stride=2), :]
            flat_ref[pl.ds(tp * 2 + lo, 32, stride=8), :] = jnp.concatenate([even, odd], axis=1)
    for h in range(32):
        out_ref[:, h * 128:(h + 1) * 128] = flat_ref[h * 8:(h + 1) * 8, :]


def coarse_layout(x):
    vmem = pl.BlockSpec(memory_space=pltpu.VMEM)
    return pl.pallas_call(
        coarse_out_kernel,
        in_specs=[vmem],
        out_specs=vmem,
        scratch_shapes=[pltpu.VMEM((128, B), jnp.float32), pltpu.VMEM((256, 128), jnp.float32)],
        out_shape=jax.ShapeDtypeStruct((KC, B * B), jnp.float32),
        name="coarse_layout",
    )(x)


def pick_rows(table, index):
    hot = (index[..., None] == jnp.arange(table.shape[0], dtype=jnp.int32)).astype(jnp.bfloat16)
    rows = jnp.einsum(
        "...k,km->...m", hot, table.astype(jnp.bfloat16), preferred_element_type=jnp.float32
    )
    return rows.astype(jnp.int32)


def index_slab(index):
    wide = jnp.pad(index.astype(jnp.bfloat16), ((0, B - index.shape[0]), (0, KP * B - KP)))
    return wide[None]


def step(a_blocks, a_index, p_blocks, p_index, ap_index, coarse_index):
    row = lax.axis_index("row")
    col = lax.axis_index("col")
    z, core = row // 2, row % 2
    y, x = col // 4, col % 4
    at = jnp.stack([x, y, z, core]).astype(jnp.int32)
    half = x % 2

    own = p_blocks[:, 0].reshape(8, KP, B, B)
    pt = own.transpose(0, 3, 1, 2).reshape(8, B, KP * B)
    pt = jnp.concatenate([pt, index_slab(p_index[:, 0])], axis=0)
    by_z = [pt] + [along_row(pt, d, 0) for d in (1, 2, 3)]
    partner = along_row(pt, 0, 1)

    pn = own.reshape(8, KP, 32, 2, B).transpose(0, 3, 2, 1, 4).reshape(2, 4, B, KP * B)
    halves = jnp.stack(
        [
            jnp.concatenate([pn[h], index_slab(p_index[4 * h:4 * h + 4, 0])], axis=0)
            for h in range(2)
        ]
    )
    *by_z, halves = lax.optimization_barrier((*by_z, halves))
    parts = [by_z[0], partner]
    for part in by_z[1:]:
        parts += [part, along_row(part, 0, 1)]
    same = lax.dynamic_index_in_dim(halves, half, 0, keepdims=False)
    diff = lax.dynamic_index_in_dim(halves, 1 - half, 0, keepdims=False)
    by_x = [same, along_col(diff, 1, 0), along_col(same, 2, 0), along_col(diff, 3, 0)]
    by_x = jnp.stack(by_x)
    ps = [by_x] + [along_col(by_x, 0, d) for d in (1, 2, 3)]

    a = spread(a_blocks[:, 0]).reshape(4, 2, NCOL, B, KA * B)

    a_idx = a_index[:, 0]
    from_row = a_idx // 8
    place = ((z - from_row // 2) % 4) * 2 + (core + from_row) % 2
    place = place * 8 + a_idx % 8
    dup, cols_k = table(parts)
    picked = pick_rows(cols_k[:, :KP], place)
    equal = picked[:, :, None, :] == ap_index[:, None, :, None]
    ids = place[:, :, None, None] * KP + jnp.arange(KP, dtype=jnp.int32)
    idx = jnp.min(jnp.where(equal, ids, NK * KP), axis=3).reshape(-1)

    cols_p = jnp.stack([p[:, 4, :4, :KP] for p in ps]).reshape(NCOL, 16)
    cc = jnp.arange(NCOL, dtype=jnp.int32)
    where = ((y - cc // 4) % 4) * 4 + (x - cc % 4) % 4
    cols_i = pick_rows(cols_p, where).reshape(NCOL, 4, KP)
    slots = lax.dynamic_index_in_dim(
        ap_index.reshape(2, 4, NCOL, KAP), half, 0, keepdims=False
    ).transpose(1, 0, 2)
    targets = pick_rows(coarse_index, cols_i)
    hit = targets[:, :, :, None, :] == slots[:, :, None, :, None]
    slot = cols_i[:, :, :, None, None] * KC + jnp.arange(KC, dtype=jnp.int32)
    tgt = jnp.min(jnp.where(hit, slot, NCB * KC), axis=4).reshape(-1)

    x1, x3 = x_products(1, idx, at, a, dup)
    got_x1, got_x3 = along_col(x1, 1, 0), along_col(x3, 3, 0)
    ya = y_products(0, idx, at, a, dup)
    got_ya = [along_col(ya[d], 0, d) for d in (1, 2, 3)]
    x0, x2 = x_products(0, idx, at, a, dup)
    got_x2 = along_col(x2, 2, 0)
    yb = y_products(1, idx, at, a, dup)
    got_yb = [along_col(yb[d], 0, d) for d in (1, 2, 3)]
    s0 = middle(x_middle_kernel, at, [x0, got_x1, got_x2, got_x3])
    y_last = [along_col(s0[d], 0, d) for d in (1, 2, 3)]
    s1 = middle(y_middle_kernel, at, [ya[0], *got_ya, yb[0], *got_yb])
    x_last = [along_col(s1[d], d, 0) for d in (1, 2, 3)]

    apt, keep, send = coarse_terms(tgt, at, [s0[0], *y_last, s1[0], *x_last], ps)
    got = along_row(send, 0, 1)
    sums = [keep[d] + got[d] for d in range(4)]
    coarse = sums[0]
    moved = [along_row(sums[d], d, 0) for d in (1, 2, 3)]
    for part in moved:
        coarse = coarse + part
    back = lax.all_to_all(apt, "col", 0, 0, tiled=True)
    ap_out = ap_layout(back).reshape(8, 1, KAP, B * B)
    coarse = lax.all_to_all(coarse, "col", 0, 0, tiled=True)
    coarse_out = coarse_layout(coarse).reshape(1, KC, B * B)
    return ap_out, coarse_out


def solution(mesh):
    placed = (
        P("row", "col", None, None),
        P("row", "col", None),
        P("row", "col", None, None),
        P("row", "col", None),
        P("row", None),
        P(),
    )
    return jax.shard_map(
        step,
        mesh=mesh,
        in_specs=placed,
        out_specs=(P("row", "col", None, None), P(("row", "col"), None, None)),
        check_vma=False,
    )
```

```python
import jax
import jax.numpy as jnp
from jax import lax
from jax.experimental import pallas as pl
from jax.experimental.pallas import tpu as pltpu
from jax.sharding import PartitionSpec as P


B = 64
KA = 4
KP = 4
KAP = 8
KC = 8
NCOL = 16
NK = 64
NCB = 128
FULL = 14.0
TINY = 1e-30


def along_row(v, dz, flip):
    pairs = [(r, ((r // 2 + dz) % 4) * 2 + (r % 2 + flip) % 2) for r in range(8)]
    return lax.ppermute(v, "row", pairs)


def along_col(v, dx, dy):
    pairs = [(c, ((c // 4 + dy) % 4) * 4 + (c % 4 + dx) % 4) for c in range(16)]
    return lax.ppermute(v, "col", pairs)


def low_lanes(rows):
    return lax.broadcasted_iota(jnp.int32, (rows, 128), 1) < B


def spread_kernel(a_ref, out_ref, buf_ref):
    low = low_lanes(32)

    def some(g, carry):
        for u in range(4):
            i = g * 4 + u
            v = a_ref[i].astype(jnp.float32)
            for h in range(32):
                buf_ref[u, h * 4:(h + 1) * 4, :] = v[:, h * 128:(h + 1) * 128]
        for u in range(4):
            i = g * 4 + u
            for ep in range(2):
                v0 = buf_ref[u, pl.ds(2 * ep, 32, stride=4), :]
                v1 = buf_ref[u, pl.ds(2 * ep + 1, 32, stride=4), :]
                top = jnp.where(low, v0, pltpu.roll(v1, B, 1))
                bottom = jnp.where(low, pltpu.roll(v0, B, 1), v1)
                out_ref[i, 0:32, ep * 128:(ep + 1) * 128] = top.astype(jnp.bfloat16)
                out_ref[i, 32:64, ep * 128:(ep + 1) * 128] = bottom.astype(jnp.bfloat16)
        return carry

    lax.fori_loop(0, 4, some, 0)


def spread(a):
    return pl.pallas_call(
        spread_kernel,
        grid=(8,),
        in_specs=[pl.BlockSpec((16, KA, B * B), lambda g: (g, 0, 0))],
        out_specs=pl.BlockSpec((16, B, KA * B), lambda g: (g, 0, 0)),
        scratch_shapes=[pltpu.VMEM((4, 128, 128), jnp.float32)],
        out_shape=jax.ShapeDtypeStruct((128, B, KA * B), jnp.bfloat16),
        name="spread",
        compiler_params=pltpu.CompilerParams(vmem_limit_bytes=8 * 1024 * 1024),
    )(a)


def table_kernel(*refs):
    parts, out_ref, cols_ref = refs[:8], refs[8], refs[9]
    low = low_lanes(B)
    for n, part in enumerate(parts):
        cols_ref[n * 8:(n + 1) * 8, :] = part[8, 0:8, 0:128].astype(jnp.float32)

        def fill(q, carry):
            for mh in range(2):
                v = part[q, :, mh * 128:(mh + 1) * 128]
                turned = jnp.concatenate([v[:, B:], v[:, :B]], axis=1)
                at = (n * 8 + q) * 4 + 2 * mh
                out_ref[at] = jnp.where(low, v, turned)
                out_ref[at + 1] = jnp.where(low, turned, v)
            return carry

        lax.fori_loop(0, 8, fill, 0, unroll=2)
    out_ref[NK * KP] = jnp.zeros((B, 128), jnp.bfloat16)


def table(parts):
    whole = pl.BlockSpec(memory_space=pltpu.VMEM)
    return pl.pallas_call(
        table_kernel,
        in_specs=[whole] * 8,
        out_specs=[whole, whole],
        out_shape=[
            jax.ShapeDtypeStruct((NK * KP + 1, B, 128), jnp.bfloat16),
            jax.ShapeDtypeStruct((NK, 128), jnp.float32),
        ],
        name="table",
        compiler_params=pltpu.CompilerParams(vmem_limit_bytes=12 * 1024 * 1024),
    )(*parts)


def nt_dot(a, b):
    return lax.dot_general(a, b, (((1,), (1,)), ((), ())), preferred_element_type=jnp.float32)


def exponent(most):
    return jnp.ceil(jnp.log2(jnp.maximum(most, TINY)))


def coded(v, mul):
    return jnp.round(v * mul).astype(jnp.int32).astype(jnp.int16)


def row_pair(lhs, rhs_top, rhs_bottom):
    zero = jnp.zeros((B, KA * B), jnp.bfloat16)
    stacked = jnp.concatenate(
        [
            jnp.concatenate([rhs_top, zero], axis=1),
            jnp.concatenate([zero, rhs_bottom], axis=1),
        ],
        axis=0,
    )
    return nt_dot(lhs, stacked)


def chosen_blocks(idx_ref, dup_ref, low, first_row):
    rows = []
    for s in range(KAP):
        pieces = []
        for lo in range(2):
            base = (first_row + lo * NCOL) * (KA * KAP)
            for ep in range(2):
                first = dup_ref[idx_ref[base + (2 * ep) * KAP + s]]
                second = dup_ref[idx_ref[base + (2 * ep + 1) * KAP + s]]
                pieces.append(jnp.where(low, first, second))
        rows.append(jnp.concatenate(pieces, axis=1))
    return jnp.concatenate(rows, axis=0)


def coded_products(res):
    e = exponent(jnp.max(jnp.abs(res), axis=0, keepdims=True))
    q = jnp.round(res * jnp.exp2(FULL - e)).astype(jnp.int32)

    def tile(bg, sp):
        r0 = 2 * sp * B + bg * 8
        return jnp.concatenate([q[r0:r0 + 8], q[r0 + B:r0 + B + 8]], axis=0)

    return e, tile


def pipelined(count, multiply, encode, r0_ref, r1_ref):
    r1_ref[...] = jnp.zeros_like(r1_ref)

    def two(k, carry):
        r0_ref[...] = multiply(2 * k)
        encode(jnp.maximum(2 * k - 1, 0), r1_ref[...])
        r1_ref[...] = multiply(2 * k + 1)
        encode(2 * k, r0_ref[...])
        return carry

    lax.fori_loop(0, count // 2, two, 0)
    encode(count - 1, r1_ref[...])


def x_product_kernel(
    j, idx_ref, at_ref, a_ref, dup_ref, near_ref, far_ref, exp_ref, r0_ref, r1_ref
):
    cblk = pl.program_id(0)
    low = low_lanes(B)
    goal = lax.rem(at_ref[0] + j, 4)
    ih = lax.rem(goal, 2)
    count = a_ref.shape[2]
    is_low = goal < 2

    def multiply(cc):
        lhs = chosen_blocks(idx_ref, dup_ref, low, ih * 4 * NCOL + cblk * count + cc)
        return row_pair(lhs, a_ref[0, 0, cc], a_ref[0, 1, cc])

    def encode(cc, res):
        c = cblk * count + cc
        e, tile = coded_products(res)
        exp_ref[pl.ds(c, 1), :] = e
        for u in range(4):
            for sp in range(4):
                t0, t1 = tile(2 * u, sp), tile(2 * u + 1, sp)
                at = (u * NCOL + c) * 4 + sp
                near_ref[at] = jnp.where(is_low, t0, t1).astype(jnp.int16)
                far_ref[at] = jnp.where(is_low, t1, t0).astype(jnp.int16)

    pipelined(count, multiply, encode, r0_ref, r1_ref)

    @pl.when(cblk == pl.num_programs(0) - 1)
    def _():
        e = exp_ref[...].astype(jnp.int32).astype(jnp.int16)
        near_ref[256] = e
        far_ref[256] = e


def x_products(j, idx, at, a, dup):
    block = 8
    out = pl.BlockSpec((257, 16, 128), lambda c, idx, at: (0, 0, 0))
    return pl.pallas_call(
        lambda *refs: x_product_kernel(j, *refs),
        grid_spec=pltpu.PrefetchScalarGridSpec(
            num_scalar_prefetch=2,
            grid=(NCOL // block,),
            in_specs=[
                pl.BlockSpec(
                    (1, 2, block, B, KA * B),
                    lambda c, idx, at: (lax.rem(at[0] + j, 2) * 2, 0, c, 0, 0),
                ),
                pl.BlockSpec(memory_space=pltpu.VMEM),
            ],
            out_specs=[out, out],
            scratch_shapes=[pltpu.VMEM((NCOL, 128), jnp.float32)]
            + [pltpu.VMEM((KAP * B, 128), jnp.float32)] * 2,
        ),
        out_shape=[jax.ShapeDtypeStruct((257, 16, 128), jnp.int16)] * 2,
        compiler_params=pltpu.CompilerParams(vmem_limit_bytes=20 * 1024 * 1024),
    )(idx, at, a, pltpu.with_memory_space_constraint(dup, pltpu.VMEM))


def y_product_kernel(
    part, idx_ref, at_ref, a_ref, dup_ref, o0_ref, o1_ref, o2_ref, o3_ref, exp_ref, r0_ref, r1_ref
):
    ih = pl.program_id(0)
    low = low_lanes(B)
    y = at_ref[1]
    count = a_ref.shape[2]
    outs = (o0_ref, o1_ref, o2_ref, o3_ref)
    turn1 = lax.rem(y, 2) == 1
    turn2 = y >= 2

    def multiply(cc):
        lhs = chosen_blocks(idx_ref, dup_ref, low, (ih * 4 + 2) * NCOL + part * count + cc)
        return row_pair(lhs, a_ref[0, 0, cc], a_ref[0, 1, cc])

    def encode(cc, res):
        e, tile = coded_products(res)
        exp_ref[pl.ds(ih * 8 + cc, 1), :] = e
        for g in range(2):
            for sp in range(4):
                t = [tile(2 * k + g, sp) for k in range(4)]
                t = [jnp.where(turn1, t[(k + 1) % 4], t[k]) for k in range(4)]
                t = [jnp.where(turn2, t[(k + 2) % 4], t[k]) for k in range(4)]
                for d in range(4):
                    outs[d][((2 * g + ih) * 8 + cc) * 4 + sp] = t[d].astype(jnp.int16)

    pipelined(count, multiply, encode, r0_ref, r1_ref)

    @pl.when(ih == 1)
    def _():
        e = exp_ref[...].astype(jnp.int32).astype(jnp.int16)
        for o_ref in outs:
            o_ref[128] = e


def y_products(part, idx, at, a, dup):
    block = 8
    out = pl.BlockSpec((129, 16, 128), lambda ih, idx, at: (0, 0, 0))
    return pl.pallas_call(
        lambda *refs: y_product_kernel(part, *refs),
        grid_spec=pltpu.PrefetchScalarGridSpec(
            num_scalar_prefetch=2,
            grid=(2,),
            in_specs=[
                pl.BlockSpec(
                    (1, 2, block, B, KA * B), lambda ih, idx, at: (ih * 2 + 1, 0, part, 0, 0)
                ),
                pl.BlockSpec(memory_space=pltpu.VMEM),
            ],
            out_specs=[out] * 4,
            scratch_shapes=[pltpu.VMEM((NCOL, 128), jnp.float32)]
            + [pltpu.VMEM((KAP * B, 128), jnp.float32)] * 2,
        ),
        out_shape=[jax.ShapeDtypeStruct((129, 16, 128), jnp.int16)] * 4,
        compiler_params=pltpu.CompilerParams(vmem_limit_bytes=20 * 1024 * 1024),
    )(idx, at, a, pltpu.with_memory_space_constraint(dup, pltpu.VMEM))


def sum_and_code(tiles, out_ref, c):
    most = jnp.maximum(
        jnp.maximum(jnp.abs(tiles[0]), jnp.abs(tiles[1])),
        jnp.maximum(jnp.abs(tiles[2]), jnp.abs(tiles[3])),
    )
    e = exponent(jnp.max(most, axis=0, keepdims=True))
    mul = jnp.exp2(FULL - e)
    for sp in range(4):
        out_ref[c * 4 + sp] = coded(tiles[sp], mul)
    return e


def x_middle_kernel(at_ref, m0, m1, m2, m3, o0, o1, o2, o3, scale_ref, exp_ref):
    parts = (m0, m1, m2, m3)
    for d, m in enumerate(parts):
        scale_ref[d] = jnp.exp2(m[256].astype(jnp.float32) - FULL)
    for d2, out_ref in enumerate((o0, o1, o2, o3)):
        u = lax.rem(at_ref[1] + d2, 4)

        def one(c, carry):
            scales = [scale_ref[d, pl.ds(c, 1), :] for d in range(4)]
            tiles = []
            for sp in range(4):
                terms = [
                    m[(u * NCOL + c) * 4 + sp].astype(jnp.float32) * scale
                    for m, scale in zip(parts, scales)
                ]
                tiles.append((terms[0] + terms[1]) + (terms[2] + terms[3]))
            exp_ref[pl.ds(c, 1), :] = sum_and_code(tiles, out_ref, c)
            return carry

        lax.fori_loop(0, NCOL, one, 0, unroll=2)
        out_ref[64] = exp_ref[...].astype(jnp.int32).astype(jnp.int16)


def y_middle_kernel(at_ref, *refs):
    parts, outs, scale_ref, exp_ref = refs[:8], refs[8:12], refs[12], refs[13]
    for n, m in enumerate(parts):
        scale_ref[n] = jnp.exp2(m[128].astype(jnp.float32) - FULL)
    for d2, out_ref in enumerate(outs):
        u = lax.rem(at_ref[0] + d2, 4)
        ih = lax.rem(u, 2)
        for half in range(2):
            own = parts[half * 4:half * 4 + 4]

            def one(cc, carry):
                scales = [scale_ref[half * 4 + d, pl.ds(ih * 8 + cc, 1), :] for d in range(4)]
                tiles = []
                for sp in range(4):
                    terms = [
                        m[(u * 8 + cc) * 4 + sp].astype(jnp.float32) * scale
                        for m, scale in zip(own, scales)
                    ]
                    tiles.append((terms[0] + terms[1]) + (terms[2] + terms[3]))
                c = half * 8 + cc
                exp_ref[pl.ds(c, 1), :] = sum_and_code(tiles, out_ref, c)
                return carry

            lax.fori_loop(0, 8, one, 0, unroll=2)
        out_ref[64] = exp_ref[...].astype(jnp.int32).astype(jnp.int16)


def middle(kernel, at, parts):
    vmem = pl.BlockSpec(memory_space=pltpu.VMEM)
    return pl.pallas_call(
        kernel,
        in_specs=[pl.BlockSpec(memory_space=pltpu.SMEM)] + [vmem] * len(parts),
        out_specs=[vmem] * 4,
        scratch_shapes=[
            pltpu.VMEM((len(parts), NCOL, 128), jnp.float32),
            pltpu.VMEM((NCOL, 128), jnp.float32),
        ],
        out_shape=[jax.ShapeDtypeStruct((65, 16, 128), jnp.int16)] * 4,
    )(at, *parts)


def decode(parts, out_ref, scale_ref):
    for n, m in enumerate(parts):
        scale_ref[n] = jnp.exp2(m[64].astype(jnp.float32) - FULL)

    def one(c, carry):
        for qh in range(2):
            scales = [scale_ref[qh * 4 + d, pl.ds(c, 1), :] for d in range(4)]
            for sp in range(4):
                terms = [
                    parts[qh * 4 + d][c * 4 + sp].astype(jnp.float32) * scales[d] for d in range(4)
                ]
                total = (terms[0] + terms[1]) + (terms[2] + terms[3])
                out_ref[c, qh, sp * 16:(sp + 1) * 16, :] = total.astype(jnp.bfloat16)
        return carry

    lax.fori_loop(0, NCOL, one, 0)


def coarse_kernel(tgt_ref, at_ref, *refs):
    parts, (p0_ref, p1_ref, p2_ref, p3_ref) = refs[:8], refs[8:12]
    x_ref, keep_ref, send_ref, acc_ref, scale_ref = refs[12:]
    dx = pl.program_id(0)
    low = low_lanes(8)
    low_x = low_lanes(B)
    my_x, my_y, my_z, my_core = at_ref[0], at_ref[1], at_ref[2], at_ref[3]

    @pl.when(dx == 0)
    def _():
        acc_ref[...] = jnp.zeros_like(acc_ref)
        decode(parts, x_ref, scale_ref)

    for dy, p_ref in enumerate((p0_ref, p1_ref, p2_ref, p3_ref)):
        c = lax.rem(my_y - dy + 4, 4) * 4 + lax.rem(my_x - dx + 4, 4)
        for qh in range(2):
            x = x_ref[c, qh]
            none = jnp.zeros_like(x)
            lhs = jnp.concatenate([jnp.where(low_x, x, none), jnp.where(low_x, none, x)], axis=0)
            rhs = p_ref[0, 2 * qh:2 * qh + 2].reshape(2 * B, KP * B)
            res = lax.dot_general(
                lhs, rhs, (((1,), (0,)), ((), ())), preferred_element_type=jnp.float32
            )
            for lo in range(2):
                ats, sums = [], []
                for m in range(KP):
                    for s in range(KAP):
                        at = tgt_ref[(((c * 2 + qh) * 2 + lo) * KP + m) * KAP + s]
                        rows = (lo * KAP + s) * 8
                        tile = res[rows:rows + 8, (m // 2) * 128:(m // 2) * 128 + 128]
                        keep = low if m % 2 == 0 else jnp.logical_not(low)
                        ats.append(at)
                        sums.append(acc_ref[at] + jnp.where(keep, tile, 0.0))
                for at, total in zip(ats, sums):
                    acc_ref[at] = total

    @pl.when(dx == 3)
    def _():
        for flip, out_ref in ((1, send_ref), (0, keep_ref)):
            core = lax.rem(my_core + flip, 2)
            for d in range(4):
                first = (lax.rem(my_z + d, 4) * 2 + core) * NCOL

                def fold(col, carry):
                    for tp in range(KC // 2):
                        t0 = acc_ref[(first + col) * KC + 2 * tp]
                        t1 = acc_ref[(first + col) * KC + 2 * tp + 1]
                        t0 = t0 + pltpu.roll(t0, B, 1)
                        t1 = t1 + pltpu.roll(t1, B, 1)
                        out_ref[d, col, tp] = jnp.where(low, t0, t1)
                    return carry

                lax.fori_loop(0, NCOL, fold, 0, unroll=4)


def coarse_terms(tgt, at, parts, ps):
    shape = (4, NCOL, KC // 2, 8, 128)
    out = pl.BlockSpec(shape, lambda dx, tgt, at: (0, 0, 0, 0, 0))
    return pl.pallas_call(
        coarse_kernel,
        grid_spec=pltpu.PrefetchScalarGridSpec(
            num_scalar_prefetch=2,
            grid=(4,),
            in_specs=[pl.BlockSpec((65, 16, 128), lambda dx, tgt, at: (0, 0, 0))] * 8
            + [pl.BlockSpec((1, 5, B, KP * B), lambda dx, tgt, at: (dx, 0, 0, 0))] * 4,
            out_specs=[
                pl.BlockSpec((NCOL, 2, B, 128), lambda dx, tgt, at: (0, 0, 0, 0)), out, out
            ],
            scratch_shapes=[
                pltpu.VMEM((NCB * KC + 1, 8, 128), jnp.float32),
                pltpu.VMEM((8, NCOL, 128), jnp.float32),
            ],
        ),
        out_shape=[
            jax.ShapeDtypeStruct((NCOL, 2, B, 128), jnp.bfloat16),
            jax.ShapeDtypeStruct(shape, jnp.float32),
            jax.ShapeDtypeStruct(shape, jnp.float32),
        ],
        name="coarse_terms",
    )(tgt, at, *parts, *ps)


def ap_out_kernel(x_ref, out_ref, turn_ref):
    for ih in range(2):
        for qh in range(2):
            for s in range(KAP):
                m = jnp.concatenate(
                    [x_ref[bg * 2 + ih, qh, s * 8:(s + 1) * 8, :] for bg in range(8)], axis=0
                )
                t = m.astype(jnp.float32).T
                for lo in range(2):
                    top, bottom = t[lo * B:lo * B + 32], t[lo * B + 32:lo * B + B]
                    turn_ref[lo, pl.ds(s, 32, stride=8), :] = jnp.concatenate([top, bottom], axis=1)
            for lo in range(2):
                for h in range(32):
                    tile = turn_ref[lo, h * 8:(h + 1) * 8, :]
                    out_ref[ih * 4 + qh * 2 + lo, :, h * 128:(h + 1) * 128] = tile.astype(jnp.bfloat16)


def ap_layout(x):
    vmem = pl.BlockSpec(memory_space=pltpu.VMEM)
    return pl.pallas_call(
        ap_out_kernel,
        in_specs=[vmem],
        out_specs=vmem,
        scratch_shapes=[pltpu.VMEM((2, 256, 128), jnp.float32)],
        out_shape=jax.ShapeDtypeStruct((8, KAP, B * B), jnp.bfloat16),
        name="ap_layout",
    )(x)


def coarse_out_kernel(x_ref, out_ref, turn_ref, flat_ref):
    for tp in range(KC // 2):
        m = jnp.concatenate([x_ref[bg * 2, tp] + x_ref[bg * 2 + 1, tp] for bg in range(8)], axis=0)
        turn_ref[...] = m.T
        for lo in range(2):
            even = turn_ref[pl.ds(lo * B, 32, stride=2), :]
            odd = turn_ref[pl.ds(lo * B + 1, 32, stride=2), :]
            flat_ref[pl.ds(tp * 2 + lo, 32, stride=8), :] = jnp.concatenate([even, odd], axis=1)
    for h in range(32):
        out_ref[:, h * 128:(h + 1) * 128] = flat_ref[h * 8:(h + 1) * 8, :]


def coarse_layout(x):
    vmem = pl.BlockSpec(memory_space=pltpu.VMEM)
    return pl.pallas_call(
        coarse_out_kernel,
        in_specs=[vmem],
        out_specs=vmem,
        scratch_shapes=[pltpu.VMEM((128, B), jnp.float32), pltpu.VMEM((256, 128), jnp.float32)],
        out_shape=jax.ShapeDtypeStruct((KC, B * B), jnp.float32),
        name="coarse_layout",
    )(x)


def pick_rows(table, index):
    hot = (index[..., None] == jnp.arange(table.shape[0], dtype=jnp.int32)).astype(jnp.bfloat16)
    rows = jnp.einsum(
        "...k,km->...m", hot, table.astype(jnp.bfloat16), preferred_element_type=jnp.float32
    )
    return rows.astype(jnp.int32)


def index_slab(index):
    wide = jnp.pad(index.astype(jnp.bfloat16), ((0, B - index.shape[0]), (0, KP * B - KP)))
    return wide[None]


def step(a_blocks, a_index, p_blocks, p_index, ap_index, coarse_index):
    row = lax.axis_index("row")
    col = lax.axis_index("col")
    z, core = row // 2, row % 2
    y, x = col // 4, col % 4
    at = jnp.stack([x, y, z, core]).astype(jnp.int32)
    half = x % 2

    own = p_blocks[:, 0].reshape(8, KP, B, B)
    pt = own.transpose(0, 3, 1, 2).reshape(8, B, KP * B)
    pt = jnp.concatenate([pt, index_slab(p_index[:, 0])], axis=0)
    by_z = [pt] + [along_row(pt, d, 0) for d in (1, 2, 3)]
    partner = along_row(pt, 0, 1)

    pn = own.reshape(8, KP, 32, 2, B).transpose(0, 3, 2, 1, 4).reshape(2, 4, B, KP * B)
    halves = jnp.stack(
        [
            jnp.concatenate([pn[h], index_slab(p_index[4 * h:4 * h + 4, 0])], axis=0)
            for h in range(2)
        ]
    )
    *by_z, halves = lax.optimization_barrier((*by_z, halves))
    parts = [by_z[0], partner]
    for part in by_z[1:]:
        parts += [part, along_row(part, 0, 1)]
    same = lax.dynamic_index_in_dim(halves, half, 0, keepdims=False)
    diff = lax.dynamic_index_in_dim(halves, 1 - half, 0, keepdims=False)
    by_x = [same, along_col(diff, 1, 0), along_col(same, 2, 0), along_col(diff, 3, 0)]
    by_x = jnp.stack(by_x)
    ps = [by_x] + [along_col(by_x, 0, d) for d in (1, 2, 3)]

    a = spread(a_blocks[:, 0]).reshape(4, 2, NCOL, B, KA * B)

    a_idx = a_index[:, 0]
    from_row = a_idx // 8
    place = ((z - from_row // 2) % 4) * 2 + (core + from_row) % 2
    place = place * 8 + a_idx % 8
    dup, cols_k = table(parts)
    picked = pick_rows(cols_k[:, :KP], place)
    equal = picked[:, :, None, :] == ap_index[:, None, :, None]
    ids = place[:, :, None, None] * KP + jnp.arange(KP, dtype=jnp.int32)
    idx = jnp.min(jnp.where(equal, ids, NK * KP), axis=3).reshape(-1)

    cols_p = jnp.stack([p[:, 4, :4, :KP] for p in ps]).reshape(NCOL, 16)
    cc = jnp.arange(NCOL, dtype=jnp.int32)
    where = ((y - cc // 4) % 4) * 4 + (x - cc % 4) % 4
    cols_i = pick_rows(cols_p, where).reshape(NCOL, 4, KP)
    slots = lax.dynamic_index_in_dim(
        ap_index.reshape(2, 4, NCOL, KAP), half, 0, keepdims=False
    ).transpose(1, 0, 2)
    targets = pick_rows(coarse_index, cols_i)
    hit = targets[:, :, :, None, :] == slots[:, :, None, :, None]
    slot = cols_i[:, :, :, None, None] * KC + jnp.arange(KC, dtype=jnp.int32)
    tgt = jnp.min(jnp.where(hit, slot, NCB * KC), axis=4).reshape(-1)

    x1, x3 = x_products(1, idx, at, a, dup)
    got_x1, got_x3 = along_col(x1, 1, 0), along_col(x3, 3, 0)
    ya = y_products(0, idx, at, a, dup)
    got_ya = [along_col(ya[d], 0, d) for d in (1, 2, 3)]
    x0, x2 = x_products(0, idx, at, a, dup)
    got_x2 = along_col(x2, 2, 0)
    yb = y_products(1, idx, at, a, dup)
    got_yb = [along_col(yb[d], 0, d) for d in (1, 2, 3)]
    s0 = middle(x_middle_kernel, at, [x0, got_x1, got_x2, got_x3])
    y_last = [along_col(s0[d], 0, d) for d in (1, 2, 3)]
    s1 = middle(y_middle_kernel, at, [ya[0], *got_ya, yb[0], *got_yb])
    x_last = [along_col(s1[d], d, 0) for d in (1, 2, 3)]

    apt, keep, send = coarse_terms(tgt, at, [s0[0], *y_last, s1[0], *x_last], ps)
    got = along_row(send, 0, 1)
    sums = [keep[d] + got[d] for d in range(4)]
    coarse = sums[0]
    moved = [along_row(sums[d], d, 0) for d in (1, 2, 3)]
    for part in moved:
        coarse = coarse + part
    back = lax.all_to_all(apt, "col", 0, 0, tiled=True)
    ap_out = ap_layout(back).reshape(8, 1, KAP, B * B)
    coarse = lax.all_to_all(coarse, "col", 0, 0, tiled=True)
    coarse_out = coarse_layout(coarse).reshape(1, KC, B * B)
    return ap_out, coarse_out


def solution(mesh):
    placed = (
        P("row", "col", None, None),
        P("row", "col", None),
        P("row", "col", None, None),
        P("row", "col", None),
        P("row", None),
        P(),
    )
    return jax.shard_map(
        step,
        mesh=mesh,
        in_specs=placed,
        out_specs=(P("row", "col", None, None), P(("row", "col"), None, None)),
        check_vma=False,
    )
```

```python
import jax
import jax.numpy as jnp
from jax import lax
from jax.experimental import pallas as pl
from jax.experimental.pallas import tpu as pltpu
from jax.sharding import PartitionSpec as P


B = 64
KA = 4
KP = 4
KAP = 8
KC = 8
NCOL = 16
NK = 64
NCB = 128
FULL = 14.0
TINY = 1e-30


def along_row(v, dz, flip):
    pairs = [(r, ((r // 2 + dz) % 4) * 2 + (r % 2 + flip) % 2) for r in range(8)]
    return lax.ppermute(v, "row", pairs)


def along_col(v, dx, dy):
    pairs = [(c, ((c // 4 + dy) % 4) * 4 + (c % 4 + dx) % 4) for c in range(16)]
    return lax.ppermute(v, "col", pairs)


def low_lanes(rows):
    return lax.broadcasted_iota(jnp.int32, (rows, 128), 1) < B


def spread_kernel(a_ref, out_ref, buf_ref):
    low = low_lanes(32)

    def some(g, carry):
        for u in range(4):
            i = g * 4 + u
            v = a_ref[i].astype(jnp.float32)
            for h in range(32):
                buf_ref[u, h * 4:(h + 1) * 4, :] = v[:, h * 128:(h + 1) * 128]
        for u in range(4):
            i = g * 4 + u
            for ep in range(2):
                v0 = buf_ref[u, pl.ds(2 * ep, 32, stride=4), :]
                v1 = buf_ref[u, pl.ds(2 * ep + 1, 32, stride=4), :]
                top = jnp.where(low, v0, pltpu.roll(v1, B, 1))
                bottom = jnp.where(low, pltpu.roll(v0, B, 1), v1)
                out_ref[i, 0:32, ep * 128:(ep + 1) * 128] = top.astype(jnp.bfloat16)
                out_ref[i, 32:64, ep * 128:(ep + 1) * 128] = bottom.astype(jnp.bfloat16)
        return carry

    lax.fori_loop(0, 4, some, 0)


def spread(a):
    return pl.pallas_call(
        spread_kernel,
        grid=(8,),
        in_specs=[pl.BlockSpec((16, KA, B * B), lambda g: (g, 0, 0))],
        out_specs=pl.BlockSpec((16, B, KA * B), lambda g: (g, 0, 0)),
        scratch_shapes=[pltpu.VMEM((4, 128, 128), jnp.float32)],
        out_shape=pltpu.HBM((128, B, KA * B), jnp.bfloat16),
        name="spread",
        compiler_params=pltpu.CompilerParams(vmem_limit_bytes=8 * 1024 * 1024),
    )(pltpu.with_memory_space_constraint(a, pltpu.HBM))


def table_kernel(*refs):
    parts, out_ref, cols_ref = refs[:8], refs[8], refs[9]
    low = low_lanes(B)
    for n, part in enumerate(parts):
        cols_ref[n * 8:(n + 1) * 8, :] = part[8 * B:8 * B + 8, 0:128].astype(jnp.float32)

        def fill(q, carry):
            for mh in range(2):
                v = part[pl.ds(pl.multiple_of(q * B, B), B), mh * 128:(mh + 1) * 128]
                turned = jnp.concatenate([v[:, B:], v[:, :B]], axis=1)
                at = (n * 8 + q) * 4 + 2 * mh
                out_ref[at] = jnp.where(low, v, turned)
                out_ref[at + 1] = jnp.where(low, turned, v)
            return carry

        lax.fori_loop(0, 8, fill, 0, unroll=2)
    out_ref[NK * KP] = jnp.zeros((B, 128), jnp.bfloat16)


def table(parts):
    whole = pl.BlockSpec(memory_space=pltpu.VMEM)
    return pl.pallas_call(
        table_kernel,
        in_specs=[whole] * 8,
        out_specs=[whole, whole],
        out_shape=[
            pltpu.HBM((NK * KP + 1, B, 128), jnp.bfloat16),
            jax.ShapeDtypeStruct((NK, 128), jnp.float32),
        ],
        name="table",
        compiler_params=pltpu.CompilerParams(vmem_limit_bytes=12 * 1024 * 1024),
    )(*parts)


def nt_dot(a, b):
    return lax.dot_general(a, b, (((1,), (1,)), ((), ())), preferred_element_type=jnp.float32)


def exponent(most):
    return jnp.ceil(jnp.log2(jnp.maximum(most, TINY)))


def coded(v, mul):
    return jnp.round(v * mul).astype(jnp.int32).astype(jnp.int16)


def row_pair(lhs, rhs_top, rhs_bottom):
    zero = jnp.zeros((B, KA * B), jnp.bfloat16)
    stacked = jnp.concatenate(
        [
            jnp.concatenate([rhs_top, zero], axis=1),
            jnp.concatenate([zero, rhs_bottom], axis=1),
        ],
        axis=0,
    )
    return nt_dot(lhs, stacked)


def chosen_blocks(idx_ref, dup_ref, low, first_row):
    rows = []
    for s in range(KAP):
        pieces = []
        for lo in range(2):
            base = (first_row + lo * NCOL) * (KA * KAP)
            for ep in range(2):
                first = dup_ref[idx_ref[base + (2 * ep) * KAP + s]]
                second = dup_ref[idx_ref[base + (2 * ep + 1) * KAP + s]]
                pieces.append(jnp.where(low, first, second))
        rows.append(jnp.concatenate(pieces, axis=1))
    return jnp.concatenate(rows, axis=0)


def coded_products(res):
    e = exponent(jnp.max(jnp.abs(res), axis=0, keepdims=True))
    q = jnp.round(res * jnp.exp2(FULL - e)).astype(jnp.int32)

    def tile(bg, sp):
        r0 = 2 * sp * B + bg * 8
        return jnp.concatenate([q[r0:r0 + 8], q[r0 + B:r0 + B + 8]], axis=0)

    return e, tile


def pipelined(count, multiply, encode, r0_ref, r1_ref):
    r1_ref[...] = jnp.zeros_like(r1_ref)

    def two(k, carry):
        r0_ref[...] = multiply(2 * k)
        encode(jnp.maximum(2 * k - 1, 0), r1_ref[...])
        r1_ref[...] = multiply(2 * k + 1)
        encode(2 * k, r0_ref[...])
        return carry

    lax.fori_loop(0, count // 2, two, 0)
    encode(count - 1, r1_ref[...])


def x_product_kernel(
    j, idx_ref, at_ref, a_ref, dup_ref, near_ref, far_ref, exp_ref, r0_ref, r1_ref
):
    cblk = pl.program_id(0)
    low = low_lanes(B)
    goal = lax.rem(at_ref[0] + j, 4)
    ih = lax.rem(goal, 2)
    count = a_ref.shape[2]
    is_low = goal < 2

    def multiply(cc):
        lhs = chosen_blocks(idx_ref, dup_ref, low, ih * 4 * NCOL + cblk * count + cc)
        return row_pair(lhs, a_ref[0, 0, cc], a_ref[0, 1, cc])

    def encode(cc, res):
        c = cblk * count + cc
        e, tile = coded_products(res)
        exp_ref[pl.ds(c, 1), :] = e
        for u in range(4):
            for sp in range(4):
                t0, t1 = tile(2 * u, sp), tile(2 * u + 1, sp)
                at = (u * NCOL + c) * 4 + sp
                near_ref[at] = jnp.where(is_low, t0, t1).astype(jnp.int16)
                far_ref[at] = jnp.where(is_low, t1, t0).astype(jnp.int16)

    pipelined(count, multiply, encode, r0_ref, r1_ref)

    @pl.when(cblk == pl.num_programs(0) - 1)
    def _():
        e = exp_ref[...].astype(jnp.int32).astype(jnp.int16)
        near_ref[256] = e
        far_ref[256] = e


def x_products(j, idx, at, a, dup):
    block = 8
    out = pl.BlockSpec((257, 16, 128), lambda c, idx, at: (0, 0, 0))
    return pl.pallas_call(
        lambda *refs: x_product_kernel(j, *refs),
        grid_spec=pltpu.PrefetchScalarGridSpec(
            num_scalar_prefetch=2,
            grid=(NCOL // block,),
            in_specs=[
                pl.BlockSpec(
                    (1, 2, block, B, KA * B),
                    lambda c, idx, at: (lax.rem(at[0] + j, 2) * 2, 0, c, 0, 0),
                ),
                pl.BlockSpec(memory_space=pltpu.VMEM),
            ],
            out_specs=[out, out],
            scratch_shapes=[pltpu.VMEM((NCOL, 128), jnp.float32)]
            + [pltpu.VMEM((KAP * B, 128), jnp.float32)] * 2,
        ),
        out_shape=[jax.ShapeDtypeStruct((257, 16, 128), jnp.int16)] * 2,
        compiler_params=pltpu.CompilerParams(vmem_limit_bytes=20 * 1024 * 1024),
    )(
        idx,
        at,
        pltpu.with_memory_space_constraint(a, pltpu.HBM),
        pltpu.with_memory_space_constraint(dup, pltpu.VMEM),
    )


def y_product_kernel(
    part, idx_ref, at_ref, a_ref, dup_ref, o0_ref, o1_ref, o2_ref, o3_ref, exp_ref, r0_ref, r1_ref
):
    ih = pl.program_id(0)
    low = low_lanes(B)
    y = at_ref[1]
    count = a_ref.shape[2]
    outs = (o0_ref, o1_ref, o2_ref, o3_ref)
    turn1 = lax.rem(y, 2) == 1
    turn2 = y >= 2

    def multiply(cc):
        lhs = chosen_blocks(idx_ref, dup_ref, low, (ih * 4 + 2) * NCOL + part * count + cc)
        return row_pair(lhs, a_ref[0, 0, cc], a_ref[0, 1, cc])

    def encode(cc, res):
        e, tile = coded_products(res)
        exp_ref[pl.ds(ih * 8 + cc, 1), :] = e
        for g in range(2):
            for sp in range(4):
                t = [tile(2 * k + g, sp) for k in range(4)]
                t = [jnp.where(turn1, t[(k + 1) % 4], t[k]) for k in range(4)]
                t = [jnp.where(turn2, t[(k + 2) % 4], t[k]) for k in range(4)]
                for d in range(4):
                    outs[d][((2 * g + ih) * 8 + cc) * 4 + sp] = t[d].astype(jnp.int16)

    pipelined(count, multiply, encode, r0_ref, r1_ref)

    @pl.when(ih == 1)
    def _():
        e = exp_ref[...].astype(jnp.int32).astype(jnp.int16)
        for o_ref in outs:
            o_ref[128] = e


def y_products(part, idx, at, a, dup):
    block = 8
    out = pl.BlockSpec((129, 16, 128), lambda ih, idx, at: (0, 0, 0))
    return pl.pallas_call(
        lambda *refs: y_product_kernel(part, *refs),
        grid_spec=pltpu.PrefetchScalarGridSpec(
            num_scalar_prefetch=2,
            grid=(2,),
            in_specs=[
                pl.BlockSpec(
                    (1, 2, block, B, KA * B), lambda ih, idx, at: (ih * 2 + 1, 0, part, 0, 0)
                ),
                pl.BlockSpec(memory_space=pltpu.VMEM),
            ],
            out_specs=[out] * 4,
            scratch_shapes=[pltpu.VMEM((NCOL, 128), jnp.float32)]
            + [pltpu.VMEM((KAP * B, 128), jnp.float32)] * 2,
        ),
        out_shape=[jax.ShapeDtypeStruct((129, 16, 128), jnp.int16)] * 4,
        compiler_params=pltpu.CompilerParams(vmem_limit_bytes=20 * 1024 * 1024),
    )(
        idx,
        at,
        pltpu.with_memory_space_constraint(a, pltpu.HBM),
        pltpu.with_memory_space_constraint(dup, pltpu.VMEM),
    )


def sum_and_code(tiles, out_ref, c):
    most = jnp.maximum(
        jnp.maximum(jnp.abs(tiles[0]), jnp.abs(tiles[1])),
        jnp.maximum(jnp.abs(tiles[2]), jnp.abs(tiles[3])),
    )
    e = exponent(jnp.max(most, axis=0, keepdims=True))
    mul = jnp.exp2(FULL - e)
    for sp in range(4):
        out_ref[c * 4 + sp] = coded(tiles[sp], mul)
    return e


def x_middle_kernel(at_ref, m0, m1, m2, m3, o0, o1, o2, o3, scale_ref, exp_ref):
    parts = (m0, m1, m2, m3)
    for d, m in enumerate(parts):
        scale_ref[d] = jnp.exp2(m[256].astype(jnp.float32) - FULL)
    for d2, out_ref in enumerate((o0, o1, o2, o3)):
        u = lax.rem(at_ref[1] + d2, 4)

        def one(c, carry):
            scales = [scale_ref[d, pl.ds(c, 1), :] for d in range(4)]
            tiles = []
            for sp in range(4):
                terms = [
                    m[(u * NCOL + c) * 4 + sp].astype(jnp.float32) * scale
                    for m, scale in zip(parts, scales)
                ]
                tiles.append((terms[0] + terms[1]) + (terms[2] + terms[3]))
            exp_ref[pl.ds(c, 1), :] = sum_and_code(tiles, out_ref, c)
            return carry

        lax.fori_loop(0, NCOL, one, 0, unroll=2)
        out_ref[64] = exp_ref[...].astype(jnp.int32).astype(jnp.int16)


def y_middle_kernel(at_ref, *refs):
    parts, outs, scale_ref, exp_ref = refs[:8], refs[8:12], refs[12], refs[13]
    for n, m in enumerate(parts):
        scale_ref[n] = jnp.exp2(m[128].astype(jnp.float32) - FULL)
    for d2, out_ref in enumerate(outs):
        u = lax.rem(at_ref[0] + d2, 4)
        ih = lax.rem(u, 2)
        for half in range(2):
            own = parts[half * 4:half * 4 + 4]

            def one(cc, carry):
                scales = [scale_ref[half * 4 + d, pl.ds(ih * 8 + cc, 1), :] for d in range(4)]
                tiles = []
                for sp in range(4):
                    terms = [
                        m[(u * 8 + cc) * 4 + sp].astype(jnp.float32) * scale
                        for m, scale in zip(own, scales)
                    ]
                    tiles.append((terms[0] + terms[1]) + (terms[2] + terms[3]))
                c = half * 8 + cc
                exp_ref[pl.ds(c, 1), :] = sum_and_code(tiles, out_ref, c)
                return carry

            lax.fori_loop(0, 8, one, 0, unroll=2)
        out_ref[64] = exp_ref[...].astype(jnp.int32).astype(jnp.int16)


def middle(kernel, at, parts):
    vmem = pl.BlockSpec(memory_space=pltpu.VMEM)
    return pl.pallas_call(
        kernel,
        in_specs=[pl.BlockSpec(memory_space=pltpu.SMEM)] + [vmem] * len(parts),
        out_specs=[vmem] * 4,
        scratch_shapes=[
            pltpu.VMEM((len(parts), NCOL, 128), jnp.float32),
            pltpu.VMEM((NCOL, 128), jnp.float32),
        ],
        out_shape=[jax.ShapeDtypeStruct((65, 16, 128), jnp.int16)] * 4,
    )(at, *parts)


def decode(parts, out_ref, scale_ref):
    for n, m in enumerate(parts):
        scale_ref[n] = jnp.exp2(m[64].astype(jnp.float32) - FULL)

    def one(c, carry):
        for qh in range(2):
            scales = [scale_ref[qh * 4 + d, pl.ds(c, 1), :] for d in range(4)]
            for sp in range(4):
                terms = [
                    parts[qh * 4 + d][c * 4 + sp].astype(jnp.float32) * scales[d] for d in range(4)
                ]
                total = (terms[0] + terms[1]) + (terms[2] + terms[3])
                out_ref[c, qh, sp * 16:(sp + 1) * 16, :] = total.astype(jnp.bfloat16)
        return carry

    lax.fori_loop(0, NCOL, one, 0)


def coarse_kernel(tgt_ref, at_ref, *refs):
    parts, (p0_ref, p1_ref, p2_ref, p3_ref) = refs[:8], refs[8:12]
    x_ref, keep_ref, send_ref, acc_ref, scale_ref = refs[12:]
    dx = pl.program_id(0)
    low = low_lanes(8)
    low_x = low_lanes(B)
    my_x, my_y, my_z, my_core = at_ref[0], at_ref[1], at_ref[2], at_ref[3]

    @pl.when(dx == 0)
    def _():
        acc_ref[...] = jnp.zeros_like(acc_ref)
        decode(parts, x_ref, scale_ref)

    for dy, p_ref in enumerate((p0_ref, p1_ref, p2_ref, p3_ref)):
        c = lax.rem(my_y - dy + 4, 4) * 4 + lax.rem(my_x - dx + 4, 4)
        for qh in range(2):
            x = x_ref[c, qh]
            none = jnp.zeros_like(x)
            lhs = jnp.concatenate([jnp.where(low_x, x, none), jnp.where(low_x, none, x)], axis=0)
            rhs = p_ref[0, qh * 2 * B:(qh + 1) * 2 * B, :]
            res = lax.dot_general(
                lhs, rhs, (((1,), (0,)), ((), ())), preferred_element_type=jnp.float32
            )
            for lo in range(2):
                ats, sums = [], []
                for m in range(KP):
                    for s in range(KAP):
                        at = tgt_ref[(((c * 2 + qh) * 2 + lo) * KP + m) * KAP + s]
                        rows = (lo * KAP + s) * 8
                        tile = res[rows:rows + 8, (m // 2) * 128:(m // 2) * 128 + 128]
                        keep = low if m % 2 == 0 else jnp.logical_not(low)
                        ats.append(at)
                        sums.append(acc_ref[at] + jnp.where(keep, tile, 0.0))
                for at, total in zip(ats, sums):
                    acc_ref[at] = total

    @pl.when(dx == 3)
    def _():
        for flip, out_ref in ((1, send_ref), (0, keep_ref)):
            core = lax.rem(my_core + flip, 2)
            for d in range(4):
                first = (lax.rem(my_z + d, 4) * 2 + core) * NCOL

                def fold(col, carry):
                    for tp in range(KC // 2):
                        t0 = acc_ref[(first + col) * KC + 2 * tp]
                        t1 = acc_ref[(first + col) * KC + 2 * tp + 1]
                        t0 = t0 + pltpu.roll(t0, B, 1)
                        t1 = t1 + pltpu.roll(t1, B, 1)
                        out_ref[d, col, tp] = jnp.where(low, t0, t1)
                    return carry

                lax.fori_loop(0, NCOL, fold, 0, unroll=4)


def coarse_terms(tgt, at, parts, ps):
    shape = (4, NCOL, KC // 2, 8, 128)
    out = pl.BlockSpec(shape, lambda dx, tgt, at: (0, 0, 0, 0, 0))
    return pl.pallas_call(
        coarse_kernel,
        grid_spec=pltpu.PrefetchScalarGridSpec(
            num_scalar_prefetch=2,
            grid=(4,),
            in_specs=[pl.BlockSpec((65, 16, 128), lambda dx, tgt, at: (0, 0, 0))] * 8
            + [pl.BlockSpec((1, 4 * B + 16, KP * B), lambda dx, tgt, at: (dx, 0, 0))] * 4,
            out_specs=[
                pl.BlockSpec((NCOL, 2, B, 128), lambda dx, tgt, at: (0, 0, 0, 0)), out, out
            ],
            scratch_shapes=[
                pltpu.VMEM((NCB * KC + 1, 8, 128), jnp.float32),
                pltpu.VMEM((8, NCOL, 128), jnp.float32),
            ],
        ),
        out_shape=[
            jax.ShapeDtypeStruct((NCOL, 2, B, 128), jnp.bfloat16),
            jax.ShapeDtypeStruct(shape, jnp.float32),
            jax.ShapeDtypeStruct(shape, jnp.float32),
        ],
        name="coarse_terms",
    )(tgt, at, *parts, *ps)


def ap_out_kernel(x_ref, out_ref, turn_ref):
    for ih in range(2):
        for qh in range(2):
            for s in range(KAP):
                m = jnp.concatenate(
                    [x_ref[bg * 2 + ih, qh, s * 8:(s + 1) * 8, :] for bg in range(8)], axis=0
                )
                t = m.astype(jnp.float32).T
                for lo in range(2):
                    top, bottom = t[lo * B:lo * B + 32], t[lo * B + 32:lo * B + B]
                    turn_ref[lo, pl.ds(s, 32, stride=8), :] = jnp.concatenate([top, bottom], axis=1)
            for lo in range(2):
                for h in range(32):
                    tile = turn_ref[lo, h * 8:(h + 1) * 8, :]
                    out_ref[ih * 4 + qh * 2 + lo, :, h * 128:(h + 1) * 128] = tile.astype(jnp.bfloat16)


def ap_layout(x):
    vmem = pl.BlockSpec(memory_space=pltpu.VMEM)
    return pl.pallas_call(
        ap_out_kernel,
        in_specs=[vmem],
        out_specs=vmem,
        scratch_shapes=[pltpu.VMEM((2, 256, 128), jnp.float32)],
        out_shape=jax.ShapeDtypeStruct((8, KAP, B * B), jnp.bfloat16),
        name="ap_layout",
    )(x)


def coarse_out_kernel(x_ref, out_ref, turn_ref, flat_ref):
    for tp in range(KC // 2):
        m = jnp.concatenate([x_ref[bg * 2, tp] + x_ref[bg * 2 + 1, tp] for bg in range(8)], axis=0)
        turn_ref[...] = m.T
        for lo in range(2):
            even = turn_ref[pl.ds(lo * B, 32, stride=2), :]
            odd = turn_ref[pl.ds(lo * B + 1, 32, stride=2), :]
            flat_ref[pl.ds(tp * 2 + lo, 32, stride=8), :] = jnp.concatenate([even, odd], axis=1)
    for h in range(32):
        out_ref[:, h * 128:(h + 1) * 128] = flat_ref[h * 8:(h + 1) * 8, :]


def coarse_layout(x):
    vmem = pl.BlockSpec(memory_space=pltpu.VMEM)
    return pl.pallas_call(
        coarse_out_kernel,
        in_specs=[vmem],
        out_specs=vmem,
        scratch_shapes=[pltpu.VMEM((128, B), jnp.float32), pltpu.VMEM((256, 128), jnp.float32)],
        out_shape=jax.ShapeDtypeStruct((KC, B * B), jnp.float32),
        name="coarse_layout",
    )(x)


def pick_rows(table, index):
    hot = (index[..., None] == jnp.arange(table.shape[0], dtype=jnp.int32)).astype(jnp.bfloat16)
    rows = jnp.einsum(
        "...k,km->...m", hot, table.astype(jnp.bfloat16), preferred_element_type=jnp.float32
    )
    return rows.astype(jnp.int32)


def index_slab(index):
    return jnp.pad(index.astype(jnp.bfloat16), ((0, 16 - index.shape[0]), (0, KP * B - KP)))


def step(a_blocks, a_index, p_blocks, p_index, ap_index, coarse_index):
    row = lax.axis_index("row")
    col = lax.axis_index("col")
    z, core = row // 2, row % 2
    y, x = col // 4, col % 4
    at = jnp.stack([x, y, z, core]).astype(jnp.int32)
    half = x % 2

    own = p_blocks[:, 0].reshape(8, KP, B, B)
    pt = own.transpose(0, 3, 1, 2).reshape(8 * B, KP * B)
    pt = jnp.concatenate([pt, index_slab(p_index[:, 0])], axis=0)
    by_z = [pt] + [along_row(pt, d, 0) for d in (1, 2, 3)]
    partner = along_row(pt, 0, 1)

    pn = own.reshape(8, KP, 32, 2, B).transpose(0, 3, 2, 1, 4).reshape(2, 4 * B, KP * B)
    halves = jnp.stack(
        [
            jnp.concatenate([pn[h], index_slab(p_index[4 * h:4 * h + 4, 0])], axis=0)
            for h in range(2)
        ]
    )
    *by_z, halves = lax.optimization_barrier((*by_z, halves))
    parts = [by_z[0], partner]
    for part in by_z[1:]:
        parts += [part, along_row(part, 0, 1)]
    same = lax.dynamic_index_in_dim(halves, half, 0, keepdims=False)
    diff = lax.dynamic_index_in_dim(halves, 1 - half, 0, keepdims=False)
    by_x = [same, along_col(diff, 1, 0), along_col(same, 2, 0), along_col(diff, 3, 0)]
    by_x = jnp.stack(by_x)
    ps = [by_x] + [along_col(by_x, 0, d) for d in (1, 2, 3)]

    a = spread(a_blocks[:, 0]).reshape(4, 2, NCOL, B, KA * B)

    a_idx = a_index[:, 0]
    from_row = a_idx // 8
    place = ((z - from_row // 2) % 4) * 2 + (core + from_row) % 2
    place = place * 8 + a_idx % 8
    dup, cols_k = table(parts)
    picked = pick_rows(cols_k[:, :KP], place)
    equal = picked[:, :, None, :] == ap_index[:, None, :, None]
    ids = place[:, :, None, None] * KP + jnp.arange(KP, dtype=jnp.int32)
    idx = jnp.min(jnp.where(equal, ids, NK * KP), axis=3).reshape(-1)

    cols_p = jnp.stack([p[:, 4 * B:4 * B + 4, :KP] for p in ps]).reshape(NCOL, 16)
    cc = jnp.arange(NCOL, dtype=jnp.int32)
    where = ((y - cc // 4) % 4) * 4 + (x - cc % 4) % 4
    cols_i = pick_rows(cols_p, where).reshape(NCOL, 4, KP)
    slots = lax.dynamic_index_in_dim(
        ap_index.reshape(2, 4, NCOL, KAP), half, 0, keepdims=False
    ).transpose(1, 0, 2)
    targets = pick_rows(coarse_index, cols_i)
    hit = targets[:, :, :, None, :] == slots[:, :, None, :, None]
    slot = cols_i[:, :, :, None, None] * KC + jnp.arange(KC, dtype=jnp.int32)
    tgt = jnp.min(jnp.where(hit, slot, NCB * KC), axis=4).reshape(-1)

    x1, x3 = x_products(1, idx, at, a, dup)
    got_x1, got_x3 = along_col(x1, 1, 0), along_col(x3, 3, 0)
    ya = y_products(0, idx, at, a, dup)
    got_ya = [along_col(ya[d], 0, d) for d in (1, 2, 3)]
    x0, x2 = x_products(0, idx, at, a, dup)
    got_x2 = along_col(x2, 2, 0)
    yb = y_products(1, idx, at, a, dup)
    got_yb = [along_col(yb[d], 0, d) for d in (1, 2, 3)]
    s0 = middle(x_middle_kernel, at, [x0, got_x1, got_x2, got_x3])
    y_last = [along_col(s0[d], 0, d) for d in (1, 2, 3)]
    s1 = middle(y_middle_kernel, at, [ya[0], *got_ya, yb[0], *got_yb])
    x_last = [along_col(s1[d], d, 0) for d in (1, 2, 3)]

    apt, keep, send = coarse_terms(tgt, at, [s0[0], *y_last, s1[0], *x_last], ps)
    got = along_row(send, 0, 1)
    sums = [keep[d] + got[d] for d in range(4)]
    coarse = sums[0]
    moved = [along_row(sums[d], d, 0) for d in (1, 2, 3)]
    for part in moved:
        coarse = coarse + part
    back = lax.all_to_all(apt, "col", 0, 0, tiled=True)
    ap_out = ap_layout(back).reshape(8, 1, KAP, B * B)
    coarse = lax.all_to_all(coarse, "col", 0, 0, tiled=True)
    coarse_out = coarse_layout(coarse).reshape(1, KC, B * B)
    return ap_out, coarse_out


def solution(mesh):
    placed = (
        P("row", "col", None, None),
        P("row", "col", None),
        P("row", "col", None, None),
        P("row", "col", None),
        P("row", None),
        P(),
    )
    return jax.shard_map(
        step,
        mesh=mesh,
        in_specs=placed,
        out_specs=(P("row", "col", None, None), P(("row", "col"), None, None)),
        check_vma=False,
    )
```

```python
import jax
import jax.numpy as jnp
from jax import lax
from jax.experimental import pallas as pl
from jax.experimental.pallas import tpu as pltpu
from jax.sharding import PartitionSpec as P


B = 64
KA = 4
KP = 4
KAP = 8
KC = 8
NCOL = 16
NK = 64
NCB = 128
FULL = 14.0
TINY = 1e-30


def along_row(v, dz, flip):
    pairs = [(r, ((r // 2 + dz) % 4) * 2 + (r % 2 + flip) % 2) for r in range(8)]
    return lax.ppermute(v, "row", pairs)


def along_col(v, dx, dy):
    pairs = [(c, ((c // 4 + dy) % 4) * 4 + (c % 4 + dx) % 4) for c in range(16)]
    return lax.ppermute(v, "col", pairs)


def low_lanes(rows):
    return lax.broadcasted_iota(jnp.int32, (rows, 128), 1) < B


def spread_kernel(a_ref, out_ref, buf_ref):
    low = low_lanes(32)

    def some(g, carry):
        for u in range(4):
            i = g * 4 + u
            v = a_ref[i].astype(jnp.float32)
            for h in range(32):
                buf_ref[u, h * 4:(h + 1) * 4, :] = v[:, h * 128:(h + 1) * 128]
        for u in range(4):
            i = g * 4 + u
            for ep in range(2):
                v0 = buf_ref[u, pl.ds(2 * ep, 32, stride=4), :]
                v1 = buf_ref[u, pl.ds(2 * ep + 1, 32, stride=4), :]
                top = jnp.where(low, v0, pltpu.roll(v1, B, 1))
                bottom = jnp.where(low, pltpu.roll(v0, B, 1), v1)
                out_ref[i, 0:32, ep * 128:(ep + 1) * 128] = top.astype(jnp.bfloat16)
                out_ref[i, 32:64, ep * 128:(ep + 1) * 128] = bottom.astype(jnp.bfloat16)
        return carry

    lax.fori_loop(0, 4, some, 0)


def spread(a):
    return pl.pallas_call(
        spread_kernel,
        grid=(8,),
        in_specs=[pl.BlockSpec((16, KA, B * B), lambda g: (g, 0, 0))],
        out_specs=pl.BlockSpec((16, B, KA * B), lambda g: (g, 0, 0)),
        scratch_shapes=[pltpu.VMEM((4, 128, 128), jnp.float32)],
        out_shape=pltpu.HBM((128, B, KA * B), jnp.bfloat16),
        name="spread",
        compiler_params=pltpu.CompilerParams(vmem_limit_bytes=8 * 1024 * 1024),
    )(pltpu.with_memory_space_constraint(a, pltpu.HBM))


def table_kernel(*refs):
    parts, out_ref, cols_ref = refs[:8], refs[8], refs[9]
    low = low_lanes(B)
    for n, part in enumerate(parts):
        cols_ref[n * 8:(n + 1) * 8, :] = part[8 * B:8 * B + 8, 0:128].astype(jnp.float32)

        def fill(q, carry):
            for mh in range(2):
                v = part[pl.ds(pl.multiple_of(q * B, B), B), mh * 128:(mh + 1) * 128]
                turned = jnp.concatenate([v[:, B:], v[:, :B]], axis=1)
                at = (n * 8 + q) * 4 + 2 * mh
                out_ref[at] = jnp.where(low, v, turned)
                out_ref[at + 1] = jnp.where(low, turned, v)
            return carry

        lax.fori_loop(0, 8, fill, 0, unroll=2)
    out_ref[NK * KP] = jnp.zeros((B, 128), jnp.bfloat16)


def table(parts):
    whole = pl.BlockSpec(memory_space=pltpu.VMEM)
    return pl.pallas_call(
        table_kernel,
        in_specs=[whole] * 8,
        out_specs=[whole, whole],
        out_shape=[
            pltpu.HBM((NK * KP + 1, B, 128), jnp.bfloat16),
            jax.ShapeDtypeStruct((NK, 128), jnp.float32),
        ],
        name="table",
        compiler_params=pltpu.CompilerParams(vmem_limit_bytes=12 * 1024 * 1024),
    )(*parts)


def nt_dot(a, b):
    return lax.dot_general(a, b, (((1,), (1,)), ((), ())), preferred_element_type=jnp.float32)


def exponent(most):
    return jnp.ceil(jnp.log2(jnp.maximum(most, TINY)))


def coded(v, mul):
    return jnp.round(v * mul).astype(jnp.int32).astype(jnp.int16)


def row_pair(lhs, rhs_top, rhs_bottom):
    zero = jnp.zeros((B, KA * B), jnp.bfloat16)
    stacked = jnp.concatenate(
        [
            jnp.concatenate([rhs_top, zero], axis=1),
            jnp.concatenate([zero, rhs_bottom], axis=1),
        ],
        axis=0,
    )
    return nt_dot(lhs, stacked)


def chosen_blocks(idx_ref, dup_ref, low, first_row):
    rows = []
    for s in range(KAP):
        pieces = []
        for lo in range(2):
            base = (first_row + lo * NCOL) * (KA * KAP)
            for ep in range(2):
                first = dup_ref[idx_ref[base + (2 * ep) * KAP + s]]
                second = dup_ref[idx_ref[base + (2 * ep + 1) * KAP + s]]
                pieces.append(jnp.where(low, first, second))
        rows.append(jnp.concatenate(pieces, axis=1))
    return jnp.concatenate(rows, axis=0)


def coded_products(res):
    e = exponent(jnp.max(jnp.abs(res), axis=0, keepdims=True))
    q = jnp.round(res * jnp.exp2(FULL - e)).astype(jnp.int32)

    def tile(bg, sp):
        r0 = 2 * sp * B + bg * 8
        return jnp.concatenate([q[r0:r0 + 8], q[r0 + B:r0 + B + 8]], axis=0)

    return e, tile


def pipelined(count, multiply, encode, r0_ref, r1_ref):
    r1_ref[...] = jnp.zeros_like(r1_ref)

    def two(k, carry):
        r0_ref[...] = multiply(2 * k)
        encode(jnp.maximum(2 * k - 1, 0), r1_ref[...])
        r1_ref[...] = multiply(2 * k + 1)
        encode(2 * k, r0_ref[...])
        return carry

    lax.fori_loop(0, count // 2, two, 0)
    encode(count - 1, r1_ref[...])


def x_product_kernel(
    j, idx_ref, at_ref, a_ref, dup_ref, near_ref, far_ref, exp_ref, r0_ref, r1_ref
):
    cblk = pl.program_id(0)
    low = low_lanes(B)
    goal = lax.rem(at_ref[0] + j, 4)
    ih = lax.rem(goal, 2)
    count = a_ref.shape[2]
    is_low = goal < 2

    def multiply(cc):
        lhs = chosen_blocks(idx_ref, dup_ref, low, ih * 4 * NCOL + cblk * count + cc)
        return row_pair(lhs, a_ref[0, 0, cc], a_ref[0, 1, cc])

    def encode(cc, res):
        c = cblk * count + cc
        e, tile = coded_products(res)
        exp_ref[pl.ds(c, 1), :] = e
        for u in range(4):
            for sp in range(4):
                t0, t1 = tile(2 * u, sp), tile(2 * u + 1, sp)
                at = (u * NCOL + c) * 4 + sp
                near_ref[at] = jnp.where(is_low, t0, t1).astype(jnp.int16)
                far_ref[at] = jnp.where(is_low, t1, t0).astype(jnp.int16)

    pipelined(count, multiply, encode, r0_ref, r1_ref)

    @pl.when(cblk == pl.num_programs(0) - 1)
    def _():
        e = exp_ref[...].astype(jnp.int32).astype(jnp.int16)
        near_ref[256] = e
        far_ref[256] = e


def x_products(j, idx, at, a, dup):
    block = 8
    out = pl.BlockSpec((257, 16, 128), lambda c, idx, at: (0, 0, 0))
    return pl.pallas_call(
        lambda *refs: x_product_kernel(j, *refs),
        grid_spec=pltpu.PrefetchScalarGridSpec(
            num_scalar_prefetch=2,
            grid=(NCOL // block,),
            in_specs=[
                pl.BlockSpec(
                    (1, 2, block, B, KA * B),
                    lambda c, idx, at: (lax.rem(at[0] + j, 2) * 2, 0, c, 0, 0),
                ),
                pl.BlockSpec(memory_space=pltpu.VMEM),
            ],
            out_specs=[out, out],
            scratch_shapes=[pltpu.VMEM((NCOL, 128), jnp.float32)]
            + [pltpu.VMEM((KAP * B, 128), jnp.float32)] * 2,
        ),
        out_shape=[
            (pltpu.HBM if j == 0 else jax.ShapeDtypeStruct)((257, 16, 128), jnp.int16),
            jax.ShapeDtypeStruct((257, 16, 128), jnp.int16),
        ],
        compiler_params=pltpu.CompilerParams(vmem_limit_bytes=20 * 1024 * 1024),
    )(
        idx,
        at,
        pltpu.with_memory_space_constraint(a, pltpu.HBM),
        pltpu.with_memory_space_constraint(dup, pltpu.VMEM),
    )


def y_product_kernel(
    part, idx_ref, at_ref, a_ref, dup_ref, o0_ref, o1_ref, o2_ref, o3_ref, exp_ref, r0_ref, r1_ref
):
    ih = pl.program_id(0)
    low = low_lanes(B)
    y = at_ref[1]
    count = a_ref.shape[2]
    outs = (o0_ref, o1_ref, o2_ref, o3_ref)
    turn1 = lax.rem(y, 2) == 1
    turn2 = y >= 2

    def multiply(cc):
        lhs = chosen_blocks(idx_ref, dup_ref, low, (ih * 4 + 2) * NCOL + part * count + cc)
        return row_pair(lhs, a_ref[0, 0, cc], a_ref[0, 1, cc])

    def encode(cc, res):
        e, tile = coded_products(res)
        exp_ref[pl.ds(ih * 8 + cc, 1), :] = e
        for g in range(2):
            for sp in range(4):
                t = [tile(2 * k + g, sp) for k in range(4)]
                t = [jnp.where(turn1, t[(k + 1) % 4], t[k]) for k in range(4)]
                t = [jnp.where(turn2, t[(k + 2) % 4], t[k]) for k in range(4)]
                for d in range(4):
                    outs[d][((2 * g + ih) * 8 + cc) * 4 + sp] = t[d].astype(jnp.int16)

    pipelined(count, multiply, encode, r0_ref, r1_ref)

    @pl.when(ih == 1)
    def _():
        e = exp_ref[...].astype(jnp.int32).astype(jnp.int16)
        for o_ref in outs:
            o_ref[128] = e


def y_products(part, idx, at, a, dup):
    block = 8
    out = pl.BlockSpec((129, 16, 128), lambda ih, idx, at: (0, 0, 0))
    return pl.pallas_call(
        lambda *refs: y_product_kernel(part, *refs),
        grid_spec=pltpu.PrefetchScalarGridSpec(
            num_scalar_prefetch=2,
            grid=(2,),
            in_specs=[
                pl.BlockSpec(
                    (1, 2, block, B, KA * B), lambda ih, idx, at: (ih * 2 + 1, 0, part, 0, 0)
                ),
                pl.BlockSpec(memory_space=pltpu.VMEM),
            ],
            out_specs=[out] * 4,
            scratch_shapes=[pltpu.VMEM((NCOL, 128), jnp.float32)]
            + [pltpu.VMEM((KAP * B, 128), jnp.float32)] * 2,
        ),
        out_shape=[pltpu.HBM((129, 16, 128), jnp.int16)]
        + [jax.ShapeDtypeStruct((129, 16, 128), jnp.int16)] * 3,
        compiler_params=pltpu.CompilerParams(vmem_limit_bytes=20 * 1024 * 1024),
    )(
        idx,
        at,
        pltpu.with_memory_space_constraint(a, pltpu.HBM),
        pltpu.with_memory_space_constraint(dup, pltpu.VMEM),
    )


def sum_and_code(tiles, out_ref, c):
    most = jnp.maximum(
        jnp.maximum(jnp.abs(tiles[0]), jnp.abs(tiles[1])),
        jnp.maximum(jnp.abs(tiles[2]), jnp.abs(tiles[3])),
    )
    e = exponent(jnp.max(most, axis=0, keepdims=True))
    mul = jnp.exp2(FULL - e)
    for sp in range(4):
        out_ref[c * 4 + sp] = coded(tiles[sp], mul)
    return e


def x_middle_kernel(at_ref, m0, m1, m2, m3, o0, o1, o2, o3, scale_ref, exp_ref):
    parts = (m0, m1, m2, m3)
    for d, m in enumerate(parts):
        scale_ref[d] = jnp.exp2(m[256].astype(jnp.float32) - FULL)
    for d2, out_ref in enumerate((o0, o1, o2, o3)):
        u = lax.rem(at_ref[1] + d2, 4)

        def one(c, carry):
            scales = [scale_ref[d, pl.ds(c, 1), :] for d in range(4)]
            tiles = []
            for sp in range(4):
                terms = [
                    m[(u * NCOL + c) * 4 + sp].astype(jnp.float32) * scale
                    for m, scale in zip(parts, scales)
                ]
                tiles.append((terms[0] + terms[1]) + (terms[2] + terms[3]))
            exp_ref[pl.ds(c, 1), :] = sum_and_code(tiles, out_ref, c)
            return carry

        lax.fori_loop(0, NCOL, one, 0, unroll=2)
        out_ref[64] = exp_ref[...].astype(jnp.int32).astype(jnp.int16)


def y_middle_kernel(at_ref, *refs):
    parts, outs, scale_ref, exp_ref = refs[:8], refs[8:12], refs[12], refs[13]
    for n, m in enumerate(parts):
        scale_ref[n] = jnp.exp2(m[128].astype(jnp.float32) - FULL)
    for d2, out_ref in enumerate(outs):
        u = lax.rem(at_ref[0] + d2, 4)
        ih = lax.rem(u, 2)
        for half in range(2):
            own = parts[half * 4:half * 4 + 4]

            def one(cc, carry):
                scales = [scale_ref[half * 4 + d, pl.ds(ih * 8 + cc, 1), :] for d in range(4)]
                tiles = []
                for sp in range(4):
                    terms = [
                        m[(u * 8 + cc) * 4 + sp].astype(jnp.float32) * scale
                        for m, scale in zip(own, scales)
                    ]
                    tiles.append((terms[0] + terms[1]) + (terms[2] + terms[3]))
                c = half * 8 + cc
                exp_ref[pl.ds(c, 1), :] = sum_and_code(tiles, out_ref, c)
                return carry

            lax.fori_loop(0, 8, one, 0, unroll=2)
        out_ref[64] = exp_ref[...].astype(jnp.int32).astype(jnp.int16)


def middle(kernel, at, parts):
    vmem = pl.BlockSpec(memory_space=pltpu.VMEM)
    return pl.pallas_call(
        kernel,
        in_specs=[pl.BlockSpec(memory_space=pltpu.SMEM)] + [vmem] * len(parts),
        out_specs=[vmem] * 4,
        scratch_shapes=[
            pltpu.VMEM((len(parts), NCOL, 128), jnp.float32),
            pltpu.VMEM((NCOL, 128), jnp.float32),
        ],
        out_shape=[jax.ShapeDtypeStruct((65, 16, 128), jnp.int16)] * 4,
    )(at, *parts)


def decode(parts, out_ref, scale_ref):
    for n, m in enumerate(parts):
        scale_ref[n] = jnp.exp2(m[64].astype(jnp.float32) - FULL)

    def one(c, carry):
        for qh in range(2):
            scales = [scale_ref[qh * 4 + d, pl.ds(c, 1), :] for d in range(4)]
            for sp in range(4):
                terms = [
                    parts[qh * 4 + d][c * 4 + sp].astype(jnp.float32) * scales[d] for d in range(4)
                ]
                total = (terms[0] + terms[1]) + (terms[2] + terms[3])
                row = qh * B + sp * 16
                out_ref[c, row:row + 16, :] = total.astype(jnp.bfloat16)
        return carry

    lax.fori_loop(0, NCOL, one, 0)


def coarse_kernel(tgt_ref, at_ref, *refs):
    parts, (p0_ref, p1_ref, p2_ref, p3_ref) = refs[:8], refs[8:12]
    x_ref, keep_ref, send_ref, acc_ref, scale_ref = refs[12:]
    dy = pl.program_id(0)
    low = low_lanes(8)
    low_x = low_lanes(B)
    my_x, my_y, my_z, my_core = at_ref[0], at_ref[1], at_ref[2], at_ref[3]

    @pl.when(dy == 0)
    def _():
        acc_ref[...] = jnp.zeros_like(acc_ref)
        decode(parts, x_ref, scale_ref)

    for dx, p_ref in enumerate((p0_ref, p1_ref, p2_ref, p3_ref)):
        c = lax.rem(my_y - dy + 4, 4) * 4 + lax.rem(my_x - dx + 4, 4)
        for qh in range(2):
            x = x_ref[c, qh * B:(qh + 1) * B, :]
            none = jnp.zeros_like(x)
            lhs = jnp.concatenate([jnp.where(low_x, x, none), jnp.where(low_x, none, x)], axis=0)
            rhs = p_ref[0, qh * 2 * B:(qh + 1) * 2 * B, :]
            res = lax.dot_general(
                lhs, rhs, (((1,), (0,)), ((), ())), preferred_element_type=jnp.float32
            )
            for lo in range(2):
                ats, sums = [], []
                for m in range(KP):
                    for s in range(KAP):
                        at = tgt_ref[(((c * 2 + qh) * 2 + lo) * KP + m) * KAP + s]
                        rows = (lo * KAP + s) * 8
                        tile = res[rows:rows + 8, (m // 2) * 128:(m // 2) * 128 + 128]
                        keep = low if m % 2 == 0 else jnp.logical_not(low)
                        ats.append(at)
                        sums.append(acc_ref[at] + jnp.where(keep, tile, 0.0))
                for at, total in zip(ats, sums):
                    acc_ref[at] = total

    @pl.when(dy == 3)
    def _():
        for flip, out_ref in ((1, send_ref), (0, keep_ref)):
            core = lax.rem(my_core + flip, 2)
            for d in range(4):
                first = (lax.rem(my_z + d, 4) * 2 + core) * NCOL

                def fold(col, carry):
                    for tp in range(KC // 2):
                        t0 = acc_ref[(first + col) * KC + 2 * tp]
                        t1 = acc_ref[(first + col) * KC + 2 * tp + 1]
                        t0 = t0 + pltpu.roll(t0, B, 1)
                        t1 = t1 + pltpu.roll(t1, B, 1)
                        out_ref[d, col, tp] = jnp.where(low, t0, t1)
                    return carry

                lax.fori_loop(0, NCOL, fold, 0, unroll=4)


def coarse_terms(tgt, at, parts, ps):
    shape = (4, NCOL, KC // 2, 8, 128)
    out = pl.BlockSpec(shape, lambda dx, tgt, at: (0, 0, 0, 0, 0))
    return pl.pallas_call(
        coarse_kernel,
        grid_spec=pltpu.PrefetchScalarGridSpec(
            num_scalar_prefetch=2,
            grid=(4,),
            in_specs=[pl.BlockSpec((65, 16, 128), lambda dx, tgt, at: (0, 0, 0))] * 8
            + [pl.BlockSpec((1, 4 * B + 16, KP * B), lambda dx, tgt, at: (dx, 0, 0))] * 4,
            out_specs=[
                pl.BlockSpec((NCOL, 3 * B, 128), lambda dx, tgt, at: (0, 0, 0)), out, out
            ],
            scratch_shapes=[
                pltpu.VMEM((NCB * KC + 1, 8, 128), jnp.float32),
                pltpu.VMEM((8, NCOL, 128), jnp.float32),
            ],
        ),
        out_shape=[
            jax.ShapeDtypeStruct((NCOL, 3 * B, 128), jnp.bfloat16),
            jax.ShapeDtypeStruct(shape, jnp.float32),
            jax.ShapeDtypeStruct(shape, jnp.float32),
        ],
        name="coarse_terms",
    )(tgt, at, *parts, *ps)


def layout_kernel(x_ref, ap_ref, coarse_ref, turn_ref, wide_ref, flat_ref):
    for tp in range(KC // 2):
        rows = []
        for bg in range(8):
            total = None
            for ih in range(2):
                for part in range(2):
                    r0 = 2 * B + part * 32 + tp * 8
                    term = x_ref[bg * 2 + ih, r0:r0 + 8, :].astype(jnp.float32)
                    total = term if total is None else total + term
            rows.append(total)
        wide_ref[...] = jnp.concatenate(rows, axis=0).T
        for lo in range(2):
            even = wide_ref[pl.ds(lo * B, 32, stride=2), :]
            odd = wide_ref[pl.ds(lo * B + 1, 32, stride=2), :]
            flat_ref[pl.ds(tp * 2 + lo, 32, stride=8), :] = jnp.concatenate([even, odd], axis=1)
    for h in range(32):
        coarse_ref[:, h * 128:(h + 1) * 128] = flat_ref[h * 8:(h + 1) * 8, :]
    for ih in range(2):
        for qh in range(2):
            for s in range(KAP):
                r0 = qh * B + s * 8
                m = jnp.concatenate(
                    [x_ref[bg * 2 + ih, r0:r0 + 8, :] for bg in range(8)], axis=0
                )
                t = m.astype(jnp.float32).T
                for lo in range(2):
                    top, bottom = t[lo * B:lo * B + 32], t[lo * B + 32:lo * B + B]
                    turn_ref[lo, pl.ds(s, 32, stride=8), :] = jnp.concatenate([top, bottom], axis=1)
            for lo in range(2):
                for h in range(32):
                    tile = turn_ref[lo, h * 8:(h + 1) * 8, :]
                    ap_ref[ih * 4 + qh * 2 + lo, :, h * 128:(h + 1) * 128] = tile.astype(jnp.bfloat16)


def layout(x):
    vmem = pl.BlockSpec(memory_space=pltpu.VMEM)
    return pl.pallas_call(
        layout_kernel,
        in_specs=[vmem],
        out_specs=[vmem, vmem],
        scratch_shapes=[
            pltpu.VMEM((2, 256, 128), jnp.float32),
            pltpu.VMEM((128, B), jnp.float32),
            pltpu.VMEM((256, 128), jnp.float32),
        ],
        out_shape=[
            jax.ShapeDtypeStruct((8, KAP, B * B), jnp.bfloat16),
            jax.ShapeDtypeStruct((KC, B * B), jnp.float32),
        ],
        name="layout",
    )(x)


def pick_rows(table, index):
    hot = (index[..., None] == jnp.arange(table.shape[0], dtype=jnp.int32)).astype(jnp.bfloat16)
    rows = jnp.einsum(
        "...k,km->...m", hot, table.astype(jnp.bfloat16), preferred_element_type=jnp.float32
    )
    return rows.astype(jnp.int32)


def index_slab(index):
    return jnp.pad(index.astype(jnp.bfloat16), ((0, 16 - index.shape[0]), (0, KP * B - KP)))


def step(a_blocks, a_index, p_blocks, p_index, ap_index, coarse_index):
    row = lax.axis_index("row")
    col = lax.axis_index("col")
    z, core = row // 2, row % 2
    y, x = col // 4, col % 4
    at = jnp.stack([x, y, z, core]).astype(jnp.int32)
    half = x % 2

    own = p_blocks[:, 0].reshape(8, KP, B, B)
    pt = own.transpose(0, 3, 1, 2).reshape(8 * B, KP * B)
    pt = jnp.concatenate([pt, index_slab(p_index[:, 0])], axis=0)
    by_z = [pt] + [along_row(pt, d, 0) for d in (1, 2, 3)]
    partner = along_row(pt, 0, 1)

    pn = own.reshape(8, KP, 32, 2, B).transpose(0, 3, 2, 1, 4).reshape(2, 4 * B, KP * B)
    halves = jnp.stack(
        [
            jnp.concatenate([pn[h], index_slab(p_index[4 * h:4 * h + 4, 0])], axis=0)
            for h in range(2)
        ]
    )
    *by_z, halves = lax.optimization_barrier((*by_z, halves))
    parts = [by_z[0], partner]
    for part in by_z[1:]:
        parts += [part, along_row(part, 0, 1)]
    by_y = [halves] + [along_col(halves, 0, d) for d in (1, 2, 3)]

    a = spread(a_blocks[:, 0]).reshape(4, 2, NCOL, B, KA * B)

    a_idx = a_index[:, 0]
    from_row = a_idx // 8
    place = ((z - from_row // 2) % 4) * 2 + (core + from_row) % 2
    place = place * 8 + a_idx % 8
    dup, cols_k = table(parts)
    picked = pick_rows(cols_k[:, :KP], place)
    equal = picked[:, :, None, :] == ap_index[:, None, :, None]
    ids = place[:, :, None, None] * KP + jnp.arange(KP, dtype=jnp.int32)
    idx = jnp.min(jnp.where(equal, ids, NK * KP), axis=3).reshape(-1)

    x1, x3 = x_products(1, idx, at, a, dup)
    got_x1, got_x3 = along_col(x1, 1, 0), along_col(x3, 3, 0)
    ya = y_products(0, idx, at, a, dup)
    got_ya = [along_col(ya[d], 0, d) for d in (1, 2, 3)]
    x0, x2 = x_products(0, idx, at, a, dup)
    got_x2 = along_col(x2, 2, 0)
    yb = y_products(1, idx, at, a, dup)
    got_yb = [along_col(yb[d], 0, d) for d in (1, 2, 3)]
    s0 = middle(x_middle_kernel, at, [x0, got_x1, got_x2, got_x3])
    y_last = [along_col(s0[d], 0, d) for d in (1, 2, 3)]
    s1 = middle(y_middle_kernel, at, [ya[0], *got_ya, yb[0], *got_yb])
    x_last = [along_col(s1[d], d, 0) for d in (1, 2, 3)]

    by_y = jnp.stack(by_y)
    same = lax.dynamic_index_in_dim(by_y, half, 1, keepdims=False)
    diff = lax.dynamic_index_in_dim(by_y, 1 - half, 1, keepdims=False)
    ps = [same, along_col(diff, 1, 0), along_col(same, 2, 0), along_col(diff, 3, 0)]

    cols_p = jnp.stack([p[:, 4 * B:4 * B + 4, :KP] for p in ps]).reshape(NCOL, 16)
    cc = jnp.arange(NCOL, dtype=jnp.int32)
    where = ((x - cc % 4) % 4) * 4 + (y - cc // 4) % 4
    cols_i = pick_rows(cols_p, where).reshape(NCOL, 4, KP)
    slots = lax.dynamic_index_in_dim(
        ap_index.reshape(2, 4, NCOL, KAP), half, 0, keepdims=False
    ).transpose(1, 0, 2)
    targets = pick_rows(coarse_index, cols_i)
    hit = targets[:, :, :, None, :] == slots[:, :, None, :, None]
    slot = cols_i[:, :, :, None, None] * KC + jnp.arange(KC, dtype=jnp.int32)
    tgt = jnp.min(jnp.where(hit, slot, NCB * KC), axis=4).reshape(-1)

    apt, keep, send = coarse_terms(tgt, at, [s0[0], *y_last, s1[0], *x_last], ps)
    got = along_row(send, 0, 1)
    sums = [keep[d] + got[d] for d in range(4)]
    coarse = sums[0]
    moved = [along_row(sums[d], d, 0) for d in (1, 2, 3)]
    for part in moved:
        coarse = coarse + part
    high = lax.reduce_precision(coarse, exponent_bits=8, mantissa_bits=7)
    pair = jnp.concatenate(
        [v.astype(jnp.bfloat16).reshape(NCOL, 32, 128) for v in (high, coarse - high)], axis=1
    )
    both = lax.dynamic_update_slice(apt, pair, (0, 2 * B, 0))
    both = lax.all_to_all(both, "col", 0, 0, tiled=True)
    ap_out, coarse_out = layout(both)
    ap_out = ap_out.reshape(8, 1, KAP, B * B)
    coarse_out = coarse_out.reshape(1, KC, B * B)
    return ap_out, coarse_out


def solution(mesh):
    placed = (
        P("row", "col", None, None),
        P("row", "col", None),
        P("row", "col", None, None),
        P("row", "col", None),
        P("row", None),
        P(),
    )
    return jax.shard_map(
        step,
        mesh=mesh,
        in_specs=placed,
        out_specs=(P("row", "col", None, None), P(("row", "col"), None, None)),
        check_vma=False,
    )
```

```python
import jax
import jax.numpy as jnp
from jax import lax
from jax.experimental import pallas as pl
from jax.experimental.pallas import tpu as pltpu
from jax.sharding import PartitionSpec as P


B = 64
KA = 4
KP = 4
KAP = 8
KC = 8
NCOL = 16
NK = 64
NCB = 128
FULL = 14.0
TINY = 1e-30


def along_row(v, dz, flip):
    pairs = [(r, ((r // 2 + dz) % 4) * 2 + (r % 2 + flip) % 2) for r in range(8)]
    return lax.ppermute(v, "row", pairs)


def along_col(v, dx, dy):
    pairs = [(c, ((c // 4 + dy) % 4) * 4 + (c % 4 + dx) % 4) for c in range(16)]
    return lax.ppermute(v, "col", pairs)


def low_lanes(rows):
    return lax.broadcasted_iota(jnp.int32, (rows, 128), 1) < B


def spread_kernel(a_ref, out_ref, buf_ref):
    low = low_lanes(32)

    def some(g, carry):
        for u in range(4):
            i = g * 4 + u
            v = a_ref[i].astype(jnp.float32)
            for h in range(32):
                buf_ref[u, h * 4:(h + 1) * 4, :] = v[:, h * 128:(h + 1) * 128]
        for u in range(4):
            i = g * 4 + u
            for ep in range(2):
                v0 = buf_ref[u, pl.ds(2 * ep, 32, stride=4), :]
                v1 = buf_ref[u, pl.ds(2 * ep + 1, 32, stride=4), :]
                top = jnp.where(low, v0, pltpu.roll(v1, B, 1))
                bottom = jnp.where(low, pltpu.roll(v0, B, 1), v1)
                out_ref[i, 0:32, ep * 128:(ep + 1) * 128] = top.astype(jnp.bfloat16)
                out_ref[i, 32:64, ep * 128:(ep + 1) * 128] = bottom.astype(jnp.bfloat16)
        return carry

    lax.fori_loop(0, 4, some, 0)


def spread(a):
    return pl.pallas_call(
        spread_kernel,
        grid=(8,),
        in_specs=[pl.BlockSpec((16, KA, B * B), lambda g: (g, 0, 0))],
        out_specs=pl.BlockSpec((16, B, KA * B), lambda g: (g, 0, 0)),
        scratch_shapes=[pltpu.VMEM((4, 128, 128), jnp.float32)],
        out_shape=pltpu.HBM((128, B, KA * B), jnp.bfloat16),
        name="spread",
        compiler_params=pltpu.CompilerParams(vmem_limit_bytes=8 * 1024 * 1024),
    )(pltpu.with_memory_space_constraint(a, pltpu.HBM))


def table_kernel(*refs):
    parts, out_ref, cols_ref = refs[:8], refs[8], refs[9]
    low = low_lanes(B)
    for n, part in enumerate(parts):
        cols_ref[n * 8:(n + 1) * 8, :] = part[8 * B:8 * B + 8, 0:128].astype(jnp.float32)

        def fill(q, carry):
            for mh in range(2):
                v = part[pl.ds(pl.multiple_of(q * B, B), B), mh * 128:(mh + 1) * 128]
                turned = jnp.concatenate([v[:, B:], v[:, :B]], axis=1)
                at = (n * 8 + q) * 4 + 2 * mh
                out_ref[at] = jnp.where(low, v, turned)
                out_ref[at + 1] = jnp.where(low, turned, v)
            return carry

        lax.fori_loop(0, 8, fill, 0, unroll=2)
    out_ref[NK * KP] = jnp.zeros((B, 128), jnp.bfloat16)


def table(parts):
    whole = pl.BlockSpec(memory_space=pltpu.VMEM)
    return pl.pallas_call(
        table_kernel,
        in_specs=[whole] * 8,
        out_specs=[whole, whole],
        out_shape=[
            pltpu.HBM((NK * KP + 1, B, 128), jnp.bfloat16),
            jax.ShapeDtypeStruct((NK, 128), jnp.float32),
        ],
        name="table",
        compiler_params=pltpu.CompilerParams(vmem_limit_bytes=12 * 1024 * 1024),
    )(*parts)


def nt_dot(a, b):
    return lax.dot_general(a, b, (((1,), (1,)), ((), ())), preferred_element_type=jnp.float32)


def exponent(most):
    return jnp.ceil(jnp.log2(jnp.maximum(most, TINY)))


def coded(v, mul):
    return jnp.round(v * mul).astype(jnp.int32).astype(jnp.int16)


def row_pair(lhs, rhs_top, rhs_bottom):
    zero = jnp.zeros((B, KA * B), jnp.bfloat16)
    stacked = jnp.concatenate(
        [
            jnp.concatenate([rhs_top, zero], axis=1),
            jnp.concatenate([zero, rhs_bottom], axis=1),
        ],
        axis=0,
    )
    return nt_dot(lhs, stacked)


def chosen_blocks(idx_ref, dup_ref, low, first_row):
    rows = []
    for s in range(KAP):
        pieces = []
        for lo in range(2):
            base = (first_row + lo * NCOL) * (KA * KAP)
            for ep in range(2):
                first = dup_ref[idx_ref[base + (2 * ep) * KAP + s]]
                second = dup_ref[idx_ref[base + (2 * ep + 1) * KAP + s]]
                pieces.append(jnp.where(low, first, second))
        rows.append(jnp.concatenate(pieces, axis=1))
    return jnp.concatenate(rows, axis=0)


def coded_products(res):
    e = exponent(jnp.max(jnp.abs(res), axis=0, keepdims=True))
    q = jnp.round(res * jnp.exp2(FULL - e)).astype(jnp.int32)

    def tile(bg, sp):
        r0 = 2 * sp * B + bg * 8
        return jnp.concatenate([q[r0:r0 + 8], q[r0 + B:r0 + B + 8]], axis=0)

    return e, tile


def pipelined(count, multiply, encode, r0_ref, r1_ref):
    r1_ref[...] = jnp.zeros_like(r1_ref)

    def two(k, carry):
        r0_ref[...] = multiply(2 * k)
        encode(jnp.maximum(2 * k - 1, 0), r1_ref[...])
        r1_ref[...] = multiply(2 * k + 1)
        encode(2 * k, r0_ref[...])
        return carry

    lax.fori_loop(0, count // 2, two, 0)
    encode(count - 1, r1_ref[...])


def x_product_kernel(
    j, idx_ref, at_ref, a_ref, dup_ref, near_ref, far_ref, exp_ref, r0_ref, r1_ref
):
    cblk = pl.program_id(0)
    low = low_lanes(B)
    goal = lax.rem(at_ref[0] + j, 4)
    ih = lax.rem(goal, 2)
    count = a_ref.shape[2]
    is_low = goal < 2

    def multiply(cc):
        lhs = chosen_blocks(idx_ref, dup_ref, low, ih * 4 * NCOL + cblk * count + cc)
        return row_pair(lhs, a_ref[0, 0, cc], a_ref[0, 1, cc])

    def encode(cc, res):
        c = cblk * count + cc
        e, tile = coded_products(res)
        exp_ref[pl.ds(c, 1), :] = e
        for u in range(4):
            for sp in range(4):
                t0, t1 = tile(2 * u, sp), tile(2 * u + 1, sp)
                at = (u * NCOL + c) * 4 + sp
                near_ref[at] = jnp.where(is_low, t0, t1).astype(jnp.int16)
                far_ref[at] = jnp.where(is_low, t1, t0).astype(jnp.int16)

    pipelined(count, multiply, encode, r0_ref, r1_ref)

    @pl.when(cblk == pl.num_programs(0) - 1)
    def _():
        e = exp_ref[...].astype(jnp.int32).astype(jnp.int16)
        near_ref[256] = e
        far_ref[256] = e


def x_products(j, idx, at, a, dup):
    block = 8
    out = pl.BlockSpec((257, 16, 128), lambda c, idx, at: (0, 0, 0))
    return pl.pallas_call(
        lambda *refs: x_product_kernel(j, *refs),
        grid_spec=pltpu.PrefetchScalarGridSpec(
            num_scalar_prefetch=2,
            grid=(NCOL // block,),
            in_specs=[
                pl.BlockSpec(
                    (1, 2, block, B, KA * B),
                    lambda c, idx, at: (lax.rem(at[0] + j, 2) * 2, 0, c, 0, 0),
                ),
                pl.BlockSpec(memory_space=pltpu.VMEM),
            ],
            out_specs=[out, out],
            scratch_shapes=[pltpu.VMEM((NCOL, 128), jnp.float32)]
            + [pltpu.VMEM((KAP * B, 128), jnp.float32)] * 2,
        ),
        out_shape=[
            (pltpu.HBM if j == 0 else jax.ShapeDtypeStruct)((257, 16, 128), jnp.int16),
            jax.ShapeDtypeStruct((257, 16, 128), jnp.int16),
        ],
        compiler_params=pltpu.CompilerParams(vmem_limit_bytes=20 * 1024 * 1024),
    )(
        idx,
        at,
        pltpu.with_memory_space_constraint(a, pltpu.HBM),
        pltpu.with_memory_space_constraint(dup, pltpu.VMEM),
    )


def y_product_kernel(
    part, idx_ref, at_ref, a_ref, dup_ref, o0_ref, o1_ref, o2_ref, o3_ref, exp_ref, r0_ref, r1_ref
):
    ih = pl.program_id(0)
    low = low_lanes(B)
    y = at_ref[1]
    count = a_ref.shape[2]
    outs = (o0_ref, o1_ref, o2_ref, o3_ref)
    turn1 = lax.rem(y, 2) == 1
    turn2 = y >= 2

    def multiply(cc):
        lhs = chosen_blocks(idx_ref, dup_ref, low, (ih * 4 + 2) * NCOL + part * count + cc)
        return row_pair(lhs, a_ref[0, 0, cc], a_ref[0, 1, cc])

    def encode(cc, res):
        e, tile = coded_products(res)
        exp_ref[pl.ds(ih * 8 + cc, 1), :] = e
        for g in range(2):
            for sp in range(4):
                t = [tile(2 * k + g, sp) for k in range(4)]
                t = [jnp.where(turn1, t[(k + 1) % 4], t[k]) for k in range(4)]
                t = [jnp.where(turn2, t[(k + 2) % 4], t[k]) for k in range(4)]
                for d in range(4):
                    outs[d][((2 * g + ih) * 8 + cc) * 4 + sp] = t[d].astype(jnp.int16)

    pipelined(count, multiply, encode, r0_ref, r1_ref)

    @pl.when(ih == 1)
    def _():
        e = exp_ref[...].astype(jnp.int32).astype(jnp.int16)
        for o_ref in outs:
            o_ref[128] = e


def y_products(part, idx, at, a, dup):
    block = 8
    out = pl.BlockSpec((129, 16, 128), lambda ih, idx, at: (0, 0, 0))
    return pl.pallas_call(
        lambda *refs: y_product_kernel(part, *refs),
        grid_spec=pltpu.PrefetchScalarGridSpec(
            num_scalar_prefetch=2,
            grid=(2,),
            in_specs=[
                pl.BlockSpec(
                    (1, 2, block, B, KA * B), lambda ih, idx, at: (ih * 2 + 1, 0, part, 0, 0)
                ),
                pl.BlockSpec(memory_space=pltpu.VMEM),
            ],
            out_specs=[out] * 4,
            scratch_shapes=[pltpu.VMEM((NCOL, 128), jnp.float32)]
            + [pltpu.VMEM((KAP * B, 128), jnp.float32)] * 2,
        ),
        out_shape=[pltpu.HBM((129, 16, 128), jnp.int16)]
        + [jax.ShapeDtypeStruct((129, 16, 128), jnp.int16)] * 3,
        compiler_params=pltpu.CompilerParams(vmem_limit_bytes=20 * 1024 * 1024),
    )(
        idx,
        at,
        pltpu.with_memory_space_constraint(a, pltpu.HBM),
        pltpu.with_memory_space_constraint(dup, pltpu.VMEM),
    )


def sum_and_code(tiles, out_ref, c):
    most = jnp.maximum(
        jnp.maximum(jnp.abs(tiles[0]), jnp.abs(tiles[1])),
        jnp.maximum(jnp.abs(tiles[2]), jnp.abs(tiles[3])),
    )
    e = exponent(jnp.max(most, axis=0, keepdims=True))
    mul = jnp.exp2(FULL - e)
    for sp in range(4):
        out_ref[c * 4 + sp] = coded(tiles[sp], mul)
    return e


def x_middle_kernel(at_ref, m0, m1, m2, m3, o0, o1, o2, o3, scale_ref, exp_ref):
    parts = (m0, m1, m2, m3)
    for d, m in enumerate(parts):
        scale_ref[d] = jnp.exp2(m[256].astype(jnp.float32) - FULL)
    for d2, out_ref in enumerate((o0, o1, o2, o3)):
        u = lax.rem(at_ref[1] + d2, 4)

        def one(c, carry):
            scales = [scale_ref[d, pl.ds(c, 1), :] for d in range(4)]
            tiles = []
            for sp in range(4):
                terms = [
                    m[(u * NCOL + c) * 4 + sp].astype(jnp.float32) * scale
                    for m, scale in zip(parts, scales)
                ]
                tiles.append((terms[0] + terms[1]) + (terms[2] + terms[3]))
            exp_ref[pl.ds(c, 1), :] = sum_and_code(tiles, out_ref, c)
            return carry

        lax.fori_loop(0, NCOL, one, 0, unroll=2)
        out_ref[64] = exp_ref[...].astype(jnp.int32).astype(jnp.int16)


def y_middle_kernel(at_ref, *refs):
    parts, outs, scale_ref, exp_ref = refs[:8], refs[8:12], refs[12], refs[13]
    for n, m in enumerate(parts):
        scale_ref[n] = jnp.exp2(m[128].astype(jnp.float32) - FULL)
    for d2, out_ref in enumerate(outs):
        u = lax.rem(at_ref[0] + d2, 4)
        ih = lax.rem(u, 2)
        for half in range(2):
            own = parts[half * 4:half * 4 + 4]

            def one(cc, carry):
                scales = [scale_ref[half * 4 + d, pl.ds(ih * 8 + cc, 1), :] for d in range(4)]
                tiles = []
                for sp in range(4):
                    terms = [
                        m[(u * 8 + cc) * 4 + sp].astype(jnp.float32) * scale
                        for m, scale in zip(own, scales)
                    ]
                    tiles.append((terms[0] + terms[1]) + (terms[2] + terms[3]))
                c = half * 8 + cc
                exp_ref[pl.ds(c, 1), :] = sum_and_code(tiles, out_ref, c)
                return carry

            lax.fori_loop(0, 8, one, 0, unroll=2)
        out_ref[64] = exp_ref[...].astype(jnp.int32).astype(jnp.int16)


def middle(kernel, at, parts):
    vmem = pl.BlockSpec(memory_space=pltpu.VMEM)
    return pl.pallas_call(
        kernel,
        in_specs=[pl.BlockSpec(memory_space=pltpu.SMEM)] + [vmem] * len(parts),
        out_specs=[vmem] * 4,
        scratch_shapes=[
            pltpu.VMEM((len(parts), NCOL, 128), jnp.float32),
            pltpu.VMEM((NCOL, 128), jnp.float32),
        ],
        out_shape=[jax.ShapeDtypeStruct((65, 16, 128), jnp.int16)] * 4,
    )(at, *parts)


def decode(parts, out_ref, first_row, scale_ref):
    for n, m in enumerate(parts):
        scale_ref[n] = jnp.exp2(m[64].astype(jnp.float32) - FULL)

    def one(c, carry):
        scales = [scale_ref[d, pl.ds(c, 1), :] for d in range(4)]
        for sp in range(4):
            terms = [parts[d][c * 4 + sp].astype(jnp.float32) * scales[d] for d in range(4)]
            total = (terms[0] + terms[1]) + (terms[2] + terms[3])
            row = first_row + sp * 16
            out_ref[c, row:row + 16, :] = total.astype(jnp.bfloat16)
        return carry

    lax.fori_loop(0, NCOL, one, 0, unroll=2)


def add_terms(qh, tgt_ref, at_ref, x_ref, p_refs, acc_ref):
    dy = pl.program_id(0)
    low = low_lanes(8)
    low_x = low_lanes(B)
    for dx, p_ref in enumerate(p_refs):
        c = lax.rem(at_ref[1] - dy + 4, 4) * 4 + lax.rem(at_ref[0] - dx + 4, 4)
        x = x_ref[c, qh * B:(qh + 1) * B, :]
        none = jnp.zeros_like(x)
        lhs = jnp.concatenate([jnp.where(low_x, x, none), jnp.where(low_x, none, x)], axis=0)
        rhs = p_ref[0]
        res = lax.dot_general(
            lhs, rhs, (((1,), (0,)), ((), ())), preferred_element_type=jnp.float32
        )
        for lo in range(2):
            ats, sums = [], []
            for m in range(KP):
                for s in range(KAP):
                    at = tgt_ref[(((c * 2 + qh) * 2 + lo) * KP + m) * KAP + s]
                    rows = (lo * KAP + s) * 8
                    tile = res[rows:rows + 8, (m // 2) * 128:(m // 2) * 128 + 128]
                    keep = low if m % 2 == 0 else jnp.logical_not(low)
                    ats.append(at)
                    sums.append(acc_ref[at] + jnp.where(keep, tile, 0.0))
            for at, total in zip(ats, sums):
                acc_ref[at] = total


def first_coarse_kernel(tgt_ref, at_ref, *refs):
    parts, p_refs, (x_ref, acc_ref, scale_ref) = refs[:4], refs[4:8], refs[8:]

    @pl.when(pl.program_id(0) == 0)
    def _():
        acc_ref[...] = jnp.zeros_like(acc_ref)
        decode(parts, x_ref, 0, scale_ref)

    add_terms(0, tgt_ref, at_ref, x_ref, p_refs, acc_ref)


def second_coarse_kernel(tgt_ref, at_ref, *refs):
    parts, p_refs, (x0_ref, before_ref) = refs[:4], refs[4:8], refs[8:10]
    x_ref, keep_ref, send_ref, acc_ref, scale_ref = refs[10:]
    low = low_lanes(8)

    @pl.when(pl.program_id(0) == 0)
    def _():
        acc_ref[...] = jnp.zeros_like(acc_ref)
        decode(parts, x_ref, B, scale_ref)
        x_ref[:, 0:B, :] = x0_ref[...]

    add_terms(1, tgt_ref, at_ref, x_ref, p_refs, acc_ref)

    @pl.when(pl.program_id(0) == 3)
    def _():
        for flip, out_ref in ((1, send_ref), (0, keep_ref)):
            core = lax.rem(at_ref[3] + flip, 2)
            for d in range(4):
                first = (lax.rem(at_ref[2] + d, 4) * 2 + core) * NCOL

                def fold(col, carry):
                    for tp in range(KC // 2):
                        at = (first + col) * KC + 2 * tp
                        t0 = acc_ref[at] + before_ref[at]
                        t1 = acc_ref[at + 1] + before_ref[at + 1]
                        t0 = t0 + pltpu.roll(t0, B, 1)
                        t1 = t1 + pltpu.roll(t1, B, 1)
                        out_ref[d, col, tp] = jnp.where(low, t0, t1)
                    return carry

                lax.fori_loop(0, NCOL, fold, 0, unroll=4)


def coarse_specs(qh):
    whole = pl.BlockSpec((65, 16, 128), lambda dy, tgt, at: (0, 0, 0))
    return [whole] * 4 + [
        pl.BlockSpec((1, 2 * B, KP * B), lambda dy, tgt, at: (dy, qh, 0))
    ] * 4


def first_coarse(tgt, at, parts, ps):
    return pl.pallas_call(
        first_coarse_kernel,
        grid_spec=pltpu.PrefetchScalarGridSpec(
            num_scalar_prefetch=2,
            grid=(4,),
            in_specs=coarse_specs(0),
            out_specs=[
                pl.BlockSpec((NCOL, B, 128), lambda dy, tgt, at: (0, 0, 0)),
                pl.BlockSpec((NCB * KC + 1, 8, 128), lambda dy, tgt, at: (0, 0, 0)),
            ],
            scratch_shapes=[pltpu.VMEM((4, NCOL, 128), jnp.float32)],
        ),
        out_shape=[
            jax.ShapeDtypeStruct((NCOL, B, 128), jnp.bfloat16),
            jax.ShapeDtypeStruct((NCB * KC + 1, 8, 128), jnp.float32),
        ],
        name="first_coarse",
        compiler_params=pltpu.CompilerParams(vmem_limit_bytes=32 * 1024 * 1024),
    )(tgt, at, *parts, *ps)


def second_coarse(tgt, at, parts, ps, x0, before):
    shape = (4, NCOL, KC // 2, 8, 128)
    out = pl.BlockSpec(shape, lambda dy, tgt, at: (0, 0, 0, 0, 0))
    return pl.pallas_call(
        second_coarse_kernel,
        grid_spec=pltpu.PrefetchScalarGridSpec(
            num_scalar_prefetch=2,
            grid=(4,),
            in_specs=coarse_specs(1)
            + [
                pl.BlockSpec((NCOL, B, 128), lambda dy, tgt, at: (0, 0, 0)),
                pl.BlockSpec(memory_space=pltpu.VMEM),
            ],
            out_specs=[
                pl.BlockSpec((NCOL, 3 * B, 128), lambda dy, tgt, at: (0, 0, 0)), out, out
            ],
            scratch_shapes=[
                pltpu.VMEM((NCB * KC + 1, 8, 128), jnp.float32),
                pltpu.VMEM((4, NCOL, 128), jnp.float32),
            ],
        ),
        out_shape=[
            jax.ShapeDtypeStruct((NCOL, 3 * B, 128), jnp.bfloat16),
            jax.ShapeDtypeStruct(shape, jnp.float32),
            jax.ShapeDtypeStruct(shape, jnp.float32),
        ],
        name="second_coarse",
        compiler_params=pltpu.CompilerParams(vmem_limit_bytes=32 * 1024 * 1024),
    )(tgt, at, *parts, *ps, x0, pltpu.with_memory_space_constraint(before, pltpu.VMEM))


def layout_kernel(x_ref, ap_ref, coarse_ref, turn_ref, wide_ref, flat_ref):
    for tp in range(KC // 2):
        rows = []
        for bg in range(8):
            total = None
            for ih in range(2):
                for part in range(2):
                    r0 = 2 * B + part * 32 + tp * 8
                    term = x_ref[bg * 2 + ih, r0:r0 + 8, :].astype(jnp.float32)
                    total = term if total is None else total + term
            rows.append(total)
        wide_ref[...] = jnp.concatenate(rows, axis=0).T
        for lo in range(2):
            even = wide_ref[pl.ds(lo * B, 32, stride=2), :]
            odd = wide_ref[pl.ds(lo * B + 1, 32, stride=2), :]
            flat_ref[pl.ds(tp * 2 + lo, 32, stride=8), :] = jnp.concatenate([even, odd], axis=1)
    for h in range(32):
        coarse_ref[:, h * 128:(h + 1) * 128] = flat_ref[h * 8:(h + 1) * 8, :]
    for ih in range(2):
        for qh in range(2):
            for s in range(KAP):
                r0 = qh * B + s * 8
                m = jnp.concatenate(
                    [x_ref[bg * 2 + ih, r0:r0 + 8, :] for bg in range(8)], axis=0
                )
                t = m.astype(jnp.float32).T
                for lo in range(2):
                    top, bottom = t[lo * B:lo * B + 32], t[lo * B + 32:lo * B + B]
                    turn_ref[lo, pl.ds(s, 32, stride=8), :] = jnp.concatenate([top, bottom], axis=1)
            for lo in range(2):
                for h in range(32):
                    tile = turn_ref[lo, h * 8:(h + 1) * 8, :]
                    ap_ref[ih * 4 + qh * 2 + lo, :, h * 128:(h + 1) * 128] = tile.astype(jnp.bfloat16)


def layout(x):
    vmem = pl.BlockSpec(memory_space=pltpu.VMEM)
    return pl.pallas_call(
        layout_kernel,
        in_specs=[vmem],
        out_specs=[vmem, vmem],
        scratch_shapes=[
            pltpu.VMEM((2, 256, 128), jnp.float32),
            pltpu.VMEM((128, B), jnp.float32),
            pltpu.VMEM((256, 128), jnp.float32),
        ],
        out_shape=[
            jax.ShapeDtypeStruct((8, KAP, B * B), jnp.bfloat16),
            jax.ShapeDtypeStruct((KC, B * B), jnp.float32),
        ],
        name="layout",
    )(x)


def pick_rows(table, index):
    hot = (index[..., None] == jnp.arange(table.shape[0], dtype=jnp.int32)).astype(jnp.bfloat16)
    rows = jnp.einsum(
        "...k,km->...m", hot, table.astype(jnp.bfloat16), preferred_element_type=jnp.float32
    )
    return rows.astype(jnp.int32)


def index_slab(index):
    return jnp.pad(index.astype(jnp.bfloat16), ((0, 16 - index.shape[0]), (0, KP * B - KP)))


def step(a_blocks, a_index, p_blocks, p_index, ap_index, coarse_index):
    row = lax.axis_index("row")
    col = lax.axis_index("col")
    z, core = row // 2, row % 2
    y, x = col // 4, col % 4
    at = jnp.stack([x, y, z, core]).astype(jnp.int32)
    half = x % 2

    own = p_blocks[:, 0].reshape(8, KP, B, B)
    pt = own.transpose(0, 3, 1, 2).reshape(8 * B, KP * B)
    pt = jnp.concatenate([pt, index_slab(p_index[:, 0])], axis=0)
    by_z = [pt] + [along_row(pt, d, 0) for d in (1, 2, 3)]
    partner = along_row(pt, 0, 1)

    pn = own.reshape(8, KP, 32, 2, B).transpose(0, 3, 2, 1, 4).reshape(2, 4 * B, KP * B)
    halves = jnp.stack(
        [
            jnp.concatenate([pn[h], index_slab(p_index[4 * h:4 * h + 4, 0])], axis=0)
            for h in range(2)
        ]
    )
    *by_z, halves = lax.optimization_barrier((*by_z, halves))
    parts = [by_z[0], partner]
    for part in by_z[1:]:
        parts += [part, along_row(part, 0, 1)]
    by_y = [halves] + [along_col(halves, 0, d) for d in (1, 2, 3)]

    a = spread(a_blocks[:, 0]).reshape(4, 2, NCOL, B, KA * B)

    a_idx = a_index[:, 0]
    from_row = a_idx // 8
    place = ((z - from_row // 2) % 4) * 2 + (core + from_row) % 2
    place = place * 8 + a_idx % 8
    dup, cols_k = table(parts)
    picked = pick_rows(cols_k[:, :KP], place)
    equal = picked[:, :, None, :] == ap_index[:, None, :, None]
    ids = place[:, :, None, None] * KP + jnp.arange(KP, dtype=jnp.int32)
    idx = jnp.min(jnp.where(equal, ids, NK * KP), axis=3).reshape(-1)

    x1, x3 = x_products(1, idx, at, a, dup)
    got_x1, got_x3 = along_col(x1, 1, 0), along_col(x3, 3, 0)
    ya = y_products(0, idx, at, a, dup)
    got_ya = [along_col(ya[d], 0, d) for d in (1, 2, 3)]
    x0, x2 = x_products(0, idx, at, a, dup)
    got_x2 = along_col(x2, 2, 0)
    yb = y_products(1, idx, at, a, dup)
    got_yb = [along_col(yb[d], 0, d) for d in (1, 2, 3)]
    s0 = middle(x_middle_kernel, at, [x0, got_x1, got_x2, got_x3])
    y_last = [along_col(s0[d], 0, d) for d in (1, 2, 3)]
    s1 = middle(y_middle_kernel, at, [ya[0], *got_ya, yb[0], *got_yb])
    far = along_col(s1[2], 2, 0)
    x_last = [along_col(s1[1], 1, 0), far, along_col(s1[3], 3, 0)]

    by_y = jnp.stack(by_y)
    same = lax.dynamic_index_in_dim(by_y, half, 1, keepdims=False)
    diff = lax.dynamic_index_in_dim(by_y, 1 - half, 1, keepdims=False)
    ps = [same, along_col(diff, 1, 0), along_col(same, 2, 0), along_col(diff, 3, 0)]

    cols_p = jnp.stack([p[:, 4 * B:4 * B + 4, :KP] for p in ps]).reshape(NCOL, 16)
    cc = jnp.arange(NCOL, dtype=jnp.int32)
    where = ((x - cc % 4) % 4) * 4 + (y - cc // 4) % 4
    cols_i = pick_rows(cols_p, where).reshape(NCOL, 4, KP)
    slots = lax.dynamic_index_in_dim(
        ap_index.reshape(2, 4, NCOL, KAP), half, 0, keepdims=False
    ).transpose(1, 0, 2)
    targets = pick_rows(coarse_index, cols_i)
    hit = targets[:, :, :, None, :] == slots[:, :, None, :, None]
    slot = cols_i[:, :, :, None, None] * KC + jnp.arange(KC, dtype=jnp.int32)
    tgt = jnp.min(jnp.where(hit, slot, NCB * KC), axis=4).reshape(-1)

    x0, before = first_coarse(tgt, at, [s0[0], *y_last], ps)
    apt, keep, send = second_coarse(tgt, at, [s1[0], *x_last], ps, x0, before)
    got = along_row(send, 0, 1)
    sums = [keep[d] + got[d] for d in range(4)]
    coarse = sums[0]
    moved = [along_row(sums[d], d, 0) for d in (1, 2, 3)]
    for part in moved:
        coarse = coarse + part
    high = lax.reduce_precision(coarse, exponent_bits=8, mantissa_bits=7)
    pair = jnp.concatenate(
        [v.astype(jnp.bfloat16).reshape(NCOL, 32, 128) for v in (high, coarse - high)], axis=1
    )
    both = lax.dynamic_update_slice(apt, pair, (0, 2 * B, 0))
    both = lax.all_to_all(both, "col", 0, 0, tiled=True)
    ap_out, coarse_out = layout(both)
    ap_out = ap_out.reshape(8, 1, KAP, B * B)
    coarse_out = coarse_out.reshape(1, KC, B * B)
    return ap_out, coarse_out


def solution(mesh):
    placed = (
        P("row", "col", None, None),
        P("row", "col", None),
        P("row", "col", None, None),
        P("row", "col", None),
        P("row", None),
        P(),
    )
    return jax.shard_map(
        step,
        mesh=mesh,
        in_specs=placed,
        out_specs=(P("row", "col", None, None), P(("row", "col"), None, None)),
        check_vma=False,
    )
```

```python
import jax
import jax.numpy as jnp
from jax import lax
from jax.experimental import pallas as pl
from jax.experimental.pallas import tpu as pltpu
from jax.sharding import PartitionSpec as P


B = 64
KA = 4
KP = 4
KAP = 8
KC = 8
NCOL = 16
NK = 64
NCB = 128
FULL = 14.0
TINY = 1e-30


def along_row(v, dz, flip):
    pairs = [(r, ((r // 2 + dz) % 4) * 2 + (r % 2 + flip) % 2) for r in range(8)]
    return lax.ppermute(v, "row", pairs)


def along_col(v, dx, dy):
    pairs = [(c, ((c // 4 + dy) % 4) * 4 + (c % 4 + dx) % 4) for c in range(16)]
    return lax.ppermute(v, "col", pairs)


def low_lanes(rows):
    return lax.broadcasted_iota(jnp.int32, (rows, 128), 1) < B


def spread_kernel(a_ref, out_ref, buf_ref):
    low = low_lanes(32)

    def some(g, carry):
        for u in range(4):
            i = g * 4 + u
            v = a_ref[i].astype(jnp.float32)
            for h in range(32):
                buf_ref[u, h * 4:(h + 1) * 4, :] = v[:, h * 128:(h + 1) * 128]
        for u in range(4):
            i = g * 4 + u
            for ep in range(2):
                v0 = buf_ref[u, pl.ds(2 * ep, 32, stride=4), :]
                v1 = buf_ref[u, pl.ds(2 * ep + 1, 32, stride=4), :]
                top = jnp.where(low, v0, pltpu.roll(v1, B, 1))
                bottom = jnp.where(low, pltpu.roll(v0, B, 1), v1)
                out_ref[i, 0:32, ep * 128:(ep + 1) * 128] = top.astype(jnp.bfloat16)
                out_ref[i, 32:64, ep * 128:(ep + 1) * 128] = bottom.astype(jnp.bfloat16)
        return carry

    lax.fori_loop(0, 4, some, 0)


def spread(a):
    return pl.pallas_call(
        spread_kernel,
        grid=(8,),
        in_specs=[pl.BlockSpec((16, KA, B * B), lambda g: (g, 0, 0))],
        out_specs=pl.BlockSpec((16, B, KA * B), lambda g: (g, 0, 0)),
        scratch_shapes=[pltpu.VMEM((4, 128, 128), jnp.float32)],
        out_shape=pltpu.HBM((128, B, KA * B), jnp.bfloat16),
        name="spread",
        compiler_params=pltpu.CompilerParams(vmem_limit_bytes=8 * 1024 * 1024),
    )(pltpu.with_memory_space_constraint(a, pltpu.HBM))


def table_kernel(*refs):
    parts, out_ref, cols_ref = refs[:8], refs[8], refs[9]
    low = low_lanes(B)
    for n, part in enumerate(parts):
        cols_ref[n * 8:(n + 1) * 8, :] = part[8 * B:8 * B + 8, 0:128].astype(jnp.float32)

        def fill(q, carry):
            for mh in range(2):
                v = part[pl.ds(pl.multiple_of(q * B, B), B), mh * 128:(mh + 1) * 128]
                turned = jnp.concatenate([v[:, B:], v[:, :B]], axis=1)
                at = (n * 8 + q) * 4 + 2 * mh
                out_ref[at] = jnp.where(low, v, turned)
                out_ref[at + 1] = jnp.where(low, turned, v)
            return carry

        lax.fori_loop(0, 8, fill, 0, unroll=2)
    out_ref[NK * KP] = jnp.zeros((B, 128), jnp.bfloat16)


def table(parts):
    whole = pl.BlockSpec(memory_space=pltpu.VMEM)
    return pl.pallas_call(
        table_kernel,
        in_specs=[whole] * 8,
        out_specs=[whole, whole],
        out_shape=[
            pltpu.VMEM((NK * KP + 1, B, 128), jnp.bfloat16),
            jax.ShapeDtypeStruct((NK, 128), jnp.float32),
        ],
        name="table",
        compiler_params=pltpu.CompilerParams(vmem_limit_bytes=12 * 1024 * 1024),
    )(*parts)


def nt_dot(a, b):
    return lax.dot_general(a, b, (((1,), (1,)), ((), ())), preferred_element_type=jnp.float32)


def exponent(most):
    return jnp.ceil(jnp.log2(jnp.maximum(most, TINY)))


def coded(v, mul):
    return jnp.round(v * mul).astype(jnp.int32).astype(jnp.int16)


def row_pair(lhs, rhs_top, rhs_bottom):
    zero = jnp.zeros((B, KA * B), jnp.bfloat16)
    stacked = jnp.concatenate(
        [
            jnp.concatenate([rhs_top, zero], axis=1),
            jnp.concatenate([zero, rhs_bottom], axis=1),
        ],
        axis=0,
    )
    return nt_dot(lhs, stacked)


def chosen_blocks(idx_ref, dup_ref, low, first_row):
    rows = []
    for s in range(KAP):
        pieces = []
        for lo in range(2):
            row = first_row + lo * NCOL
            for ep in range(2):
                first = dup_ref[idx_ref[(2 * ep) * KAP + s, row]]
                second = dup_ref[idx_ref[(2 * ep + 1) * KAP + s, row]]
                pieces.append(jnp.where(low, first, second))
        rows.append(jnp.concatenate(pieces, axis=1))
    return jnp.concatenate(rows, axis=0)


def coded_products(res):
    e = exponent(jnp.max(jnp.abs(res), axis=0, keepdims=True))
    q = jnp.round(res * jnp.exp2(FULL - e)).astype(jnp.int32)

    def tile(bg, sp):
        r0 = 2 * sp * B + bg * 8
        return jnp.concatenate([q[r0:r0 + 8], q[r0 + B:r0 + B + 8]], axis=0)

    return e, tile


def pipelined(count, multiply, encode, r0_ref, r1_ref):
    r1_ref[...] = jnp.zeros_like(r1_ref)

    def two(k, carry):
        r0_ref[...] = multiply(2 * k)
        encode(jnp.maximum(2 * k - 1, 0), r1_ref[...])
        r1_ref[...] = multiply(2 * k + 1)
        encode(2 * k, r0_ref[...])
        return carry

    lax.fori_loop(0, count // 2, two, 0)
    encode(count - 1, r1_ref[...])


def x_product_kernel(
    j, idx_ref, at_ref, a_ref, dup_ref, near_ref, far_ref, exp_ref, r0_ref, r1_ref
):
    cblk = pl.program_id(0)
    low = low_lanes(B)
    goal = lax.rem(at_ref[0] + j, 4)
    ih = lax.rem(goal, 2)
    count = a_ref.shape[2]
    is_low = goal < 2

    def multiply(cc):
        lhs = chosen_blocks(idx_ref, dup_ref, low, ih * 4 * NCOL + cblk * count + cc)
        return row_pair(lhs, a_ref[0, 0, cc], a_ref[0, 1, cc])

    def encode(cc, res):
        c = cblk * count + cc
        e, tile = coded_products(res)
        exp_ref[pl.ds(c, 1), :] = e
        for u in range(4):
            for sp in range(4):
                t0, t1 = tile(2 * u, sp), tile(2 * u + 1, sp)
                at = (u * NCOL + c) * 4 + sp
                near_ref[at] = jnp.where(is_low, t0, t1).astype(jnp.int16)
                far_ref[at] = jnp.where(is_low, t1, t0).astype(jnp.int16)

    pipelined(count, multiply, encode, r0_ref, r1_ref)

    @pl.when(cblk == pl.num_programs(0) - 1)
    def _():
        e = exp_ref[...].astype(jnp.int32).astype(jnp.int16)
        near_ref[256] = e
        far_ref[256] = e


def x_products(j, idx, at, a, dup):
    block = 8
    out = pl.BlockSpec((257, 16, 128), lambda c, idx, at: (0, 0, 0))
    return pl.pallas_call(
        lambda *refs: x_product_kernel(j, *refs),
        grid_spec=pltpu.PrefetchScalarGridSpec(
            num_scalar_prefetch=2,
            grid=(NCOL // block,),
            in_specs=[
                pl.BlockSpec(
                    (1, 2, block, B, KA * B),
                    lambda c, idx, at: (lax.rem(at[0] + j, 2) * 2, 0, c, 0, 0),
                ),
                pl.BlockSpec(memory_space=pltpu.VMEM),
            ],
            out_specs=[out, out],
            scratch_shapes=[pltpu.VMEM((NCOL, 128), jnp.float32)]
            + [pltpu.VMEM((KAP * B, 128), jnp.float32)] * 2,
        ),
        out_shape=[
            (pltpu.HBM if j == 0 else jax.ShapeDtypeStruct)((257, 16, 128), jnp.int16),
            jax.ShapeDtypeStruct((257, 16, 128), jnp.int16),
        ],
        compiler_params=pltpu.CompilerParams(vmem_limit_bytes=20 * 1024 * 1024),
    )(
        idx,
        at,
        pltpu.with_memory_space_constraint(a, pltpu.HBM),
        pltpu.with_memory_space_constraint(dup, pltpu.VMEM),
    )


def y_product_kernel(
    part, idx_ref, at_ref, a_ref, dup_ref, o0_ref, o1_ref, o2_ref, o3_ref, exp_ref, r0_ref, r1_ref
):
    ih = pl.program_id(0)
    low = low_lanes(B)
    y = at_ref[1]
    count = a_ref.shape[2]
    outs = (o0_ref, o1_ref, o2_ref, o3_ref)
    turn1 = lax.rem(y, 2) == 1
    turn2 = y >= 2

    def multiply(cc):
        lhs = chosen_blocks(idx_ref, dup_ref, low, (ih * 4 + 2) * NCOL + part * count + cc)
        return row_pair(lhs, a_ref[0, 0, cc], a_ref[0, 1, cc])

    def encode(cc, res):
        e, tile = coded_products(res)
        exp_ref[pl.ds(ih * 8 + cc, 1), :] = e
        for g in range(2):
            for sp in range(4):
                t = [tile(2 * k + g, sp) for k in range(4)]
                t = [jnp.where(turn1, t[(k + 1) % 4], t[k]) for k in range(4)]
                t = [jnp.where(turn2, t[(k + 2) % 4], t[k]) for k in range(4)]
                for d in range(4):
                    outs[d][((2 * g + ih) * 8 + cc) * 4 + sp] = t[d].astype(jnp.int16)

    pipelined(count, multiply, encode, r0_ref, r1_ref)

    @pl.when(ih == 1)
    def _():
        e = exp_ref[...].astype(jnp.int32).astype(jnp.int16)
        for o_ref in outs:
            o_ref[128] = e


def y_products(part, idx, at, a, dup):
    block = 8
    out = pl.BlockSpec((129, 16, 128), lambda ih, idx, at: (0, 0, 0))
    return pl.pallas_call(
        lambda *refs: y_product_kernel(part, *refs),
        grid_spec=pltpu.PrefetchScalarGridSpec(
            num_scalar_prefetch=2,
            grid=(2,),
            in_specs=[
                pl.BlockSpec(
                    (1, 2, block, B, KA * B), lambda ih, idx, at: (ih * 2 + 1, 0, part, 0, 0)
                ),
                pl.BlockSpec(memory_space=pltpu.VMEM),
            ],
            out_specs=[out] * 4,
            scratch_shapes=[pltpu.VMEM((NCOL, 128), jnp.float32)]
            + [pltpu.VMEM((KAP * B, 128), jnp.float32)] * 2,
        ),
        out_shape=[pltpu.HBM((129, 16, 128), jnp.int16)]
        + [jax.ShapeDtypeStruct((129, 16, 128), jnp.int16)] * 3,
        compiler_params=pltpu.CompilerParams(vmem_limit_bytes=20 * 1024 * 1024),
    )(
        idx,
        at,
        pltpu.with_memory_space_constraint(a, pltpu.HBM),
        pltpu.with_memory_space_constraint(dup, pltpu.VMEM),
    )


def sum_and_code(tiles, out_ref, c):
    most = jnp.maximum(
        jnp.maximum(jnp.abs(tiles[0]), jnp.abs(tiles[1])),
        jnp.maximum(jnp.abs(tiles[2]), jnp.abs(tiles[3])),
    )
    e = exponent(jnp.max(most, axis=0, keepdims=True))
    mul = jnp.exp2(FULL - e)
    for sp in range(4):
        out_ref[c * 4 + sp] = coded(tiles[sp], mul)
    return e


def x_middle_kernel(at_ref, m0, m1, m2, m3, o0, o1, o2, o3, scale_ref, exp_ref):
    parts = (m0, m1, m2, m3)
    for d, m in enumerate(parts):
        scale_ref[d] = jnp.exp2(m[256].astype(jnp.float32) - FULL)
    for d2, out_ref in enumerate((o0, o1, o2, o3)):
        u = lax.rem(at_ref[1] + d2, 4)

        def one(c, carry):
            scales = [scale_ref[d, pl.ds(c, 1), :] for d in range(4)]
            tiles = []
            for sp in range(4):
                terms = [
                    m[(u * NCOL + c) * 4 + sp].astype(jnp.float32) * scale
                    for m, scale in zip(parts, scales)
                ]
                tiles.append((terms[0] + terms[1]) + (terms[2] + terms[3]))
            exp_ref[pl.ds(c, 1), :] = sum_and_code(tiles, out_ref, c)
            return carry

        lax.fori_loop(0, NCOL, one, 0, unroll=2)
        out_ref[64] = exp_ref[...].astype(jnp.int32).astype(jnp.int16)


def y_middle_kernel(at_ref, *refs):
    parts, outs, scale_ref, exp_ref = refs[:8], refs[8:12], refs[12], refs[13]
    for n, m in enumerate(parts):
        scale_ref[n] = jnp.exp2(m[128].astype(jnp.float32) - FULL)
    for d2, out_ref in enumerate(outs):
        u = lax.rem(at_ref[0] + d2, 4)
        ih = lax.rem(u, 2)
        for half in range(2):
            own = parts[half * 4:half * 4 + 4]

            def one(cc, carry):
                scales = [scale_ref[half * 4 + d, pl.ds(ih * 8 + cc, 1), :] for d in range(4)]
                tiles = []
                for sp in range(4):
                    terms = [
                        m[(u * 8 + cc) * 4 + sp].astype(jnp.float32) * scale
                        for m, scale in zip(own, scales)
                    ]
                    tiles.append((terms[0] + terms[1]) + (terms[2] + terms[3]))
                c = half * 8 + cc
                exp_ref[pl.ds(c, 1), :] = sum_and_code(tiles, out_ref, c)
                return carry

            lax.fori_loop(0, 8, one, 0, unroll=2)
        out_ref[64] = exp_ref[...].astype(jnp.int32).astype(jnp.int16)


def middle(kernel, at, parts):
    vmem = pl.BlockSpec(memory_space=pltpu.VMEM)
    return pl.pallas_call(
        kernel,
        in_specs=[pl.BlockSpec(memory_space=pltpu.SMEM)] + [vmem] * len(parts),
        out_specs=[vmem] * 4,
        scratch_shapes=[
            pltpu.VMEM((len(parts), NCOL, 128), jnp.float32),
            pltpu.VMEM((NCOL, 128), jnp.float32),
        ],
        out_shape=[jax.ShapeDtypeStruct((65, 16, 128), jnp.int16)] * 4,
    )(at, *parts)


def decode(parts, out_ref, first_row, scale_ref):
    for n, m in enumerate(parts):
        scale_ref[n] = jnp.exp2(m[64].astype(jnp.float32) - FULL)

    def one(c, carry):
        scales = [scale_ref[d, pl.ds(c, 1), :] for d in range(4)]
        for sp in range(4):
            terms = [parts[d][c * 4 + sp].astype(jnp.float32) * scales[d] for d in range(4)]
            total = (terms[0] + terms[1]) + (terms[2] + terms[3])
            row = first_row + sp * 16
            out_ref[c, row:row + 16, :] = total.astype(jnp.bfloat16)
        return carry

    lax.fori_loop(0, NCOL, one, 0, unroll=2)


def add_terms(qh, tgt_ref, at_ref, x_ref, p_refs, acc_ref):
    dy = pl.program_id(0)
    low = low_lanes(8)
    low_x = low_lanes(B)
    for dx, p_ref in enumerate(p_refs):
        c = lax.rem(at_ref[1] - dy + 4, 4) * 4 + lax.rem(at_ref[0] - dx + 4, 4)
        x = x_ref[c, qh * B:(qh + 1) * B, :]
        none = jnp.zeros_like(x)
        lhs = jnp.concatenate([jnp.where(low_x, x, none), jnp.where(low_x, none, x)], axis=0)
        rhs = p_ref[0]
        res = lax.dot_general(
            lhs, rhs, (((1,), (0,)), ((), ())), preferred_element_type=jnp.float32
        )
        for lo in range(2):
            ats, sums = [], []
            for m in range(KP):
                for s in range(KAP):
                    at = tgt_ref[(((c * 2 + qh) * 2 + lo) * KP + m) * KAP + s]
                    rows = (lo * KAP + s) * 8
                    tile = res[rows:rows + 8, (m // 2) * 128:(m // 2) * 128 + 128]
                    keep = low if m % 2 == 0 else jnp.logical_not(low)
                    ats.append(at)
                    sums.append(acc_ref[at] + jnp.where(keep, tile, 0.0))
            for at, total in zip(ats, sums):
                acc_ref[at] = total


def first_coarse_kernel(tgt_ref, at_ref, *refs):
    parts, p_refs, (x_ref, acc_ref, scale_ref) = refs[:4], refs[4:8], refs[8:]

    @pl.when(pl.program_id(0) == 0)
    def _():
        acc_ref[...] = jnp.zeros_like(acc_ref)
        decode(parts, x_ref, 0, scale_ref)

    add_terms(0, tgt_ref, at_ref, x_ref, p_refs, acc_ref)


def second_coarse_kernel(tgt_ref, at_ref, *refs):
    parts, p_refs, (x0_ref, before_ref) = refs[:4], refs[4:8], refs[8:10]
    x_ref, keep_ref, send_ref, acc_ref, scale_ref = refs[10:]
    low = low_lanes(8)

    @pl.when(pl.program_id(0) == 0)
    def _():
        acc_ref[...] = jnp.zeros_like(acc_ref)
        decode(parts, x_ref, B, scale_ref)
        x_ref[:, 0:B, :] = x0_ref[...]

    add_terms(1, tgt_ref, at_ref, x_ref, p_refs, acc_ref)

    @pl.when(pl.program_id(0) == 3)
    def _():
        for flip, out_ref in ((1, send_ref), (0, keep_ref)):
            core = lax.rem(at_ref[3] + flip, 2)
            for d in range(4):
                first = (lax.rem(at_ref[2] + d, 4) * 2 + core) * NCOL

                def fold(col, carry):
                    for tp in range(KC // 2):
                        at = (first + col) * KC + 2 * tp
                        t0 = acc_ref[at] + before_ref[at]
                        t1 = acc_ref[at + 1] + before_ref[at + 1]
                        t0 = t0 + pltpu.roll(t0, B, 1)
                        t1 = t1 + pltpu.roll(t1, B, 1)
                        out_ref[d, col, tp] = jnp.where(low, t0, t1)
                    return carry

                lax.fori_loop(0, NCOL, fold, 0, unroll=4)


def coarse_specs(qh):
    whole = pl.BlockSpec((65, 16, 128), lambda dy, tgt, at: (0, 0, 0))
    return [whole] * 4 + [
        pl.BlockSpec((1, 2 * B, KP * B), lambda dy, tgt, at: (dy, qh, 0))
    ] * 4


def first_coarse(tgt, at, parts, ps):
    return pl.pallas_call(
        first_coarse_kernel,
        grid_spec=pltpu.PrefetchScalarGridSpec(
            num_scalar_prefetch=2,
            grid=(4,),
            in_specs=coarse_specs(0),
            out_specs=[
                pl.BlockSpec((NCOL, B, 128), lambda dy, tgt, at: (0, 0, 0)),
                pl.BlockSpec((NCB * KC + 1, 8, 128), lambda dy, tgt, at: (0, 0, 0)),
            ],
            scratch_shapes=[pltpu.VMEM((4, NCOL, 128), jnp.float32)],
        ),
        out_shape=[
            jax.ShapeDtypeStruct((NCOL, B, 128), jnp.bfloat16),
            jax.ShapeDtypeStruct((NCB * KC + 1, 8, 128), jnp.float32),
        ],
        name="first_coarse",
        compiler_params=pltpu.CompilerParams(vmem_limit_bytes=32 * 1024 * 1024),
    )(tgt, at, *parts, *ps)


def second_coarse(tgt, at, parts, ps, x0, before):
    shape = (4, NCOL, KC // 2, 8, 128)
    out = pl.BlockSpec(shape, lambda dy, tgt, at: (0, 0, 0, 0, 0))
    return pl.pallas_call(
        second_coarse_kernel,
        grid_spec=pltpu.PrefetchScalarGridSpec(
            num_scalar_prefetch=2,
            grid=(4,),
            in_specs=coarse_specs(1)
            + [
                pl.BlockSpec((NCOL, B, 128), lambda dy, tgt, at: (0, 0, 0)),
                pl.BlockSpec(memory_space=pltpu.VMEM),
            ],
            out_specs=[
                pl.BlockSpec((NCOL, 3 * B, 128), lambda dy, tgt, at: (0, 0, 0)), out, out
            ],
            scratch_shapes=[
                pltpu.VMEM((NCB * KC + 1, 8, 128), jnp.float32),
                pltpu.VMEM((4, NCOL, 128), jnp.float32),
            ],
        ),
        out_shape=[
            jax.ShapeDtypeStruct((NCOL, 3 * B, 128), jnp.bfloat16),
            jax.ShapeDtypeStruct(shape, jnp.float32),
            jax.ShapeDtypeStruct(shape, jnp.float32),
        ],
        name="second_coarse",
        compiler_params=pltpu.CompilerParams(vmem_limit_bytes=32 * 1024 * 1024),
    )(tgt, at, *parts, *ps, x0, pltpu.with_memory_space_constraint(before, pltpu.VMEM))


def layout_kernel(x_ref, ap_ref, coarse_ref, turn_ref, wide_ref, flat_ref):
    for tp in range(KC // 2):
        rows = []
        for bg in range(8):
            total = None
            for ih in range(2):
                for part in range(2):
                    r0 = 2 * B + part * 32 + tp * 8
                    term = x_ref[bg * 2 + ih, r0:r0 + 8, :].astype(jnp.float32)
                    total = term if total is None else total + term
            rows.append(total)
        wide_ref[...] = jnp.concatenate(rows, axis=0).T
        for lo in range(2):
            even = wide_ref[pl.ds(lo * B, 32, stride=2), :]
            odd = wide_ref[pl.ds(lo * B + 1, 32, stride=2), :]
            flat_ref[pl.ds(tp * 2 + lo, 32, stride=8), :] = jnp.concatenate([even, odd], axis=1)
    for h in range(32):
        coarse_ref[:, h * 128:(h + 1) * 128] = flat_ref[h * 8:(h + 1) * 8, :]
    for ih in range(2):
        for qh in range(2):
            for s in range(KAP):
                r0 = qh * B + s * 8
                m = jnp.concatenate(
                    [x_ref[bg * 2 + ih, r0:r0 + 8, :] for bg in range(8)], axis=0
                )
                t = m.astype(jnp.float32).T
                for lo in range(2):
                    top, bottom = t[lo * B:lo * B + 32], t[lo * B + 32:lo * B + B]
                    turn_ref[lo, pl.ds(s, 32, stride=8), :] = jnp.concatenate([top, bottom], axis=1)
            for lo in range(2):
                for h in range(32):
                    tile = turn_ref[lo, h * 8:(h + 1) * 8, :]
                    ap_ref[ih * 4 + qh * 2 + lo, :, h * 128:(h + 1) * 128] = tile.astype(jnp.bfloat16)


def layout(x):
    vmem = pl.BlockSpec(memory_space=pltpu.VMEM)
    return pl.pallas_call(
        layout_kernel,
        in_specs=[vmem],
        out_specs=[vmem, vmem],
        scratch_shapes=[
            pltpu.VMEM((2, 256, 128), jnp.float32),
            pltpu.VMEM((128, B), jnp.float32),
            pltpu.VMEM((256, 128), jnp.float32),
        ],
        out_shape=[
            jax.ShapeDtypeStruct((8, KAP, B * B), jnp.bfloat16),
            jax.ShapeDtypeStruct((KC, B * B), jnp.float32),
        ],
        name="layout",
    )(x)


def pick_rows(table, index):
    hot = (index[..., None] == jnp.arange(table.shape[0], dtype=jnp.int32)).astype(jnp.bfloat16)
    rows = jnp.einsum(
        "...k,km->...m", hot, table.astype(jnp.bfloat16), preferred_element_type=jnp.float32
    )
    return rows.astype(jnp.int32)


def index_slab(index):
    return jnp.pad(index.astype(jnp.bfloat16), ((0, 16 - index.shape[0]), (0, KP * B - KP)))


def step(a_blocks, a_index, p_blocks, p_index, ap_index, coarse_index):
    row = lax.axis_index("row")
    col = lax.axis_index("col")
    z, core = row >> 1, row & 1
    y, x = col >> 2, col & 3
    at = jnp.stack([x, y, z, core]).astype(jnp.int32)
    half = x & 1
    other_half = 1 - half

    own = p_blocks[:, 0].reshape(8, KP, B, B)
    pt = own.transpose(0, 3, 1, 2).reshape(8 * B, KP * B)
    pt = jnp.concatenate([pt, index_slab(p_index[:, 0])], axis=0)
    by_z = [pt] + [along_row(pt, d, 0) for d in (1, 2, 3)]
    partner = along_row(pt, 0, 1)

    pn = own.reshape(8, KP, 32, 2, B).transpose(0, 3, 2, 1, 4).reshape(2, 4 * B, KP * B)
    halves = jnp.stack(
        [
            jnp.concatenate([pn[h], index_slab(p_index[4 * h:4 * h + 4, 0])], axis=0)
            for h in range(2)
        ]
    )
    *by_z, halves, half, other_half = lax.optimization_barrier(
        (*by_z, halves, half, other_half)
    )
    parts = [by_z[0], partner]
    for part in by_z[1:]:
        parts += [part, along_row(part, 0, 1)]
    by_y = [halves] + [along_col(halves, 0, d) for d in (1, 2, 3)]

    a = spread(a_blocks[:, 0]).reshape(4, 2, NCOL, B, KA * B)

    a_idx = a_index[:, 0]
    from_row = a_idx >> 3
    place = ((z - (from_row >> 1)) & 3) * 2 + ((core + from_row) & 1)
    place = place * 8 + (a_idx & 7)
    dup, cols_k = table(parts)
    picked = pick_rows(cols_k[:, :KP], place)
    equal = picked[:, :, None, :] == ap_index[:, None, :, None]
    ids = place[:, :, None, None] * KP + jnp.arange(KP, dtype=jnp.int32)
    idx = jnp.min(jnp.where(equal, ids, NK * KP), axis=3)
    idx = idx.transpose(1, 2, 0).reshape(KA * KAP, 128)

    x1, x3 = x_products(1, idx, at, a, dup)
    got_x1, got_x3 = along_col(x1, 1, 0), along_col(x3, 3, 0)
    ya = y_products(0, idx, at, a, dup)
    got_ya = [along_col(ya[d], 0, d) for d in (1, 2, 3)]
    x0, x2 = x_products(0, idx, at, a, dup)
    got_x2 = along_col(x2, 2, 0)
    yb = y_products(1, idx, at, a, dup)
    got_yb = [along_col(yb[d], 0, d) for d in (1, 2, 3)]
    s0 = middle(x_middle_kernel, at, [x0, got_x1, got_x2, got_x3])
    y_last = [along_col(s0[d], 0, d) for d in (1, 2, 3)]
    s1 = middle(y_middle_kernel, at, [ya[0], *got_ya, yb[0], *got_yb])
    far = along_col(s1[2], 2, 0)
    x_last = [along_col(s1[1], 1, 0), far, along_col(s1[3], 3, 0)]

    by_y = jnp.stack(by_y)
    same = lax.dynamic_index_in_dim(by_y, half, 1, keepdims=False, allow_negative_indices=False)
    diff = lax.dynamic_index_in_dim(by_y, other_half, 1, keepdims=False, allow_negative_indices=False)
    ps = [same, along_col(diff, 1, 0), along_col(same, 2, 0), along_col(diff, 3, 0)]

    cols_p = jnp.stack([p[:, 4 * B:4 * B + 4, :KP] for p in ps]).reshape(NCOL, 16)
    cc = jnp.arange(NCOL, dtype=jnp.int32)
    where = ((x - (cc & 3)) & 3) * 4 + ((y - (cc >> 2)) & 3)
    cols_i = pick_rows(cols_p, where).reshape(NCOL, 4, KP)
    slots = lax.dynamic_index_in_dim(
        ap_index.reshape(2, 4, NCOL, KAP), half, 0, keepdims=False, allow_negative_indices=False
    ).transpose(1, 0, 2)
    targets = pick_rows(coarse_index, cols_i)
    hit = targets[:, :, :, None, :] == slots[:, :, None, :, None]
    slot = cols_i[:, :, :, None, None] * KC + jnp.arange(KC, dtype=jnp.int32)
    tgt = jnp.min(jnp.where(hit, slot, NCB * KC), axis=4).reshape(-1)

    x0, before = first_coarse(tgt, at, [s0[0], *y_last], ps)
    apt, keep, send = second_coarse(tgt, at, [s1[0], *x_last], ps, x0, before)
    got = along_row(send, 0, 1)
    sums = [keep[d] + got[d] for d in range(4)]
    coarse = sums[0]
    moved = [along_row(sums[d], d, 0) for d in (1, 2, 3)]
    for part in moved:
        coarse = coarse + part
    high = lax.reduce_precision(coarse, exponent_bits=8, mantissa_bits=7)
    pair = jnp.concatenate(
        [v.astype(jnp.bfloat16).reshape(NCOL, 32, 128) for v in (high, coarse - high)], axis=1
    )
    both = lax.dynamic_update_slice(apt, pair, (0, 2 * B, 0))
    both = lax.all_to_all(both, "col", 0, 0, tiled=True)
    ap_out, coarse_out = layout(both)
    ap_out = ap_out.reshape(8, 1, KAP, B * B)
    coarse_out = coarse_out.reshape(1, KC, B * B)
    return ap_out, coarse_out


def solution(mesh):
    placed = (
        P("row", "col", None, None),
        P("row", "col", None),
        P("row", "col", None, None),
        P("row", "col", None),
        P("row", None),
        P(),
    )
    return jax.shard_map(
        step,
        mesh=mesh,
        in_specs=placed,
        out_specs=(P("row", "col", None, None), P(("row", "col"), None, None)),
        check_vma=False,
    )
```

```python
import jax
import jax.numpy as jnp
from jax import lax
from jax.experimental import pallas as pl
from jax.experimental.pallas import tpu as pltpu
from jax.sharding import PartitionSpec as P


B = 64
KA = 4
KP = 4
KAP = 8
KC = 8
NCOL = 16
NK = 64
NCB = 128
FULL = 14.0
TINY = 1e-30


def along_row(v, dz, flip):
    pairs = [(r, ((r // 2 + dz) % 4) * 2 + (r % 2 + flip) % 2) for r in range(8)]
    return lax.ppermute(v, "row", pairs)


def along_col(v, dx, dy):
    pairs = [(c, ((c // 4 + dy) % 4) * 4 + (c % 4 + dx) % 4) for c in range(16)]
    return lax.ppermute(v, "col", pairs)


def low_lanes(rows):
    return lax.broadcasted_iota(jnp.int32, (rows, 128), 1) < B


def spread_kernel(a_ref, out_ref, buf_ref):
    low = low_lanes(32)

    def some(g, carry):
        for u in range(4):
            i = g * 4 + u
            v = a_ref[i].astype(jnp.float32)
            for h in range(32):
                buf_ref[u, h * 4:(h + 1) * 4, :] = v[:, h * 128:(h + 1) * 128]
        for u in range(4):
            i = g * 4 + u
            for ep in range(2):
                v0 = buf_ref[u, pl.ds(2 * ep, 32, stride=4), :]
                v1 = buf_ref[u, pl.ds(2 * ep + 1, 32, stride=4), :]
                top = jnp.where(low, v0, pltpu.roll(v1, B, 1))
                bottom = jnp.where(low, pltpu.roll(v0, B, 1), v1)
                out_ref[i, 0:32, ep * 128:(ep + 1) * 128] = top.astype(jnp.bfloat16)
                out_ref[i, 32:64, ep * 128:(ep + 1) * 128] = bottom.astype(jnp.bfloat16)
        return carry

    lax.fori_loop(0, 4, some, 0)


def spread(a):
    return pl.pallas_call(
        spread_kernel,
        grid=(8,),
        in_specs=[pl.BlockSpec((16, KA, B * B), lambda g: (g, 0, 0))],
        out_specs=pl.BlockSpec((16, B, KA * B), lambda g: (g, 0, 0)),
        scratch_shapes=[pltpu.VMEM((4, 128, 128), jnp.float32)],
        out_shape=pltpu.VMEM((128, B, KA * B), jnp.bfloat16),
        name="spread",
        compiler_params=pltpu.CompilerParams(vmem_limit_bytes=8 * 1024 * 1024),
    )(pltpu.with_memory_space_constraint(a, pltpu.HBM))


def table_kernel(*refs):
    parts, out_ref, cols_ref = refs[:8], refs[8], refs[9]
    low = low_lanes(B)
    for n, part in enumerate(parts):
        cols_ref[n * 8:(n + 1) * 8, :] = part[8 * B:8 * B + 8, 0:128].astype(jnp.float32)

        def fill(q, carry):
            for mh in range(2):
                v = part[pl.ds(pl.multiple_of(q * B, B), B), mh * 128:(mh + 1) * 128]
                turned = jnp.concatenate([v[:, B:], v[:, :B]], axis=1)
                at = (n * 8 + q) * 4 + 2 * mh
                out_ref[at] = jnp.where(low, v, turned)
                out_ref[at + 1] = jnp.where(low, turned, v)
            return carry

        lax.fori_loop(0, 8, fill, 0, unroll=2)
    out_ref[NK * KP] = jnp.zeros((B, 128), jnp.bfloat16)


def table(parts):
    whole = pl.BlockSpec(memory_space=pltpu.VMEM)
    return pl.pallas_call(
        table_kernel,
        in_specs=[whole] * 8,
        out_specs=[whole, whole],
        out_shape=[
            pltpu.VMEM((NK * KP + 1, B, 128), jnp.bfloat16),
            jax.ShapeDtypeStruct((NK, 128), jnp.float32),
        ],
        name="table",
        compiler_params=pltpu.CompilerParams(vmem_limit_bytes=12 * 1024 * 1024),
    )(*parts)


def nt_dot(a, b):
    return lax.dot_general(a, b, (((1,), (1,)), ((), ())), preferred_element_type=jnp.float32)


def exponent(most):
    return jnp.ceil(jnp.log2(jnp.maximum(most, TINY)))


def coded(v, mul):
    return jnp.round(v * mul).astype(jnp.int32).astype(jnp.int16)


def row_pair(lhs, rhs_top, rhs_bottom):
    zero = jnp.zeros((B, KA * B), jnp.bfloat16)
    stacked = jnp.concatenate(
        [
            jnp.concatenate([rhs_top, zero], axis=1),
            jnp.concatenate([zero, rhs_bottom], axis=1),
        ],
        axis=0,
    )
    return nt_dot(lhs, stacked)


def chosen_blocks(idx_ref, dup_ref, low, first_row):
    rows = []
    for s in range(KAP):
        pieces = []
        for lo in range(2):
            row = first_row + lo * NCOL
            for ep in range(2):
                first = dup_ref[idx_ref[(2 * ep) * KAP + s, row]]
                second = dup_ref[idx_ref[(2 * ep + 1) * KAP + s, row]]
                pieces.append(jnp.where(low, first, second))
        rows.append(jnp.concatenate(pieces, axis=1))
    return jnp.concatenate(rows, axis=0)


def coded_products(res):
    e = exponent(jnp.max(jnp.abs(res), axis=0, keepdims=True))
    q = jnp.round(res * jnp.exp2(FULL - e)).astype(jnp.int32)

    def tile(bg, sp):
        r0 = 2 * sp * B + bg * 8
        return jnp.concatenate([q[r0:r0 + 8], q[r0 + B:r0 + B + 8]], axis=0)

    return e, tile


def pipelined(count, multiply, encode, r0_ref, r1_ref):
    r1_ref[...] = jnp.zeros_like(r1_ref)

    def two(k, carry):
        r0_ref[...] = multiply(2 * k)
        encode(jnp.maximum(2 * k - 1, 0), r1_ref[...])
        r1_ref[...] = multiply(2 * k + 1)
        encode(2 * k, r0_ref[...])
        return carry

    lax.fori_loop(0, count // 2, two, 0)
    encode(count - 1, r1_ref[...])


def x_product_kernel(
    j, idx_ref, at_ref, a_ref, dup_ref, near_ref, far_ref, exp_ref, r0_ref, r1_ref
):
    cblk = pl.program_id(0)
    low = low_lanes(B)
    goal = lax.rem(at_ref[0] + j, 4)
    ih = lax.rem(goal, 2)
    count = a_ref.shape[2]
    is_low = goal < 2

    def multiply(cc):
        lhs = chosen_blocks(idx_ref, dup_ref, low, ih * 4 * NCOL + cblk * count + cc)
        return row_pair(lhs, a_ref[0, 0, cc], a_ref[0, 1, cc])

    def encode(cc, res):
        c = cblk * count + cc
        e, tile = coded_products(res)
        exp_ref[pl.ds(c, 1), :] = e
        for u in range(4):
            for sp in range(4):
                t0, t1 = tile(2 * u, sp), tile(2 * u + 1, sp)
                at = (u * NCOL + c) * 4 + sp
                near_ref[at] = jnp.where(is_low, t0, t1).astype(jnp.int16)
                far_ref[at] = jnp.where(is_low, t1, t0).astype(jnp.int16)

    pipelined(count, multiply, encode, r0_ref, r1_ref)

    @pl.when(cblk == pl.num_programs(0) - 1)
    def _():
        e = exp_ref[...].astype(jnp.int32).astype(jnp.int16)
        near_ref[256] = e
        far_ref[256] = e


def x_products(j, idx, at, a, dup):
    block = 8
    out = pl.BlockSpec((257, 16, 128), lambda c, idx, at: (0, 0, 0))
    return pl.pallas_call(
        lambda *refs: x_product_kernel(j, *refs),
        grid_spec=pltpu.PrefetchScalarGridSpec(
            num_scalar_prefetch=2,
            grid=(NCOL // block,),
            in_specs=[
                pl.BlockSpec(
                    (1, 2, block, B, KA * B),
                    lambda c, idx, at: (lax.rem(at[0] + j, 2) * 2, 0, c, 0, 0),
                ),
                pl.BlockSpec(memory_space=pltpu.VMEM),
            ],
            out_specs=[out, out],
            scratch_shapes=[pltpu.VMEM((NCOL, 128), jnp.float32)]
            + [pltpu.VMEM((KAP * B, 128), jnp.float32)] * 2,
        ),
        out_shape=[
            (pltpu.HBM if j == 0 else jax.ShapeDtypeStruct)((257, 16, 128), jnp.int16),
            jax.ShapeDtypeStruct((257, 16, 128), jnp.int16),
        ],
        compiler_params=pltpu.CompilerParams(vmem_limit_bytes=20 * 1024 * 1024),
    )(
        idx,
        at,
        pltpu.with_memory_space_constraint(a, pltpu.VMEM),
        pltpu.with_memory_space_constraint(dup, pltpu.VMEM),
    )


def y_product_kernel(
    part, idx_ref, at_ref, a_ref, dup_ref, o0_ref, o1_ref, o2_ref, o3_ref, exp_ref, r0_ref, r1_ref
):
    ih = pl.program_id(0)
    low = low_lanes(B)
    y = at_ref[1]
    count = a_ref.shape[2]
    outs = (o0_ref, o1_ref, o2_ref, o3_ref)
    turn1 = lax.rem(y, 2) == 1
    turn2 = y >= 2

    def multiply(cc):
        lhs = chosen_blocks(idx_ref, dup_ref, low, (ih * 4 + 2) * NCOL + part * count + cc)
        return row_pair(lhs, a_ref[0, 0, cc], a_ref[0, 1, cc])

    def encode(cc, res):
        e, tile = coded_products(res)
        exp_ref[pl.ds(ih * 8 + cc, 1), :] = e
        for g in range(2):
            for sp in range(4):
                t = [tile(2 * k + g, sp) for k in range(4)]
                t = [jnp.where(turn1, t[(k + 1) % 4], t[k]) for k in range(4)]
                t = [jnp.where(turn2, t[(k + 2) % 4], t[k]) for k in range(4)]
                for d in range(4):
                    outs[d][((2 * g + ih) * 8 + cc) * 4 + sp] = t[d].astype(jnp.int16)

    pipelined(count, multiply, encode, r0_ref, r1_ref)

    @pl.when(ih == 1)
    def _():
        e = exp_ref[...].astype(jnp.int32).astype(jnp.int16)
        for o_ref in outs:
            o_ref[128] = e


def y_products(part, idx, at, a, dup):
    block = 8
    out = pl.BlockSpec((129, 16, 128), lambda ih, idx, at: (0, 0, 0))
    return pl.pallas_call(
        lambda *refs: y_product_kernel(part, *refs),
        grid_spec=pltpu.PrefetchScalarGridSpec(
            num_scalar_prefetch=2,
            grid=(2,),
            in_specs=[
                pl.BlockSpec(
                    (1, 2, block, B, KA * B), lambda ih, idx, at: (ih * 2 + 1, 0, part, 0, 0)
                ),
                pl.BlockSpec(memory_space=pltpu.VMEM),
            ],
            out_specs=[out] * 4,
            scratch_shapes=[pltpu.VMEM((NCOL, 128), jnp.float32)]
            + [pltpu.VMEM((KAP * B, 128), jnp.float32)] * 2,
        ),
        out_shape=[pltpu.HBM((129, 16, 128), jnp.int16)]
        + [jax.ShapeDtypeStruct((129, 16, 128), jnp.int16)] * 3,
        compiler_params=pltpu.CompilerParams(vmem_limit_bytes=20 * 1024 * 1024),
    )(
        idx,
        at,
        pltpu.with_memory_space_constraint(a, pltpu.VMEM),
        pltpu.with_memory_space_constraint(dup, pltpu.VMEM),
    )


def sum_and_code(tiles, out_ref, c):
    most = jnp.maximum(
        jnp.maximum(jnp.abs(tiles[0]), jnp.abs(tiles[1])),
        jnp.maximum(jnp.abs(tiles[2]), jnp.abs(tiles[3])),
    )
    e = exponent(jnp.max(most, axis=0, keepdims=True))
    mul = jnp.exp2(FULL - e)
    for sp in range(4):
        out_ref[c * 4 + sp] = coded(tiles[sp], mul)
    return e


def x_middle_kernel(at_ref, m0, m1, m2, m3, o0, o1, o2, o3, scale_ref, exp_ref):
    parts = (m0, m1, m2, m3)
    for d, m in enumerate(parts):
        scale_ref[d] = jnp.exp2(m[256].astype(jnp.float32) - FULL)
    for d2, out_ref in enumerate((o0, o1, o2, o3)):
        u = lax.rem(at_ref[1] + d2, 4)

        def one(c, carry):
            scales = [scale_ref[d, pl.ds(c, 1), :] for d in range(4)]
            tiles = []
            for sp in range(4):
                terms = [
                    m[(u * NCOL + c) * 4 + sp].astype(jnp.float32) * scale
                    for m, scale in zip(parts, scales)
                ]
                tiles.append((terms[0] + terms[1]) + (terms[2] + terms[3]))
            exp_ref[pl.ds(c, 1), :] = sum_and_code(tiles, out_ref, c)
            return carry

        lax.fori_loop(0, NCOL, one, 0, unroll=2)
        out_ref[64] = exp_ref[...].astype(jnp.int32).astype(jnp.int16)


def y_middle_kernel(at_ref, *refs):
    parts, outs, scale_ref, exp_ref = refs[:8], refs[8:12], refs[12], refs[13]
    for n, m in enumerate(parts):
        scale_ref[n] = jnp.exp2(m[128].astype(jnp.float32) - FULL)
    for d2, out_ref in enumerate(outs):
        u = lax.rem(at_ref[0] + d2, 4)
        ih = lax.rem(u, 2)
        for half in range(2):
            own = parts[half * 4:half * 4 + 4]

            def one(cc, carry):
                scales = [scale_ref[half * 4 + d, pl.ds(ih * 8 + cc, 1), :] for d in range(4)]
                tiles = []
                for sp in range(4):
                    terms = [
                        m[(u * 8 + cc) * 4 + sp].astype(jnp.float32) * scale
                        for m, scale in zip(own, scales)
                    ]
                    tiles.append((terms[0] + terms[1]) + (terms[2] + terms[3]))
                c = half * 8 + cc
                exp_ref[pl.ds(c, 1), :] = sum_and_code(tiles, out_ref, c)
                return carry

            lax.fori_loop(0, 8, one, 0, unroll=2)
        out_ref[64] = exp_ref[...].astype(jnp.int32).astype(jnp.int16)


def middle(kernel, at, parts):
    vmem = pl.BlockSpec(memory_space=pltpu.VMEM)
    return pl.pallas_call(
        kernel,
        in_specs=[pl.BlockSpec(memory_space=pltpu.SMEM)] + [vmem] * len(parts),
        out_specs=[vmem] * 4,
        scratch_shapes=[
            pltpu.VMEM((len(parts), NCOL, 128), jnp.float32),
            pltpu.VMEM((NCOL, 128), jnp.float32),
        ],
        out_shape=[jax.ShapeDtypeStruct((65, 16, 128), jnp.int16)] * 4,
    )(at, *parts)


def decode(parts, out_ref, first_row, scale_ref):
    for n, m in enumerate(parts):
        scale_ref[n] = jnp.exp2(m[64].astype(jnp.float32) - FULL)

    def one(c, carry):
        scales = [scale_ref[d, pl.ds(c, 1), :] for d in range(4)]
        for sp in range(4):
            terms = [parts[d][c * 4 + sp].astype(jnp.float32) * scales[d] for d in range(4)]
            total = (terms[0] + terms[1]) + (terms[2] + terms[3])
            row = first_row + sp * 16
            out_ref[c, row:row + 16, :] = total.astype(jnp.bfloat16)
        return carry

    lax.fori_loop(0, NCOL, one, 0, unroll=2)


def add_terms(qh, tgt_ref, at_ref, x_ref, p_refs, acc_ref):
    dy = pl.program_id(0)
    low = low_lanes(8)
    low_x = low_lanes(B)
    for dx, p_ref in enumerate(p_refs):
        c = lax.rem(at_ref[1] - dy + 4, 4) * 4 + lax.rem(at_ref[0] - dx + 4, 4)
        x = x_ref[c, qh * B:(qh + 1) * B, :]
        none = jnp.zeros_like(x)
        lhs = jnp.concatenate([jnp.where(low_x, x, none), jnp.where(low_x, none, x)], axis=0)
        rhs = p_ref[0]
        res = lax.dot_general(
            lhs, rhs, (((1,), (0,)), ((), ())), preferred_element_type=jnp.float32
        )
        for lo in range(2):
            ats, sums = [], []
            for m in range(KP):
                for s in range(KAP):
                    at = tgt_ref[(((c * 2 + qh) * 2 + lo) * KP + m) * KAP + s]
                    rows = (lo * KAP + s) * 8
                    tile = res[rows:rows + 8, (m // 2) * 128:(m // 2) * 128 + 128]
                    keep = low if m % 2 == 0 else jnp.logical_not(low)
                    ats.append(at)
                    sums.append(acc_ref[at] + jnp.where(keep, tile, 0.0))
            for at, total in zip(ats, sums):
                acc_ref[at] = total


def first_coarse_kernel(tgt_ref, at_ref, *refs):
    parts, p_refs, (x_ref, acc_ref, scale_ref) = refs[:4], refs[4:8], refs[8:]

    @pl.when(pl.program_id(0) == 0)
    def _():
        acc_ref[...] = jnp.zeros_like(acc_ref)
        decode(parts, x_ref, 0, scale_ref)

    add_terms(0, tgt_ref, at_ref, x_ref, p_refs, acc_ref)


def second_coarse_kernel(tgt_ref, at_ref, *refs):
    parts, p_refs, (x0_ref, before_ref) = refs[:4], refs[4:8], refs[8:10]
    x_ref, keep_ref, send_ref, acc_ref, scale_ref = refs[10:]
    low = low_lanes(8)

    @pl.when(pl.program_id(0) == 0)
    def _():
        acc_ref[...] = jnp.zeros_like(acc_ref)
        decode(parts, x_ref, B, scale_ref)
        x_ref[:, 0:B, :] = x0_ref[...]

    add_terms(1, tgt_ref, at_ref, x_ref, p_refs, acc_ref)

    @pl.when(pl.program_id(0) == 3)
    def _():
        for flip, out_ref in ((1, send_ref), (0, keep_ref)):
            core = lax.rem(at_ref[3] + flip, 2)
            for d in range(4):
                first = (lax.rem(at_ref[2] + d, 4) * 2 + core) * NCOL

                def fold(col, carry):
                    for tp in range(KC // 2):
                        at = (first + col) * KC + 2 * tp
                        t0 = acc_ref[at] + before_ref[at]
                        t1 = acc_ref[at + 1] + before_ref[at + 1]
                        t0 = t0 + pltpu.roll(t0, B, 1)
                        t1 = t1 + pltpu.roll(t1, B, 1)
                        out_ref[d, col, tp] = jnp.where(low, t0, t1)
                    return carry

                lax.fori_loop(0, NCOL, fold, 0, unroll=4)


def coarse_specs(qh):
    whole = pl.BlockSpec((65, 16, 128), lambda dy, tgt, at: (0, 0, 0))
    return [whole] * 4 + [
        pl.BlockSpec((1, 2 * B, KP * B), lambda dy, tgt, at: (dy, qh, 0))
    ] * 4


def first_coarse(tgt, at, parts, ps):
    return pl.pallas_call(
        first_coarse_kernel,
        grid_spec=pltpu.PrefetchScalarGridSpec(
            num_scalar_prefetch=2,
            grid=(4,),
            in_specs=coarse_specs(0),
            out_specs=[
                pl.BlockSpec((NCOL, B, 128), lambda dy, tgt, at: (0, 0, 0)),
                pl.BlockSpec((NCB * KC + 1, 8, 128), lambda dy, tgt, at: (0, 0, 0)),
            ],
            scratch_shapes=[pltpu.VMEM((4, NCOL, 128), jnp.float32)],
        ),
        out_shape=[
            jax.ShapeDtypeStruct((NCOL, B, 128), jnp.bfloat16),
            jax.ShapeDtypeStruct((NCB * KC + 1, 8, 128), jnp.float32),
        ],
        name="first_coarse",
        compiler_params=pltpu.CompilerParams(vmem_limit_bytes=32 * 1024 * 1024),
    )(tgt, at, *parts, *ps)


def second_coarse(tgt, at, parts, ps, x0, before):
    shape = (4, NCOL, KC // 2, 8, 128)
    out = pl.BlockSpec(shape, lambda dy, tgt, at: (0, 0, 0, 0, 0))
    return pl.pallas_call(
        second_coarse_kernel,
        grid_spec=pltpu.PrefetchScalarGridSpec(
            num_scalar_prefetch=2,
            grid=(4,),
            in_specs=coarse_specs(1)
            + [
                pl.BlockSpec((NCOL, B, 128), lambda dy, tgt, at: (0, 0, 0)),
                pl.BlockSpec(memory_space=pltpu.VMEM),
            ],
            out_specs=[
                pl.BlockSpec((NCOL, 3 * B, 128), lambda dy, tgt, at: (0, 0, 0)), out, out
            ],
            scratch_shapes=[
                pltpu.VMEM((NCB * KC + 1, 8, 128), jnp.float32),
                pltpu.VMEM((4, NCOL, 128), jnp.float32),
            ],
        ),
        out_shape=[
            jax.ShapeDtypeStruct((NCOL, 3 * B, 128), jnp.bfloat16),
            jax.ShapeDtypeStruct(shape, jnp.float32),
            jax.ShapeDtypeStruct(shape, jnp.float32),
        ],
        name="second_coarse",
        compiler_params=pltpu.CompilerParams(vmem_limit_bytes=32 * 1024 * 1024),
    )(tgt, at, *parts, *ps, x0, pltpu.with_memory_space_constraint(before, pltpu.VMEM))


def layout_kernel(x_ref, ap_ref, coarse_ref, turn_ref, wide_ref, flat_ref):
    for tp in range(KC // 2):
        rows = []
        for bg in range(8):
            total = None
            for ih in range(2):
                for part in range(2):
                    r0 = 2 * B + part * 32 + tp * 8
                    term = x_ref[bg * 2 + ih, r0:r0 + 8, :].astype(jnp.float32)
                    total = term if total is None else total + term
            rows.append(total)
        wide_ref[...] = jnp.concatenate(rows, axis=0).T
        for lo in range(2):
            even = wide_ref[pl.ds(lo * B, 32, stride=2), :]
            odd = wide_ref[pl.ds(lo * B + 1, 32, stride=2), :]
            flat_ref[pl.ds(tp * 2 + lo, 32, stride=8), :] = jnp.concatenate([even, odd], axis=1)
    for h in range(32):
        coarse_ref[:, h * 128:(h + 1) * 128] = flat_ref[h * 8:(h + 1) * 8, :]
    for ih in range(2):
        for qh in range(2):
            for s in range(KAP):
                r0 = qh * B + s * 8
                m = jnp.concatenate(
                    [x_ref[bg * 2 + ih, r0:r0 + 8, :] for bg in range(8)], axis=0
                )
                t = m.astype(jnp.float32).T
                for lo in range(2):
                    top, bottom = t[lo * B:lo * B + 32], t[lo * B + 32:lo * B + B]
                    turn_ref[lo, pl.ds(s, 32, stride=8), :] = jnp.concatenate([top, bottom], axis=1)
            for lo in range(2):
                for h in range(32):
                    tile = turn_ref[lo, h * 8:(h + 1) * 8, :]
                    ap_ref[ih * 4 + qh * 2 + lo, :, h * 128:(h + 1) * 128] = tile.astype(jnp.bfloat16)


def layout(x):
    vmem = pl.BlockSpec(memory_space=pltpu.VMEM)
    return pl.pallas_call(
        layout_kernel,
        in_specs=[vmem],
        out_specs=[vmem, vmem],
        scratch_shapes=[
            pltpu.VMEM((2, 256, 128), jnp.float32),
            pltpu.VMEM((128, B), jnp.float32),
            pltpu.VMEM((256, 128), jnp.float32),
        ],
        out_shape=[
            jax.ShapeDtypeStruct((8, KAP, B * B), jnp.bfloat16),
            jax.ShapeDtypeStruct((KC, B * B), jnp.float32),
        ],
        name="layout",
    )(x)


def pick_rows(table, index):
    hot = (index[..., None] == jnp.arange(table.shape[0], dtype=jnp.int32)).astype(jnp.bfloat16)
    rows = jnp.einsum(
        "...k,km->...m", hot, table.astype(jnp.bfloat16), preferred_element_type=jnp.float32
    )
    return rows.astype(jnp.int32)


def index_slab(index):
    return jnp.pad(index.astype(jnp.bfloat16), ((0, 16 - index.shape[0]), (0, KP * B - KP)))


def step(a_blocks, a_index, p_blocks, p_index, ap_index, coarse_index):
    row = lax.axis_index("row")
    col = lax.axis_index("col")
    z, core = row >> 1, row & 1
    y, x = col >> 2, col & 3
    at = jnp.stack([x, y, z, core]).astype(jnp.int32)
    half = x & 1
    other_half = 1 - half

    own = p_blocks[:, 0].reshape(8, KP, B, B)
    pt = own.transpose(0, 3, 1, 2).reshape(8 * B, KP * B)
    pt = jnp.concatenate([pt, index_slab(p_index[:, 0])], axis=0)
    by_z = [pt] + [along_row(pt, d, 0) for d in (1, 2, 3)]
    partner = along_row(pt, 0, 1)

    pn = own.reshape(8, KP, 32, 2, B).transpose(0, 3, 2, 1, 4).reshape(2, 4 * B, KP * B)
    halves = jnp.stack(
        [
            jnp.concatenate([pn[h], index_slab(p_index[4 * h:4 * h + 4, 0])], axis=0)
            for h in range(2)
        ]
    )
    *by_z, halves, half, other_half = lax.optimization_barrier(
        (*by_z, halves, half, other_half)
    )
    parts = [by_z[0], partner]
    for part in by_z[1:]:
        parts += [part, along_row(part, 0, 1)]
    by_y = [halves] + [along_col(halves, 0, d) for d in (1, 2, 3)]

    a = spread(a_blocks[:, 0]).reshape(4, 2, NCOL, B, KA * B)

    a_idx = a_index[:, 0]
    from_row = a_idx >> 3
    place = ((z - (from_row >> 1)) & 3) * 2 + ((core + from_row) & 1)
    place = place * 8 + (a_idx & 7)
    dup, cols_k = table(parts)
    picked = pick_rows(cols_k[:, :KP], place)
    equal = picked[:, :, None, :] == ap_index[:, None, :, None]
    ids = place[:, :, None, None] * KP + jnp.arange(KP, dtype=jnp.int32)
    idx = jnp.min(jnp.where(equal, ids, NK * KP), axis=3)
    idx = idx.transpose(1, 2, 0).reshape(KA * KAP, 128)

    x1, x3 = x_products(1, idx, at, a, dup)
    got_x1, got_x3 = along_col(x1, 1, 0), along_col(x3, 3, 0)
    ya = y_products(0, idx, at, a, dup)
    got_ya = [along_col(ya[d], 0, d) for d in (1, 2, 3)]
    x0, x2 = x_products(0, idx, at, a, dup)
    got_x2 = along_col(x2, 2, 0)
    yb = y_products(1, idx, at, a, dup)
    got_yb = [along_col(yb[d], 0, d) for d in (1, 2, 3)]
    s0 = middle(x_middle_kernel, at, [x0, got_x1, got_x2, got_x3])
    y_last = [along_col(s0[d], 0, d) for d in (1, 2, 3)]
    s1 = middle(y_middle_kernel, at, [ya[0], *got_ya, yb[0], *got_yb])
    far = along_col(s1[2], 2, 0)
    x_last = [along_col(s1[1], 1, 0), far, along_col(s1[3], 3, 0)]

    by_y = jnp.stack(by_y)
    same = lax.dynamic_index_in_dim(by_y, half, 1, keepdims=False, allow_negative_indices=False)
    diff = lax.dynamic_index_in_dim(by_y, other_half, 1, keepdims=False, allow_negative_indices=False)
    ps = [same, along_col(diff, 1, 0), along_col(same, 2, 0), along_col(diff, 3, 0)]

    cols_p = jnp.stack([p[:, 4 * B:4 * B + 4, :KP] for p in ps]).reshape(NCOL, 16)
    cc = jnp.arange(NCOL, dtype=jnp.int32)
    where = ((x - (cc & 3)) & 3) * 4 + ((y - (cc >> 2)) & 3)
    cols_i = pick_rows(cols_p, where).reshape(NCOL, 4, KP)
    slots = lax.dynamic_index_in_dim(
        ap_index.reshape(2, 4, NCOL, KAP), half, 0, keepdims=False, allow_negative_indices=False
    ).transpose(1, 0, 2)
    targets = pick_rows(coarse_index, cols_i)
    hit = targets[:, :, :, None, :] == slots[:, :, None, :, None]
    slot = cols_i[:, :, :, None, None] * KC + jnp.arange(KC, dtype=jnp.int32)
    tgt = jnp.min(jnp.where(hit, slot, NCB * KC), axis=4).reshape(-1)

    x0, before = first_coarse(tgt, at, [s0[0], *y_last], ps)
    apt, keep, send = second_coarse(tgt, at, [s1[0], *x_last], ps, x0, before)
    got = along_row(send, 0, 1)
    sums = [keep[d] + got[d] for d in range(4)]
    coarse = sums[0]
    moved = [along_row(sums[d], d, 0) for d in (1, 2, 3)]
    for part in moved:
        coarse = coarse + part
    high = lax.reduce_precision(coarse, exponent_bits=8, mantissa_bits=7)
    pair = jnp.concatenate(
        [v.astype(jnp.bfloat16).reshape(NCOL, 32, 128) for v in (high, coarse - high)], axis=1
    )
    both = lax.dynamic_update_slice(apt, pair, (0, 2 * B, 0))
    both = lax.all_to_all(both, "col", 0, 0, tiled=True)
    ap_out, coarse_out = layout(both)
    ap_out = ap_out.reshape(8, 1, KAP, B * B)
    coarse_out = coarse_out.reshape(1, KC, B * B)
    return ap_out, coarse_out


def solution(mesh):
    placed = (
        P("row", "col", None, None),
        P("row", "col", None),
        P("row", "col", None, None),
        P("row", "col", None),
        P("row", None),
        P(),
    )
    return jax.shard_map(
        step,
        mesh=mesh,
        in_specs=placed,
        out_specs=(P("row", "col", None, None), P(("row", "col"), None, None)),
        check_vma=False,
    )
```
